512 devices in a mesh: req: 64 (over z, y), tensor: 8 (over x, core).
Axes of the slice: x: 4, y: 4, z: 16, core: 2. Of those that a mesh axis runs over, the one named last changes fastest.
Arguments:
- tokens: bfloat16 [16384, 2048], P('req', 'tensor'), may hold values from -6 to 6
- segment_ids: int32 [16384], P('req'), may hold values from 0 to 42, as said below
- prefix_lengths: int32 [43], replicated, may hold values from 0 to 256, as said below
- page_owner: int32 [4096, 1], P('req'), may hold values from 0 to 63; in each aligned block of 64 rows (0 to 63, 64 to 127, ...) at most 2 rows name the same one
- slot_perm: int32 [64, 128], P('req'), may hold values from 0 to 127, each once within a row
- ln_gain: float32 [2048], replicated, may hold values from 0.1 to 1.9
- ln_bias: float32 [2048], replicated, may hold values from -3 to 3
- qkv_weight: bfloat16 [2048, 3, 2048], P('req', None, 'tensor')
- qkv_bias: float32 [3, 2048], P(None, 'tensor'), may hold values from -3 to 3
- dense_weight: bfloat16 [2048, 2048], P('tensor', 'req'), may hold values from -0.375 to 0.375
- dense_bias: float32 [2048], P('tensor'), may hold values from -3 to 3
- fc1_weight: bfloat16 [2048, 4096], P('req', 'tensor'), may hold values from -0.125 to 0.125
- fc1_bias: float32 [4096], P('tensor'), may hold values from -3 to 3
- fc2_weight: bfloat16 [4096, 2048], P('tensor', 'req'), may hold values from -0.25 to 0.25
- fc2_bias: float32 [2048], P('tensor'), may hold values from -3 to 3
- prefix_cache: bfloat16 [16384, 2, 2048], P('req', None, 'tensor'), may hold values from -9 to 9
- cache_pool: bfloat16 [32768, 2, 2048], P('req', None, 'tensor'), may hold values from -6 to 6
Outputs:
- layer_out: bfloat16 [16384, 2048], P('req', 'tensor')
- new_pool: bfloat16 [32768, 2, 2048], P('req', None, 'tensor')
The draws below stay inside these ranges and needn't reach their ends.
Inputs may be any that keep to these rules, and one draw needn't show every extreme that they name: `segment_ids`: labels 1 to 42 appear in order, each as one run of 257 to 512 rows, together filling all rows before the padding; segment 1 is 512 rows long; the last 128 rows are 0. `prefix_lengths`: entry 0 is 0 and entry 1 is 256. `page_owner`: among the pages of one index of req no owner appears more than 2 times, and some owner appears exactly 2 times. `slot_perm`: each row is a permutation of 0 to 127.
All inputs are finite; a program needn't handle non-finite values.
Results may differ from the reference program's by a relative error of at most 0.006.
The reference program's roundings to bfloat16 on the way count: a program that leaves them out, or rounds other values in their place, can miss the bound.
Values may be sent and summed in bfloat16 or wider, within the bound.
A program may use at most 64 MiB of HBM per device.

```python
import math
import jax
import jax.numpy as jnp
import numpy as np
from jax import lax

D = 2048
HEADS = 32
HEAD_DIM = 64
ROT = 32
FFW = 4096
TOK_DEV = 256
PREF = 256
SPAN = 2
SINKS = 4
PAGE = 4
TOKENS = 16384
MAXLEN = 512
WINDOW = 512
NSEG = 42
PAD = 128
PAGES = 4096
PAGES_DEV = 64
CAPP = 2
POOLP = 128
N_REQ = 64


def draw_segment_ids(key, part):
    count = NSEG
    filled = TOKENS - PAD
    spare = filled - count * (TOK_DEV + 1) - (TOK_DEV - 1)
    base = spare // (count - 1)
    remain = spare - base * (count - 1)
    reach = max(0, min(base, TOK_DEV - 2 - base) // 2)
    wobble = jax.random.randint(key, (count - 1,), -reach, reach + 1)
    order = jnp.arange(count - 1, dtype=jnp.int32)
    extra = base + (order < remain).astype(jnp.int32) + wobble - jnp.roll(wobble, 1)
    lengths = jnp.concatenate([jnp.array([MAXLEN], jnp.int32), (TOK_DEV + 1 + extra).astype(jnp.int32)])
    bounds = jnp.cumsum(lengths)
    places = jnp.arange(TOKENS, dtype=jnp.int32)
    segment = 1 + jnp.sum((bounds[None, :] <= places[:, None]).astype(jnp.int32), axis=1)
    return jnp.where(places >= filled, 0, segment).astype(jnp.int32)


def draw_prefix_lengths(key, part):
    key_len = jax.random.fold_in(key, 11)
    key_keep = jax.random.fold_in(key, 12)
    values = jax.random.randint(key_len, (NSEG + 1,), 1, PREF + 1)
    keeping = jax.random.randint(key_keep, (NSEG + 1,), 0, 3) > 0
    values = jnp.where(keeping, values, 0)
    values = values.at[0].set(0).at[1].set(PREF)
    return values.astype(jnp.int32)


def draw_qkv_weight(key, part):
    base = jax.random.normal(key, (D, 3, HEADS * HEAD_DIM), jnp.float32)
    factor = 1.5 * D ** (-0.5)
    return (base * factor).astype(jnp.bfloat16)


def raised(values, rng, source, target, parts, factor):
    owner, partner = [(jnp.arange(values.shape[dim]) // (values.shape[dim] // parts)).reshape([-1 if axis == dim else 1 for axis in range(values.ndim)]) for dim in (source, target)]
    chosen = jax.random.permutation(rng, parts)[partner]
    strong = (owner == chosen) | (owner == (partner + parts // 2) % parts)
    return jnp.where(strong, factor * values, values)


def shard_levels(rng, shape, cuts, low, largest):
    level, own = 1.0, jax.random.fold_in(rng, 6)
    for dim, blocks in cuts:
        steps = jnp.exp(jax.random.uniform(jax.random.fold_in(own, dim), (blocks,), jnp.float32, low / len(cuts), largest / len(cuts)))
        level = level * jnp.repeat(steps, shape[dim] // blocks).reshape([-1 if axis == dim else 1 for axis in range(len(shape))])
    return level


def routed_block(stream_key, own, number, rows, count, top, limit, lean):
    order = jax.random.permutation(stream_key, count)
    heavy_load, common = load_shares(count, rows * top, limit, lean, True), load_shares(count, rows * top, limit, lean, False)
    places = jnp.arange(count)

    def named(tallies, offset_by):
        used = int((tallies > 0).sum())
        fixed = max(1, used // 4)
        moved = fixed + (places - fixed + offset_by * (used - fixed)) % max(1, count - fixed)
        return jnp.zeros((count,), jnp.int32).at[order[jnp.where(places < fixed, places, moved)]].set(jnp.asarray(tallies, jnp.int32))

    tallies = jnp.where(number % 4 == 0, named(heavy_load, number // 4), named(common, number - number // 4 - 1))
    mixed = jax.random.permutation(jax.random.fold_in(own, 3), count)
    source_of, receiver = mixed[0:count // 2 * 2:2], mixed[1:count // 2 * 2:2]
    margin = jnp.minimum(tallies[source_of] - 1, limit - tallies[receiver]) // 2
    margin = jnp.where((source_of == order[0]) | (receiver == order[0]) | (tallies[receiver] == 0), 0, jnp.maximum(margin, 0))
    moved = jax.random.randint(jax.random.fold_in(own, 4), (count // 2,), 0, 1 << 20) % (margin + 1)
    tallies = tallies.at[source_of].add(-moved).at[receiver].add(moved)
    items = jnp.searchsorted(jnp.cumsum(tallies), jnp.arange(rows * top), side="right").astype(jnp.int32)
    listing = items.reshape(top, rows).T
    listing = listing[jax.random.permutation(jax.random.fold_in(own, 1), rows)]
    offset_by = jax.random.randint(jax.random.fold_in(own, 2), (rows, 1), 0, top)
    return jnp.take_along_axis(listing, (jnp.arange(top)[None, :] + offset_by) % top, axis=1)


def load_shares(amount, total, most, lean, full):
    loads = [(1 << 20) // math.isqrt(grade ** lean) + 1 for grade in range(1, amount + 1)]
    largest = most if full else min(most, max(-(-total // amount), total * loads[0] // sum(loads)))
    least = 1 if total - largest >= amount - 1 else 0
    counts, surplus = [largest] + [least] * (amount - 1), total - largest - least * (amount - 1)
    while surplus > 0:
        candidates = [i for i in range(1, amount) if counts[i] < largest] or [i for i in range(1, amount) if counts[i] < most]
        mass, remaining = sum([loads[i] for i in candidates]), surplus
        for i in candidates:
            more = min(most - counts[i], max(1, remaining * loads[i] // mass), surplus)
            counts[i] = counts[i] + more
            surplus = surplus - more
    return np.array(counts)


def normal_values(stream_key, dims, width, bound, cuts=(), kind=jnp.bfloat16):
    drawn = width * jax.random.normal(stream_key, dims, jnp.float32)
    if cuts:
        drawn = drawn * shard_levels(stream_key, dims, cuts, -0.22, 0.18)
    return jnp.clip(drawn, -bound, bound).astype(kind)


def bell_draw_with(rng, shape, width, bound, shards, heavy, kind=jnp.bfloat16):
    values = width * jax.random.normal(rng, shape, jnp.float32)
    if shards:
        values = values * shard_levels(rng, shape, shards, -0.22, 0.18)
    return jnp.clip(raised(values, jax.random.fold_in(rng, 3), *heavy), -bound, bound).astype(kind)


def setup_inputs(seed: int = 0) -> dict:
    key_of = jax.random.split(jax.random.key(seed), 18)
    tokens = normal_values(key_of[0], (TOKENS, D), 1.0, 6.0, ((0, 64), (1, 8)))
    segment_ids = draw_segment_ids(jax.random.fold_in(key_of[17], 71), 0)
    prefix_lengths = draw_prefix_lengths(jax.random.fold_in(key_of[17], 71), 0)
    page_owner_keys = jax.random.split(jax.random.fold_in(key_of[3], 1), PAGES // PAGES_DEV)
    page_owner_turns = jax.random.permutation(jax.random.fold_in(key_of[3], 3), PAGES // PAGES_DEV)
    page_owner = jax.vmap(lambda own, number: routed_block(jax.random.fold_in(key_of[3], 2), own, number, PAGES_DEV, N_REQ, 1, CAPP, 2))(page_owner_keys, page_owner_turns).reshape((PAGES, 1))
    slot_perm = jax.vmap(lambda own: jax.random.permutation(own, POOLP))(jax.random.split(key_of[4], N_REQ)).reshape((N_REQ, POOLP)).astype(jnp.int32)
    ln_gain = jnp.clip(1.0 + 0.18 * jax.random.normal(key_of[5], (D,), jnp.float32), 0.1, 1.9)
    ln_bias = normal_values(key_of[6], (D,), 0.5, 3.0, (), jnp.float32)
    qkv_weight = draw_qkv_weight(jax.random.fold_in(key_of[17], 71), 0)
    qkv_bias = normal_values(key_of[8], (3, HEADS * HEAD_DIM), 0.5, 3.0, ((1, 8),), jnp.float32)
    dense_weight = bell_draw_with(key_of[9], (HEADS * HEAD_DIM, D), (HEADS * HEAD_DIM) ** -0.5, 0.375, ((0, 8), (1, 64)), (0, 1, 64, 4.0))
    dense_bias = normal_values(key_of[10], (D,), 0.5, 3.0, ((0, 8),), jnp.float32)
    fc1_weight = normal_values(key_of[11], (D, FFW), D ** -0.5, 0.125, ((0, 64), (1, 8)))
    fc1_bias = normal_values(key_of[12], (FFW,), 0.5, 3.0, ((0, 8),), jnp.float32)
    fc2_weight = bell_draw_with(key_of[13], (FFW, D), FFW ** -0.5, 0.25, ((0, 8), (1, 64)), (0, 1, 64, 4.0))
    fc2_bias = normal_values(key_of[14], (D,), 0.5, 3.0, ((0, 8),), jnp.float32)
    prefix_cache = normal_values(key_of[15], (N_REQ * PREF, 2, HEADS * HEAD_DIM), 1.5, 9.0, ((0, 64), (2, 8)))
    cache_pool = normal_values(key_of[16], (N_REQ * POOLP * PAGE, 2, HEADS * HEAD_DIM), 1.0, 6.0, ((0, 64), (2, 8)))
    return dict(tokens=tokens, segment_ids=segment_ids, prefix_lengths=prefix_lengths, page_owner=page_owner, slot_perm=slot_perm, ln_gain=ln_gain, ln_bias=ln_bias, qkv_weight=qkv_weight, qkv_bias=qkv_bias, dense_weight=dense_weight, dense_bias=dense_bias, fc1_weight=fc1_weight, fc1_bias=fc1_bias, fc2_weight=fc2_weight, fc2_bias=fc2_bias, prefix_cache=prefix_cache, cache_pool=cache_pool)


EPSILON = 1e-05

def norm_rows(widened, gain, offset_bias):
    average = lax.optimization_barrier(jnp.mean(widened, axis=-1, keepdims=True))
    centred = widened - average
    spread = lax.optimization_barrier(jnp.mean(centred * centred, axis=-1, keepdims=True))
    return (centred * lax.rsqrt(spread + EPSILON) * gain + offset_bias).astype(jnp.bfloat16)

def label_rows(places, starts, prefix_lengths):
    labels = jnp.arange(starts.shape[0], dtype=jnp.int32)
    passed = (starts[None, :] <= places[:, None]) & (labels[None, :] >= 1)
    counted = lax.optimization_barrier(jnp.sum(passed.astype(jnp.int32), axis=1))
    segment = jnp.where(places >= starts[0], 0, counted)
    segment = jnp.where(places < 0, -2, segment)
    onehot = segment[:, None] == labels[None, :]
    earliest = lax.optimization_barrier(jnp.sum(jnp.where(onehot, starts[None, :], 0), axis=1))
    offset = lax.optimization_barrier(jnp.sum(jnp.where(onehot, prefix_lengths[None, :], 0), axis=1))
    return (segment.astype(jnp.int32), (offset + places - earliest).astype(jnp.int32))

def prefix_rows(block_id, rows_dev, prefix_count, starts, prefix_lengths):
    labels = jnp.arange(starts.shape[0], dtype=jnp.int32)
    located = (starts >= block_id * rows_dev) & (starts < (block_id + 1) * rows_dev) & (labels >= 1)
    owner_label = jnp.sum(jnp.where(located, labels, 0))
    length = jnp.sum(jnp.where(located, prefix_lengths, 0))
    places = jnp.arange(prefix_count, dtype=jnp.int32)
    usable = jnp.any(located) & (places < length)
    return (jnp.where(usable, owner_label, -2).astype(jnp.int32), places)

def rotate_heads(values, position):
    half_rot = ROT // 2
    frequency = 10000.0 ** (-2.0 * jnp.arange(half_rot, dtype=jnp.float32) / ROT)
    angles = position.astype(jnp.float32)[:, None] * frequency[None, :]
    cosine = jnp.cos(angles)[:, None, :]
    sine_vals = jnp.sin(angles)[:, None, :]
    lower = values[..., :half_rot]
    upper = values[..., half_rot:ROT]
    return jnp.concatenate([lower * cosine - upper * sine_vals, upper * cosine + lower * sine_vals, values[..., ROT:]], axis=-1)

def head_attention(query_rows, key_rows, value_rows, allowed):
    head_count = query_rows.shape[1] // HEAD_DIM
    score_scale = HEAD_DIM ** (-0.5)

    def one_head(head_index):
        query_cols = lax.dynamic_slice_in_dim(query_rows, head_index * HEAD_DIM, HEAD_DIM, 1)
        key_cols = lax.dynamic_slice_in_dim(key_rows, head_index * HEAD_DIM, HEAD_DIM, 1)
        value_cols = lax.dynamic_slice_in_dim(value_rows, head_index * HEAD_DIM, HEAD_DIM, 1)
        scores = lax.dot_general(query_cols, key_cols, (((1,), (1,)), ((), ())), preferred_element_type=jnp.float32) * score_scale
        masked = jnp.where(allowed, scores, -1e+30)
        highest = lax.optimization_barrier(jnp.max(masked, axis=1, keepdims=True))
        expo = jnp.where(allowed, jnp.exp(masked - highest), 0.0)
        denom = lax.optimization_barrier(jnp.sum(expo, axis=1, keepdims=True))
        mixed = jnp.dot(expo.astype(jnp.bfloat16), value_cols, preferred_element_type=jnp.float32) / denom
        return mixed.astype(jnp.bfloat16)
    outcome = lax.map(one_head, jnp.arange(head_count, dtype=jnp.int32))
    return jnp.transpose(outcome, (1, 0, 2)).reshape(query_rows.shape[0], head_count * HEAD_DIM)

def reference(tokens, segment_ids, prefix_lengths, page_owner, slot_perm, ln_gain, ln_bias, qkv_weight, qkv_bias, dense_weight, dense_bias, fc1_weight, fc1_bias, fc2_weight, fc2_bias, prefix_cache, cache_pool):
    head_width = HEADS * HEAD_DIM
    widened = tokens.astype(jnp.float32)
    normed = norm_rows(widened, ln_gain, ln_bias)
    labels = jnp.arange(NSEG + 1, dtype=jnp.int32)
    places = jnp.arange(TOKENS, dtype=jnp.int32)
    starts = lax.optimization_barrier(jnp.min(jnp.where(segment_ids[:, None] == labels[None, :], places[:, None], TOKENS), axis=0)).astype(jnp.int32)
    projected = jnp.dot(normed, qkv_weight.reshape(D, 3 * head_width), preferred_element_type=jnp.float32)
    projected = (projected + qkv_bias.reshape(1, 3 * head_width)).reshape(TOKENS, 3, HEADS, HEAD_DIM)
    segment, position = label_rows(places, starts, prefix_lengths)
    queries = rotate_heads(projected[:, 0], position).astype(jnp.bfloat16).reshape(TOKENS, head_width)
    new_keys = rotate_heads(projected[:, 1], position).astype(jnp.bfloat16).reshape(TOKENS, head_width)
    new_values = projected[:, 2].astype(jnp.bfloat16).reshape(TOKENS, head_width)
    new_kv = jnp.stack([new_keys, new_values], axis=1)
    padded = jnp.concatenate([jnp.zeros((SPAN * TOK_DEV, 2, head_width), jnp.bfloat16), new_kv], axis=0)
    prefix_padded = jnp.concatenate([jnp.zeros((SPAN * PREF, 2, head_width), jnp.bfloat16), prefix_cache], axis=0)
    row_ids = jnp.arange(TOK_DEV, dtype=jnp.int32)

    def one_block(block_index):
        query_rows = lax.dynamic_slice_in_dim(queries, block_index * TOK_DEV, TOK_DEV, 0)
        query_seg = lax.dynamic_slice_in_dim(segment, block_index * TOK_DEV, TOK_DEV, 0)
        query_pos = lax.dynamic_slice_in_dim(position, block_index * TOK_DEV, TOK_DEV, 0)
        pieces = []
        key_segs = []
        key_poss = []
        for step_back in range(SPAN + 1):
            block_id = block_index - step_back
            pieces.append(lax.dynamic_slice_in_dim(padded, (block_id + SPAN) * TOK_DEV, TOK_DEV, 0))
            pieces.append(lax.dynamic_slice_in_dim(prefix_padded, (block_id + SPAN) * PREF, PREF, 0))
            seg_new, pos_new = label_rows(block_id * TOK_DEV + row_ids, starts, prefix_lengths)
            seg_old, pos_old = prefix_rows(block_id, TOK_DEV, PREF, starts, prefix_lengths)
            key_segs.extend([seg_new, seg_old])
            key_poss.extend([pos_new, pos_old])
        all_keys = jnp.concatenate(pieces, axis=0)
        key_segment = jnp.concatenate(key_segs)
        key_position = jnp.concatenate(key_poss)
        allowed = (key_segment[None, :] == query_seg[:, None]) & (key_position[None, :] <= query_pos[:, None])
        allowed = allowed & ((query_pos[:, None] - key_position[None, :] < WINDOW) | (key_position[None, :] < SINKS))
        return head_attention(query_rows, all_keys[:, 0, :], all_keys[:, 1, :], allowed)
    attended = lax.map(one_block, jnp.arange(N_REQ, dtype=jnp.int32)).reshape(TOKENS, head_width)
    lifted = jnp.dot(normed, fc1_weight, preferred_element_type=jnp.float32) + fc1_bias
    hidden = jax.nn.gelu(lifted, approximate=True).astype(jnp.bfloat16)
    branches = jnp.dot(attended, dense_weight, preferred_element_type=jnp.float32) + jnp.dot(hidden, fc2_weight, preferred_element_type=jnp.float32)
    layer_out = (widened + branches + dense_bias + fc2_bias).astype(jnp.bfloat16)
    pages = new_kv.reshape(PAGES, PAGE * 2 * head_width)
    owners = page_owner[:, 0].reshape(N_REQ, PAGES_DEV)
    onehot = (owners[:, :, None] == jnp.arange(N_REQ, dtype=jnp.int32)[None, None, :]).astype(jnp.int32)
    earlier = jnp.cumsum(onehot, axis=1) - onehot
    earlier_count = lax.optimization_barrier(jnp.sum(earlier * onehot, axis=2))
    source_ids = jnp.arange(N_REQ, dtype=jnp.int32)[:, None]
    column = (source_ids * CAPP + earlier_count).astype(jnp.int32)
    slot_ids = slot_perm[owners, column]
    target = (owners * POOLP + slot_ids).reshape(PAGES).astype(jnp.int32)
    pool_pages = cache_pool.reshape(N_REQ * POOLP, PAGE * 2 * head_width).at[target].set(pages)
    new_pool = pool_pages.reshape(cache_pool.shape)
    return (layer_out, new_pool)
```

```python
import jax
import jax.numpy as jnp
from jax import lax
from jax.sharding import PartitionSpec as P

HEAD_DIM = 64
ROT = 32
SPAN = 2
SINKS = 4
PAGE = 4
WINDOW = 512


EPSILON = 1e-05


def from_behind(value, axis, steps):
    count = lax.axis_size(axis)
    leading, last = (max(0, -steps), min(count, count - steps))
    return lax.ppermute(value, axis, [(source, source + steps) for source in range(leading, last)])


def norm_rows(widened, gain, offset_bias):
    average = jnp.mean(widened, axis=-1, keepdims=True)
    centred = widened - average
    spread = jnp.mean(centred * centred, axis=-1, keepdims=True)
    return (centred * lax.rsqrt(spread + EPSILON) * gain + offset_bias).astype(jnp.bfloat16)


def label_rows(places, starts, prefix_lengths):
    labels = jnp.arange(starts.shape[0], dtype=jnp.int32)
    passed = (starts[None, :] <= places[:, None]) & (labels[None, :] >= 1)
    counted = jnp.sum(passed.astype(jnp.int32), axis=1)
    segment = jnp.where(places >= starts[0], 0, counted)
    segment = jnp.where(places < 0, -2, segment)
    onehot = segment[:, None] == labels[None, :]
    earliest = jnp.sum(jnp.where(onehot, starts[None, :], 0), axis=1)
    offset = jnp.sum(jnp.where(onehot, prefix_lengths[None, :], 0), axis=1)
    return (segment, offset + places - earliest)


def prefix_rows(block_id, rows_dev, prefix_count, starts, prefix_lengths):
    labels = jnp.arange(starts.shape[0], dtype=jnp.int32)
    located = (starts >= block_id * rows_dev) & (starts < (block_id + 1) * rows_dev) & (labels >= 1)
    owner_label = jnp.sum(jnp.where(located, labels, 0))
    length = jnp.sum(jnp.where(located, prefix_lengths, 0))
    places = jnp.arange(prefix_count, dtype=jnp.int32)
    usable = jnp.any(located) & (places < length)
    return (jnp.where(usable, owner_label, -2), places)


def rotate_heads(values, position):
    half_rot = ROT // 2
    frequency = 10000.0 ** (-2.0 * jnp.arange(half_rot, dtype=jnp.float32) / ROT)
    angles = position.astype(jnp.float32)[:, None] * frequency[None, :]
    cosine = jnp.cos(angles)[:, None, :]
    sine_vals = jnp.sin(angles)[:, None, :]
    lower = values[..., :half_rot]
    upper = values[..., half_rot:ROT]
    return jnp.concatenate(
        [lower * cosine - upper * sine_vals, upper * cosine + lower * sine_vals, values[..., ROT:]],
        axis=-1,
    )


def head_attention(query_rows, key_rows, value_rows, allowed):
    head_count = query_rows.shape[1] // HEAD_DIM
    score_scale = HEAD_DIM ** (-0.5)

    def one_head(head_index):
        query_cols = lax.dynamic_slice_in_dim(query_rows, head_index * HEAD_DIM, HEAD_DIM, 1)
        key_cols = lax.dynamic_slice_in_dim(key_rows, head_index * HEAD_DIM, HEAD_DIM, 1)
        value_cols = lax.dynamic_slice_in_dim(value_rows, head_index * HEAD_DIM, HEAD_DIM, 1)
        scores = (
            lax.dot_general(
                query_cols, key_cols, (((1,), (1,)), ((), ())), preferred_element_type=jnp.float32
            )
            * score_scale
        )
        masked = jnp.where(allowed, scores, -1e30)
        highest = jnp.max(masked, axis=1, keepdims=True)
        expo = jnp.where(allowed, jnp.exp(masked - highest), 0.0)
        denom = jnp.sum(expo, axis=1, keepdims=True)
        mixed = (
            jnp.dot(expo.astype(jnp.bfloat16), value_cols, preferred_element_type=jnp.float32)
            / denom
        )
        return mixed.astype(jnp.bfloat16)

    outcome = lax.map(one_head, jnp.arange(head_count, dtype=jnp.int32))
    return jnp.transpose(outcome, (1, 0, 2)).reshape(query_rows.shape[0], head_count * HEAD_DIM)


def shards(
    tokens,
    segment_ids,
    prefix_lengths,
    page_owner,
    slot_perm,
    ln_gain,
    ln_bias,
    qkv_weight,
    qkv_bias,
    dense_weight,
    dense_bias,
    fc1_weight,
    fc1_bias,
    fc2_weight,
    fc2_bias,
    prefix_cache,
    cache_pool,
):
    req_count = lax.axis_size("req")
    req_index = lax.axis_index("req")
    tok_rows = tokens.shape[0]
    prefix_count = prefix_cache.shape[0]
    head_cols = qkv_weight.shape[2]
    pool_count = slot_perm.shape[1]
    page_cap = pool_count // req_count
    gathered = lax.all_gather(tokens, "tensor", axis=1, tiled=True)
    normed = norm_rows(gathered.astype(jnp.float32), ln_gain, ln_bias)
    row_ids = jnp.arange(tok_rows, dtype=jnp.int32)
    places = req_index * tok_rows + row_ids
    labels = jnp.arange(prefix_lengths.shape[0], dtype=jnp.int32)
    label_count = labels.shape[0]
    beyond = tok_rows * req_count
    earliest_rows = jnp.min(
        jnp.where(segment_ids[:, None] == labels[None, :], places[:, None], beyond), axis=0
    )
    weight_rows = qkv_weight.shape[0]
    digit_cols = 128
    digits = jnp.concatenate([earliest_rows // 128, earliest_rows % 128]).astype(jnp.bfloat16)
    digits = jnp.pad(digits, (0, weight_rows * digit_cols - 2 * label_count)).reshape(
        weight_rows, digit_cols
    )
    qkv_local = qkv_weight.reshape(weight_rows, 3 * head_cols)
    fc1_cols = fc1_weight.shape[1]
    dense_cols = dense_weight.shape[0]
    fc2_cols = fc2_weight.shape[0]
    packed = jnp.concatenate(
        [qkv_local, fc1_weight, dense_weight.T, fc2_weight.T, digits], axis=1
    )
    everything = lax.all_gather(packed, "req", axis=0, tiled=True)
    edges = [0]
    for width in (3 * head_cols, fc1_cols, dense_cols, fc2_cols, digit_cols):
        edges.append(edges[-1] + width)
    qkv_full, fc1_full, dense_full_t, fc2_full_t, digits_full = [
        everything[:, edges[i] : edges[i + 1]] for i in range(5)
    ]
    digit_table = digits_full.reshape(req_count, weight_rows * digit_cols)[:, : 2 * label_count]
    digit_table = digit_table.astype(jnp.int32)
    starts = jnp.min(
        digit_table[:, :label_count] * 128 + digit_table[:, label_count:], axis=0
    )

    def add_rows(portion):
        return jnp.dot(normed, portion, preferred_element_type=jnp.float32)

    projected = add_rows(qkv_full)
    lifted = add_rows(fc1_full)
    projected = (projected + qkv_bias.reshape(1, 3 * head_cols)).reshape(
        tok_rows, 3, head_cols // HEAD_DIM, HEAD_DIM
    )
    segment, position = label_rows(places, starts, prefix_lengths)
    queries = (
        rotate_heads(projected[:, 0], position).astype(jnp.bfloat16).reshape(tok_rows, head_cols)
    )
    new_keys = (
        rotate_heads(projected[:, 1], position).astype(jnp.bfloat16).reshape(tok_rows, head_cols)
    )
    new_values = projected[:, 2].astype(jnp.bfloat16).reshape(tok_rows, head_cols)
    key_value = jnp.stack([new_keys, new_values], axis=1)
    pages_here = tok_rows // PAGE
    page_width = PAGE * 2 * head_cols
    pages = key_value.reshape(pages_here, page_width)
    owners = page_owner[:, 0]
    onehot = (owners[:, None] == jnp.arange(req_count, dtype=jnp.int32)[None, :]).astype(jnp.int32)
    earlier = jnp.cumsum(onehot, axis=0) - onehot
    earlier_count = jnp.sum(earlier * onehot, axis=1)
    target = owners * page_cap + earlier_count
    selecting = (target[None, :] == jnp.arange(pool_count, dtype=jnp.int32)[:, None]).astype(
        jnp.bfloat16
    )
    outgoing = jnp.dot(selecting, pages, preferred_element_type=jnp.float32).astype(jnp.bfloat16)
    filled = jnp.sum(selecting, axis=1)
    flag_cols = 128
    flagged = jnp.concatenate(
        [outgoing, jnp.broadcast_to(filled[:, None], (pool_count, flag_cols)).astype(jnp.bfloat16)],
        axis=1,
    )
    arrived = lax.all_to_all(
        flagged.reshape(req_count, page_cap, page_width + flag_cols),
        "req",
        split_axis=0,
        concat_axis=0,
        tiled=True,
    ).reshape(pool_count, page_width + flag_cols)
    incoming = arrived[:, :page_width]
    incoming_filled = arrived[:, page_width]
    slot_ids = slot_perm[0]
    placing = (slot_ids[None, :] == jnp.arange(pool_count, dtype=jnp.int32)[:, None]) & (
        incoming_filled[None, :] > 0
    )
    written = jnp.dot(
        placing.astype(jnp.bfloat16),
        incoming,
        preferred_element_type=jnp.float32,
    ).astype(jnp.bfloat16)
    written_mask = jnp.any(placing, axis=1)
    pool_pages = cache_pool.reshape(pool_count, page_width)
    new_pool = jnp.where(written_mask[:, None], written, pool_pages).reshape(cache_pool.shape)
    local_keys = jnp.concatenate([key_value, prefix_cache], axis=0)
    blocks = [local_keys]
    for shift_by in range(1, SPAN + 1):
        blocks.append(from_behind(local_keys, "req", shift_by))
    key_segs = []
    key_poss = []
    for step_back in range(SPAN + 1):
        block_id = req_index - step_back
        seg_new, pos_new = label_rows(block_id * tok_rows + row_ids, starts, prefix_lengths)
        seg_old, pos_old = prefix_rows(block_id, tok_rows, prefix_count, starts, prefix_lengths)
        key_segs.extend([seg_new, seg_old])
        key_poss.extend([pos_new, pos_old])
    key_segment = jnp.concatenate(key_segs)
    key_position = jnp.concatenate(key_poss)
    allowed = (key_segment[None, :] == segment[:, None]) & (
        key_position[None, :] <= position[:, None]
    )
    allowed = allowed & (
        (position[:, None] - key_position[None, :] < WINDOW) | (key_position[None, :] < SINKS)
    )
    all_keys = jnp.concatenate(blocks, axis=0)
    attended = head_attention(queries, all_keys[:, 0, :], all_keys[:, 1, :], allowed)
    hidden = jax.nn.gelu(lifted + fc1_bias, approximate=True).astype(jnp.bfloat16)
    contract_rows = (((1,), (1,)), ((), ()))
    attn_part = lax.dot_general(
        attended, dense_full_t, contract_rows, preferred_element_type=jnp.float32
    )
    mlp_part = lax.dot_general(
        hidden, fc2_full_t, contract_rows, preferred_element_type=jnp.float32
    )
    branches = attn_part + mlp_part
    summed = lax.psum_scatter(branches, "tensor", scatter_dimension=1, tiled=True)
    layer_out = (tokens.astype(jnp.float32) + summed + dense_bias + fc2_bias).astype(jnp.bfloat16)
    return (layer_out, new_pool)


def solution(mesh):
    placed = (
        P("req", "tensor"),
        P("req"),
        P(),
        P("req", None),
        P("req", None),
        P(),
        P(),
        P("req", None, "tensor"),
        P(None, "tensor"),
        P("tensor", "req"),
        P("tensor"),
        P("req", "tensor"),
        P("tensor"),
        P("tensor", "req"),
        P("tensor"),
        P("req", None, "tensor"),
        P("req", None, "tensor"),
    )
    return jax.shard_map(
        shards,
        mesh=mesh,
        in_specs=placed,
        out_specs=(P("req", "tensor"), P("req", None, "tensor")),
        check_vma=False,
    )
```

```python
import functools

import jax
import jax.numpy as jnp
from jax import lax
from jax.experimental import pallas as pl
from jax.experimental.pallas import tpu as pltpu
from jax.sharding import PartitionSpec as P

HEAD_DIM = 64
ROT = 32
SPAN = 2
SINKS = 4
PAGE = 4
WINDOW = 512
INNER = 4


MESH_IDS = pl.DeviceIdType.MESH


def ring_gather_kernel(inner, outer, block_ref, out_ref, own_sem, send_sems, recv_sems):
    req_index = lax.axis_index("req")
    tensor_index = lax.axis_index("tensor")
    here_outer = req_index // inner
    here_inner = req_index % inner

    def device(outer_at, inner_at):
        outer_at = lax.rem(outer_at + outer, outer)
        inner_at = lax.rem(inner_at + inner, inner)
        return (outer_at * inner + inner_at, tensor_index)

    neighbours = (
        device(here_outer, here_inner + 1),
        device(here_outer, here_inner - 1),
        device(here_outer + 1, here_inner),
        device(here_outer - 1, here_inner),
    )
    barrier = pltpu.get_barrier_semaphore()
    for neighbour in neighbours:
        pl.semaphore_signal(barrier, inc=1, device_id=neighbour, device_id_type=MESH_IDS)
    pl.semaphore_wait(barrier, len(neighbours))

    own = pltpu.make_async_copy(block_ref, out_ref.at[here_outer, here_inner], own_sem)
    own.start()
    sent = []

    def run_ring(stage, count, place, first_source, step_to):
        plans = [(0, 1, count // 2), (1, -1, (count - 1) // 2)]
        pending = [None, None]
        for step in range(1, count // 2 + 1):
            for direction, sign, steps in plans:
                if step > steps:
                    continue
                origin = -sign * (step - 1)
                if step > 1:
                    pending[direction].wait_recv()
                source = first_source if step == 1 else place(origin)
                copy = pltpu.make_async_remote_copy(
                    src_ref=source,
                    dst_ref=place(origin),
                    send_sem=send_sems.at[stage, direction, step - 1],
                    recv_sem=recv_sems.at[stage, direction, step - 1],
                    device_id=step_to(sign),
                    device_id_type=MESH_IDS,
                )
                copy.start()
                sent.append(copy)
                pending[direction] = pltpu.make_async_remote_copy(
                    src_ref=source,
                    dst_ref=place(-sign * step),
                    send_sem=send_sems.at[stage, direction, step - 1],
                    recv_sem=recv_sems.at[stage, direction, step - 1],
                    device_id=step_to(sign),
                    device_id_type=MESH_IDS,
                )
        for waiting in pending:
            if waiting is not None:
                waiting.wait_recv()

    def inner_place(offset):
        return out_ref.at[here_outer, lax.rem(here_inner + offset + inner, inner)]

    def outer_place(offset):
        return out_ref.at[lax.rem(here_outer + offset + outer, outer)]

    run_ring(0, inner, inner_place, block_ref, lambda sign: device(here_outer, here_inner + sign))
    own.wait()
    run_ring(1, outer, outer_place, out_ref.at[here_outer], lambda sign: device(here_outer + sign, here_inner))
    for copy in sent:
        copy.wait_send()


def ring_gather(block, inner, outer):
    rows, cols = block.shape
    most_steps = max(inner, outer) // 2
    return pl.pallas_call(
        functools.partial(ring_gather_kernel, inner, outer),
        out_shape=jax.ShapeDtypeStruct((outer, inner, rows, cols), block.dtype),
        in_specs=[pl.BlockSpec(memory_space=pl.ANY)],
        out_specs=pl.BlockSpec(memory_space=pl.ANY),
        scratch_shapes=[
            pltpu.SemaphoreType.DMA(()),
            pltpu.SemaphoreType.DMA((2, 2, most_steps)),
            pltpu.SemaphoreType.DMA((2, 2, most_steps)),
        ],
        compiler_params=pltpu.CompilerParams(collective_id=0, has_side_effects=True),
    )(block).reshape(outer * inner * rows, cols)


EPSILON = 1e-05


def from_behind(value, axis, steps):
    count = lax.axis_size(axis)
    leading, last = (max(0, -steps), min(count, count - steps))
    return lax.ppermute(value, axis, [(source, source + steps) for source in range(leading, last)])


def norm_rows(widened, gain, offset_bias):
    average = jnp.mean(widened, axis=-1, keepdims=True)
    centred = widened - average
    spread = jnp.mean(centred * centred, axis=-1, keepdims=True)
    return (centred * lax.rsqrt(spread + EPSILON) * gain + offset_bias).astype(jnp.bfloat16)


def label_rows(places, starts, prefix_lengths):
    labels = jnp.arange(starts.shape[0], dtype=jnp.int32)
    passed = (starts[None, :] <= places[:, None]) & (labels[None, :] >= 1)
    counted = jnp.sum(passed.astype(jnp.int32), axis=1)
    segment = jnp.where(places >= starts[0], 0, counted)
    segment = jnp.where(places < 0, -2, segment)
    onehot = segment[:, None] == labels[None, :]
    earliest = jnp.sum(jnp.where(onehot, starts[None, :], 0), axis=1)
    offset = jnp.sum(jnp.where(onehot, prefix_lengths[None, :], 0), axis=1)
    return (segment, offset + places - earliest)


def prefix_rows(block_id, rows_dev, prefix_count, starts, prefix_lengths):
    labels = jnp.arange(starts.shape[0], dtype=jnp.int32)
    located = (starts >= block_id * rows_dev) & (starts < (block_id + 1) * rows_dev) & (labels >= 1)
    owner_label = jnp.sum(jnp.where(located, labels, 0))
    length = jnp.sum(jnp.where(located, prefix_lengths, 0))
    places = jnp.arange(prefix_count, dtype=jnp.int32)
    usable = jnp.any(located) & (places < length)
    return (jnp.where(usable, owner_label, -2), places)


def rotate_heads(values, position):
    half_rot = ROT // 2
    frequency = 10000.0 ** (-2.0 * jnp.arange(half_rot, dtype=jnp.float32) / ROT)
    angles = position.astype(jnp.float32)[:, None] * frequency[None, :]
    cosine = jnp.cos(angles)[:, None, :]
    sine_vals = jnp.sin(angles)[:, None, :]
    lower = values[..., :half_rot]
    upper = values[..., half_rot:ROT]
    return jnp.concatenate(
        [lower * cosine - upper * sine_vals, upper * cosine + lower * sine_vals, values[..., ROT:]],
        axis=-1,
    )


def head_attention(query_rows, key_rows, value_rows, allowed):
    head_count = query_rows.shape[1] // HEAD_DIM
    score_scale = HEAD_DIM ** (-0.5)

    def one_head(head_index):
        query_cols = lax.dynamic_slice_in_dim(query_rows, head_index * HEAD_DIM, HEAD_DIM, 1)
        key_cols = lax.dynamic_slice_in_dim(key_rows, head_index * HEAD_DIM, HEAD_DIM, 1)
        value_cols = lax.dynamic_slice_in_dim(value_rows, head_index * HEAD_DIM, HEAD_DIM, 1)
        scores = (
            lax.dot_general(
                query_cols, key_cols, (((1,), (1,)), ((), ())), preferred_element_type=jnp.float32
            )
            * score_scale
        )
        masked = jnp.where(allowed, scores, -1e30)
        highest = jnp.max(masked, axis=1, keepdims=True)
        expo = jnp.where(allowed, jnp.exp(masked - highest), 0.0)
        denom = jnp.sum(expo, axis=1, keepdims=True)
        mixed = (
            jnp.dot(expo.astype(jnp.bfloat16), value_cols, preferred_element_type=jnp.float32)
            / denom
        )
        return mixed.astype(jnp.bfloat16)

    outcome = lax.map(one_head, jnp.arange(head_count, dtype=jnp.int32))
    return jnp.transpose(outcome, (1, 0, 2)).reshape(query_rows.shape[0], head_count * HEAD_DIM)


def shards(
    tokens,
    segment_ids,
    prefix_lengths,
    page_owner,
    slot_perm,
    ln_gain,
    ln_bias,
    qkv_weight,
    qkv_bias,
    dense_weight,
    dense_bias,
    fc1_weight,
    fc1_bias,
    fc2_weight,
    fc2_bias,
    prefix_cache,
    cache_pool,
):
    req_count = lax.axis_size("req")
    req_index = lax.axis_index("req")
    tok_rows = tokens.shape[0]
    prefix_count = prefix_cache.shape[0]
    head_cols = qkv_weight.shape[2]
    pool_count = slot_perm.shape[1]
    page_cap = pool_count // req_count
    gathered = lax.all_gather(tokens, "tensor", axis=1, tiled=True)
    normed = norm_rows(gathered.astype(jnp.float32), ln_gain, ln_bias)
    row_ids = jnp.arange(tok_rows, dtype=jnp.int32)
    places = req_index * tok_rows + row_ids
    labels = jnp.arange(prefix_lengths.shape[0], dtype=jnp.int32)
    label_count = labels.shape[0]
    beyond = tok_rows * req_count
    earliest_rows = jnp.min(
        jnp.where(segment_ids[:, None] == labels[None, :], places[:, None], beyond), axis=0
    )
    weight_rows = qkv_weight.shape[0]
    digit_cols = 128
    digits = jnp.concatenate([earliest_rows // 128, earliest_rows % 128]).astype(jnp.bfloat16)
    digits = jnp.pad(digits, (0, weight_rows * digit_cols - 2 * label_count)).reshape(
        weight_rows, digit_cols
    )
    qkv_local = qkv_weight.reshape(weight_rows, 3 * head_cols)
    fc1_cols = fc1_weight.shape[1]
    dense_cols = dense_weight.shape[0]
    fc2_cols = fc2_weight.shape[0]
    packed = jnp.concatenate(
        [qkv_local, fc1_weight, dense_weight.T, fc2_weight.T, digits], axis=1
    )
    everything = ring_gather(packed, INNER, req_count // INNER)
    edges = [0]
    for width in (3 * head_cols, fc1_cols, dense_cols, fc2_cols, digit_cols):
        edges.append(edges[-1] + width)
    qkv_full, fc1_full, dense_full_t, fc2_full_t, digits_full = [
        everything[:, edges[i] : edges[i + 1]] for i in range(5)
    ]
    digit_table = digits_full.reshape(req_count, weight_rows * digit_cols)[:, : 2 * label_count]
    digit_table = digit_table.astype(jnp.int32)
    starts = jnp.min(
        digit_table[:, :label_count] * 128 + digit_table[:, label_count:], axis=0
    )

    def add_rows(portion):
        return jnp.dot(normed, portion, preferred_element_type=jnp.float32)

    projected = add_rows(qkv_full)
    lifted = add_rows(fc1_full)
    projected = (projected + qkv_bias.reshape(1, 3 * head_cols)).reshape(
        tok_rows, 3, head_cols // HEAD_DIM, HEAD_DIM
    )
    segment, position = label_rows(places, starts, prefix_lengths)
    queries = (
        rotate_heads(projected[:, 0], position).astype(jnp.bfloat16).reshape(tok_rows, head_cols)
    )
    new_keys = (
        rotate_heads(projected[:, 1], position).astype(jnp.bfloat16).reshape(tok_rows, head_cols)
    )
    new_values = projected[:, 2].astype(jnp.bfloat16).reshape(tok_rows, head_cols)
    key_value = jnp.stack([new_keys, new_values], axis=1)
    pages_here = tok_rows // PAGE
    page_width = PAGE * 2 * head_cols
    pages = key_value.reshape(pages_here, page_width)
    owners = page_owner[:, 0]
    onehot = (owners[:, None] == jnp.arange(req_count, dtype=jnp.int32)[None, :]).astype(jnp.int32)
    earlier = jnp.cumsum(onehot, axis=0) - onehot
    earlier_count = jnp.sum(earlier * onehot, axis=1)
    target = owners * page_cap + earlier_count
    selecting = (target[None, :] == jnp.arange(pool_count, dtype=jnp.int32)[:, None]).astype(
        jnp.bfloat16
    )
    outgoing = jnp.dot(selecting, pages, preferred_element_type=jnp.float32).astype(jnp.bfloat16)
    filled = jnp.sum(selecting, axis=1)
    flag_cols = 128
    flagged = jnp.concatenate(
        [outgoing, jnp.broadcast_to(filled[:, None], (pool_count, flag_cols)).astype(jnp.bfloat16)],
        axis=1,
    )
    arrived = lax.all_to_all(
        flagged.reshape(req_count, page_cap, page_width + flag_cols),
        "req",
        split_axis=0,
        concat_axis=0,
        tiled=True,
    ).reshape(pool_count, page_width + flag_cols)
    incoming = arrived[:, :page_width]
    incoming_filled = arrived[:, page_width]
    slot_ids = slot_perm[0]
    placing = (slot_ids[None, :] == jnp.arange(pool_count, dtype=jnp.int32)[:, None]) & (
        incoming_filled[None, :] > 0
    )
    written = jnp.dot(
        placing.astype(jnp.bfloat16),
        incoming,
        preferred_element_type=jnp.float32,
    ).astype(jnp.bfloat16)
    written_mask = jnp.any(placing, axis=1)
    pool_pages = cache_pool.reshape(pool_count, page_width)
    new_pool = jnp.where(written_mask[:, None], written, pool_pages).reshape(cache_pool.shape)
    local_keys = jnp.concatenate([key_value, prefix_cache], axis=0)
    blocks = [local_keys]
    for shift_by in range(1, SPAN + 1):
        blocks.append(from_behind(local_keys, "req", shift_by))
    key_segs = []
    key_poss = []
    for step_back in range(SPAN + 1):
        block_id = req_index - step_back
        seg_new, pos_new = label_rows(block_id * tok_rows + row_ids, starts, prefix_lengths)
        seg_old, pos_old = prefix_rows(block_id, tok_rows, prefix_count, starts, prefix_lengths)
        key_segs.extend([seg_new, seg_old])
        key_poss.extend([pos_new, pos_old])
    key_segment = jnp.concatenate(key_segs)
    key_position = jnp.concatenate(key_poss)
    allowed = (key_segment[None, :] == segment[:, None]) & (
        key_position[None, :] <= position[:, None]
    )
    allowed = allowed & (
        (position[:, None] - key_position[None, :] < WINDOW) | (key_position[None, :] < SINKS)
    )
    all_keys = jnp.concatenate(blocks, axis=0)
    attended = head_attention(queries, all_keys[:, 0, :], all_keys[:, 1, :], allowed)
    hidden = jax.nn.gelu(lifted + fc1_bias, approximate=True).astype(jnp.bfloat16)
    contract_rows = (((1,), (1,)), ((), ()))
    attn_part = lax.dot_general(
        attended, dense_full_t, contract_rows, preferred_element_type=jnp.float32
    )
    mlp_part = lax.dot_general(
        hidden, fc2_full_t, contract_rows, preferred_element_type=jnp.float32
    )
    branches = attn_part + mlp_part
    summed = lax.psum_scatter(branches, "tensor", scatter_dimension=1, tiled=True)
    layer_out = (tokens.astype(jnp.float32) + summed + dense_bias + fc2_bias).astype(jnp.bfloat16)
    return (layer_out, new_pool)


def solution(mesh):
    placed = (
        P("req", "tensor"),
        P("req"),
        P(),
        P("req", None),
        P("req", None),
        P(),
        P(),
        P("req", None, "tensor"),
        P(None, "tensor"),
        P("tensor", "req"),
        P("tensor"),
        P("req", "tensor"),
        P("tensor"),
        P("tensor", "req"),
        P("tensor"),
        P("req", None, "tensor"),
        P("req", None, "tensor"),
    )
    return jax.shard_map(
        shards,
        mesh=mesh,
        in_specs=placed,
        out_specs=(P("req", "tensor"), P("req", None, "tensor")),
        check_vma=False,
    )
```

```python
import functools

import jax
import jax.numpy as jnp
from jax import lax
from jax.experimental import pallas as pl
from jax.experimental.pallas import tpu as pltpu
from jax.sharding import PartitionSpec as P

HEAD_DIM = 64
ROT = 32
SPAN = 2
SINKS = 4
PAGE = 4
WINDOW = 512
INNER = 4


MESH_IDS = pl.DeviceIdType.MESH


def ring_gather_kernel(inner, outer, block_ref, out_ref, own_sem, send_sems, recv_sems):
    req_index = lax.axis_index("req")
    tensor_index = lax.axis_index("tensor")
    here_outer = req_index // inner
    here_inner = req_index % inner

    def device(outer_at, inner_at):
        outer_at = lax.rem(outer_at + outer, outer)
        inner_at = lax.rem(inner_at + inner, inner)
        return (outer_at * inner + inner_at, tensor_index)

    neighbours = (
        device(here_outer, here_inner + 1),
        device(here_outer, here_inner - 1),
        device(here_outer + 1, here_inner),
        device(here_outer - 1, here_inner),
    )
    barrier = pltpu.get_barrier_semaphore()
    for neighbour in neighbours:
        pl.semaphore_signal(barrier, inc=1, device_id=neighbour, device_id_type=MESH_IDS)
    pl.semaphore_wait(barrier, len(neighbours))

    own = pltpu.make_async_copy(block_ref, out_ref.at[here_outer, here_inner], own_sem)
    own.start()
    sent = []

    def run_ring(stage, count, place, first_source, step_to):
        plans = [(0, 1, count // 2), (1, -1, (count - 1) // 2)]
        pending = [None, None]
        for step in range(1, count // 2 + 1):
            for direction, sign, steps in plans:
                if step > steps:
                    continue
                origin = -sign * (step - 1)
                if step > 1:
                    pending[direction].wait_recv()
                source = first_source if step == 1 else place(origin)
                copy = pltpu.make_async_remote_copy(
                    src_ref=source,
                    dst_ref=place(origin),
                    send_sem=send_sems.at[stage, direction, step - 1],
                    recv_sem=recv_sems.at[stage, direction, step - 1],
                    device_id=step_to(sign),
                    device_id_type=MESH_IDS,
                )
                copy.start()
                sent.append(copy)
                pending[direction] = pltpu.make_async_remote_copy(
                    src_ref=source,
                    dst_ref=place(-sign * step),
                    send_sem=send_sems.at[stage, direction, step - 1],
                    recv_sem=recv_sems.at[stage, direction, step - 1],
                    device_id=step_to(sign),
                    device_id_type=MESH_IDS,
                )
        for waiting in pending:
            if waiting is not None:
                waiting.wait_recv()

    def inner_place(offset):
        return out_ref.at[here_outer, lax.rem(here_inner + offset + inner, inner)]

    def outer_place(offset):
        return out_ref.at[lax.rem(here_outer + offset + outer, outer)]

    run_ring(0, inner, inner_place, block_ref, lambda sign: device(here_outer, here_inner + sign))
    own.wait()
    run_ring(1, outer, outer_place, out_ref.at[here_outer], lambda sign: device(here_outer + sign, here_inner))
    for copy in sent:
        copy.wait_send()


def ring_gather(block, inner, outer):
    rows, cols = block.shape
    most_steps = max(inner, outer) // 2
    return pl.pallas_call(
        functools.partial(ring_gather_kernel, inner, outer),
        out_shape=jax.ShapeDtypeStruct((outer, inner, rows, cols), block.dtype),
        in_specs=[pl.BlockSpec(memory_space=pl.ANY)],
        out_specs=pl.BlockSpec(memory_space=pl.ANY),
        scratch_shapes=[
            pltpu.SemaphoreType.DMA(()),
            pltpu.SemaphoreType.DMA((2, 2, most_steps)),
            pltpu.SemaphoreType.DMA((2, 2, most_steps)),
        ],
        compiler_params=pltpu.CompilerParams(collective_id=0, has_side_effects=True),
    )(block).reshape(outer * inner * rows, cols)


def exchange_kernel(count, outgoing_ref, keys_ref, incoming_ref, behind_ref, own_sem, send_sems,
                    recv_sems, shift_send, shift_recv):
    here = lax.axis_index("req")
    tensor_index = lax.axis_index("tensor")

    def device(offset):
        return (lax.rem(here + offset + count, count), tensor_index)

    barrier = pltpu.get_barrier_semaphore()

    def greet(offset, carry):
        pl.semaphore_signal(barrier, inc=1, device_id=device(offset), device_id_type=MESH_IDS)
        return carry

    lax.fori_loop(1, count, greet, 0)
    pl.semaphore_wait(barrier, count - 1)

    own = pltpu.make_async_copy(outgoing_ref.at[here], incoming_ref.at[here], own_sem)
    own.start()

    def shift_copy(step):
        return pltpu.make_async_remote_copy(
            src_ref=keys_ref,
            dst_ref=behind_ref.at[step],
            send_sem=shift_send.at[step],
            recv_sem=shift_recv.at[step],
            device_id=device(step + 1),
            device_id_type=MESH_IDS,
        )

    for step in range(2):
        shift_copy(step).start()

    def page_copy(offset, source_at, target_at):
        return pltpu.make_async_remote_copy(
            src_ref=outgoing_ref.at[source_at],
            dst_ref=incoming_ref.at[target_at],
            send_sem=send_sems.at[offset],
            recv_sem=recv_sems.at[offset],
            device_id=device(offset),
            device_id_type=MESH_IDS,
        )

    def push(offset, carry):
        page_copy(offset, lax.rem(here + offset, count), here).start()
        return carry

    lax.fori_loop(1, count, push, 0)

    def settle(offset, carry):
        page_copy(offset, lax.rem(here + offset, count), here).wait_send()
        page_copy(offset, here, lax.rem(here - offset + count, count)).wait_recv()
        return carry

    lax.fori_loop(1, count, settle, 0)
    for step in range(2):
        shift_copy(step).wait_send()
        shift_copy(step).wait_recv()
    own.wait()


def exchange(outgoing, keys):
    count = outgoing.shape[0]
    return pl.pallas_call(
        functools.partial(exchange_kernel, count),
        out_shape=(
            jax.ShapeDtypeStruct(outgoing.shape, outgoing.dtype),
            jax.ShapeDtypeStruct((2,) + keys.shape, keys.dtype),
        ),
        in_specs=[pl.BlockSpec(memory_space=pl.ANY)] * 2,
        out_specs=(pl.BlockSpec(memory_space=pl.ANY), pl.BlockSpec(memory_space=pl.ANY)),
        scratch_shapes=[
            pltpu.SemaphoreType.DMA(()),
            pltpu.SemaphoreType.DMA((count,)),
            pltpu.SemaphoreType.DMA((count,)),
            pltpu.SemaphoreType.DMA((2,)),
            pltpu.SemaphoreType.DMA((2,)),
        ],
        compiler_params=pltpu.CompilerParams(collective_id=1, has_side_effects=True),
    )(outgoing, keys)


EPSILON = 1e-05


def from_behind(value, axis, steps):
    count = lax.axis_size(axis)
    leading, last = (max(0, -steps), min(count, count - steps))
    return lax.ppermute(value, axis, [(source, source + steps) for source in range(leading, last)])


def norm_rows(widened, gain, offset_bias):
    average = jnp.mean(widened, axis=-1, keepdims=True)
    centred = widened - average
    spread = jnp.mean(centred * centred, axis=-1, keepdims=True)
    return (centred * lax.rsqrt(spread + EPSILON) * gain + offset_bias).astype(jnp.bfloat16)


def label_rows(places, starts, prefix_lengths):
    labels = jnp.arange(starts.shape[0], dtype=jnp.int32)
    passed = (starts[None, :] <= places[:, None]) & (labels[None, :] >= 1)
    counted = jnp.sum(passed.astype(jnp.int32), axis=1)
    segment = jnp.where(places >= starts[0], 0, counted)
    segment = jnp.where(places < 0, -2, segment)
    onehot = segment[:, None] == labels[None, :]
    earliest = jnp.sum(jnp.where(onehot, starts[None, :], 0), axis=1)
    offset = jnp.sum(jnp.where(onehot, prefix_lengths[None, :], 0), axis=1)
    return (segment, offset + places - earliest)


def prefix_rows(block_id, rows_dev, prefix_count, starts, prefix_lengths):
    labels = jnp.arange(starts.shape[0], dtype=jnp.int32)
    located = (starts >= block_id * rows_dev) & (starts < (block_id + 1) * rows_dev) & (labels >= 1)
    owner_label = jnp.sum(jnp.where(located, labels, 0))
    length = jnp.sum(jnp.where(located, prefix_lengths, 0))
    places = jnp.arange(prefix_count, dtype=jnp.int32)
    usable = jnp.any(located) & (places < length)
    return (jnp.where(usable, owner_label, -2), places)


def rotate_heads(values, position):
    half_rot = ROT // 2
    frequency = 10000.0 ** (-2.0 * jnp.arange(half_rot, dtype=jnp.float32) / ROT)
    angles = position.astype(jnp.float32)[:, None] * frequency[None, :]
    cosine = jnp.cos(angles)[:, None, :]
    sine_vals = jnp.sin(angles)[:, None, :]
    lower = values[..., :half_rot]
    upper = values[..., half_rot:ROT]
    return jnp.concatenate(
        [lower * cosine - upper * sine_vals, upper * cosine + lower * sine_vals, values[..., ROT:]],
        axis=-1,
    )


def head_attention(query_rows, key_rows, value_rows, allowed):
    head_count = query_rows.shape[1] // HEAD_DIM
    score_scale = HEAD_DIM ** (-0.5)

    def one_head(head_index):
        query_cols = lax.dynamic_slice_in_dim(query_rows, head_index * HEAD_DIM, HEAD_DIM, 1)
        key_cols = lax.dynamic_slice_in_dim(key_rows, head_index * HEAD_DIM, HEAD_DIM, 1)
        value_cols = lax.dynamic_slice_in_dim(value_rows, head_index * HEAD_DIM, HEAD_DIM, 1)
        scores = (
            lax.dot_general(
                query_cols, key_cols, (((1,), (1,)), ((), ())), preferred_element_type=jnp.float32
            )
            * score_scale
        )
        masked = jnp.where(allowed, scores, -1e30)
        highest = jnp.max(masked, axis=1, keepdims=True)
        expo = jnp.where(allowed, jnp.exp(masked - highest), 0.0)
        denom = jnp.sum(expo, axis=1, keepdims=True)
        mixed = (
            jnp.dot(expo.astype(jnp.bfloat16), value_cols, preferred_element_type=jnp.float32)
            / denom
        )
        return mixed.astype(jnp.bfloat16)

    outcome = lax.map(one_head, jnp.arange(head_count, dtype=jnp.int32))
    return jnp.transpose(outcome, (1, 0, 2)).reshape(query_rows.shape[0], head_count * HEAD_DIM)


def shards(
    tokens,
    segment_ids,
    prefix_lengths,
    page_owner,
    slot_perm,
    ln_gain,
    ln_bias,
    qkv_weight,
    qkv_bias,
    dense_weight,
    dense_bias,
    fc1_weight,
    fc1_bias,
    fc2_weight,
    fc2_bias,
    prefix_cache,
    cache_pool,
):
    req_count = lax.axis_size("req")
    req_index = lax.axis_index("req")
    tok_rows = tokens.shape[0]
    prefix_count = prefix_cache.shape[0]
    head_cols = qkv_weight.shape[2]
    pool_count = slot_perm.shape[1]
    page_cap = pool_count // req_count
    gathered = lax.all_gather(tokens, "tensor", axis=1, tiled=True)
    normed = norm_rows(gathered.astype(jnp.float32), ln_gain, ln_bias)
    row_ids = jnp.arange(tok_rows, dtype=jnp.int32)
    places = req_index * tok_rows + row_ids
    labels = jnp.arange(prefix_lengths.shape[0], dtype=jnp.int32)
    label_count = labels.shape[0]
    beyond = tok_rows * req_count
    earliest_rows = jnp.min(
        jnp.where(segment_ids[:, None] == labels[None, :], places[:, None], beyond), axis=0
    )
    weight_rows = qkv_weight.shape[0]
    digit_cols = 128
    digits = jnp.concatenate([earliest_rows // 128, earliest_rows % 128]).astype(jnp.bfloat16)
    digits = jnp.pad(digits, (0, weight_rows * digit_cols - 2 * label_count)).reshape(
        weight_rows, digit_cols
    )
    qkv_local = qkv_weight.reshape(weight_rows, 3 * head_cols)
    fc1_cols = fc1_weight.shape[1]
    dense_cols = dense_weight.shape[0]
    fc2_cols = fc2_weight.shape[0]
    packed = jnp.concatenate(
        [qkv_local, fc1_weight, dense_weight.T, fc2_weight.T, digits], axis=1
    )
    everything = ring_gather(packed, INNER, req_count // INNER)
    edges = [0]
    for width in (3 * head_cols, fc1_cols, dense_cols, fc2_cols, digit_cols):
        edges.append(edges[-1] + width)
    qkv_full, fc1_full, dense_full_t, fc2_full_t, digits_full = [
        everything[:, edges[i] : edges[i + 1]] for i in range(5)
    ]
    digit_table = digits_full.reshape(req_count, weight_rows * digit_cols)[:, : 2 * label_count]
    digit_table = digit_table.astype(jnp.int32)
    starts = jnp.min(
        digit_table[:, :label_count] * 128 + digit_table[:, label_count:], axis=0
    )

    def add_rows(portion):
        return jnp.dot(normed, portion, preferred_element_type=jnp.float32)

    projected = add_rows(qkv_full)
    lifted = add_rows(fc1_full)
    projected = (projected + qkv_bias.reshape(1, 3 * head_cols)).reshape(
        tok_rows, 3, head_cols // HEAD_DIM, HEAD_DIM
    )
    segment, position = label_rows(places, starts, prefix_lengths)
    queries = (
        rotate_heads(projected[:, 0], position).astype(jnp.bfloat16).reshape(tok_rows, head_cols)
    )
    new_keys = (
        rotate_heads(projected[:, 1], position).astype(jnp.bfloat16).reshape(tok_rows, head_cols)
    )
    new_values = projected[:, 2].astype(jnp.bfloat16).reshape(tok_rows, head_cols)
    key_value = jnp.stack([new_keys, new_values], axis=1)
    pages_here = tok_rows // PAGE
    page_width = PAGE * 2 * head_cols
    pages = key_value.reshape(pages_here, page_width)
    owners = page_owner[:, 0]
    onehot = (owners[:, None] == jnp.arange(req_count, dtype=jnp.int32)[None, :]).astype(jnp.int32)
    earlier = jnp.cumsum(onehot, axis=0) - onehot
    earlier_count = jnp.sum(earlier * onehot, axis=1)
    target = owners * page_cap + earlier_count
    selecting = (target[None, :] == jnp.arange(pool_count, dtype=jnp.int32)[:, None]).astype(
        jnp.bfloat16
    )
    outgoing = jnp.dot(selecting, pages, preferred_element_type=jnp.float32).astype(jnp.bfloat16)
    filled = jnp.sum(selecting, axis=1)
    flag_cols = 128
    flagged = jnp.concatenate(
        [outgoing, jnp.broadcast_to(filled[:, None], (pool_count, flag_cols)).astype(jnp.bfloat16)],
        axis=1,
    )
    local_keys = jnp.concatenate([key_value, prefix_cache], axis=0)
    arrived, behind = exchange(
        flagged.reshape(req_count, page_cap, page_width + flag_cols), local_keys
    )
    arrived = arrived.reshape(pool_count, page_width + flag_cols)
    incoming = arrived[:, :page_width]
    incoming_filled = arrived[:, page_width]
    slot_ids = slot_perm[0]
    placing = (slot_ids[None, :] == jnp.arange(pool_count, dtype=jnp.int32)[:, None]) & (
        incoming_filled[None, :] > 0
    )
    written = jnp.dot(
        placing.astype(jnp.bfloat16),
        incoming,
        preferred_element_type=jnp.float32,
    ).astype(jnp.bfloat16)
    written_mask = jnp.any(placing, axis=1)
    pool_pages = cache_pool.reshape(pool_count, page_width)
    new_pool = jnp.where(written_mask[:, None], written, pool_pages).reshape(cache_pool.shape)
    blocks = [local_keys] + [behind[step] for step in range(SPAN)]
    key_segs = []
    key_poss = []
    for step_back in range(SPAN + 1):
        block_id = req_index - step_back
        seg_new, pos_new = label_rows(block_id * tok_rows + row_ids, starts, prefix_lengths)
        seg_old, pos_old = prefix_rows(block_id, tok_rows, prefix_count, starts, prefix_lengths)
        key_segs.extend([seg_new, seg_old])
        key_poss.extend([pos_new, pos_old])
    key_segment = jnp.concatenate(key_segs)
    key_position = jnp.concatenate(key_poss)
    allowed = (key_segment[None, :] == segment[:, None]) & (
        key_position[None, :] <= position[:, None]
    )
    allowed = allowed & (
        (position[:, None] - key_position[None, :] < WINDOW) | (key_position[None, :] < SINKS)
    )
    all_keys = jnp.concatenate(blocks, axis=0)
    attended = head_attention(queries, all_keys[:, 0, :], all_keys[:, 1, :], allowed)
    hidden = jax.nn.gelu(lifted + fc1_bias, approximate=True).astype(jnp.bfloat16)
    contract_rows = (((1,), (1,)), ((), ()))
    attn_part = lax.dot_general(
        attended, dense_full_t, contract_rows, preferred_element_type=jnp.float32
    )
    mlp_part = lax.dot_general(
        hidden, fc2_full_t, contract_rows, preferred_element_type=jnp.float32
    )
    branches = attn_part + mlp_part
    summed = lax.psum_scatter(branches, "tensor", scatter_dimension=1, tiled=True)
    layer_out = (tokens.astype(jnp.float32) + summed + dense_bias + fc2_bias).astype(jnp.bfloat16)
    return (layer_out, new_pool)


def solution(mesh):
    placed = (
        P("req", "tensor"),
        P("req"),
        P(),
        P("req", None),
        P("req", None),
        P(),
        P(),
        P("req", None, "tensor"),
        P(None, "tensor"),
        P("tensor", "req"),
        P("tensor"),
        P("req", "tensor"),
        P("tensor"),
        P("tensor", "req"),
        P("tensor"),
        P("req", None, "tensor"),
        P("req", None, "tensor"),
    )
    return jax.shard_map(
        shards,
        mesh=mesh,
        in_specs=placed,
        out_specs=(P("req", "tensor"), P("req", None, "tensor")),
        check_vma=False,
    )
```

```python
import functools

import jax
import jax.numpy as jnp
from jax import lax
from jax.experimental import pallas as pl
from jax.experimental.pallas import tpu as pltpu
from jax.sharding import PartitionSpec as P

HEAD_DIM = 64
ROT = 32
SPAN = 2
SINKS = 4
PAGE = 4
WINDOW = 512
INNER = 4
RING_COST = 40


MESH_IDS = pl.DeviceIdType.MESH


def ring_gather_kernel(inner, outer, block_ref, out_ref, own_sem, send_sems, recv_sems):
    req_index = lax.axis_index("req")
    tensor_index = lax.axis_index("tensor")
    here_outer = req_index // inner
    here_inner = req_index % inner

    def device(outer_at, inner_at):
        outer_at = lax.rem(outer_at + outer, outer)
        inner_at = lax.rem(inner_at + inner, inner)
        return (outer_at * inner + inner_at, tensor_index)

    neighbours = (
        device(here_outer, here_inner + 1),
        device(here_outer, here_inner - 1),
        device(here_outer + 1, here_inner),
        device(here_outer - 1, here_inner),
    )
    barrier = pltpu.get_barrier_semaphore()
    for neighbour in neighbours:
        pl.semaphore_signal(barrier, inc=1, device_id=neighbour, device_id_type=MESH_IDS)
    pl.semaphore_wait(barrier, len(neighbours))

    own = pltpu.make_async_copy(block_ref, out_ref.at[here_outer, here_inner], own_sem)
    own.start()
    sent = []

    def run_ring(stage, count, place, first_source, step_to):
        plans = [(0, 1, count // 2), (1, -1, (count - 1) // 2)]
        pending = [None, None]
        for step in range(1, count // 2 + 1):
            for direction, sign, steps in plans:
                if step > steps:
                    continue
                origin = -sign * (step - 1)
                if step > 1:
                    pending[direction].wait_recv()
                source = first_source if step == 1 else place(origin)
                copy = pltpu.make_async_remote_copy(
                    src_ref=source,
                    dst_ref=place(origin),
                    send_sem=send_sems.at[stage, direction, step - 1],
                    recv_sem=recv_sems.at[stage, direction, step - 1],
                    device_id=step_to(sign),
                    device_id_type=MESH_IDS,
                )
                copy.start()
                sent.append(copy)
                pending[direction] = pltpu.make_async_remote_copy(
                    src_ref=source,
                    dst_ref=place(-sign * step),
                    send_sem=send_sems.at[stage, direction, step - 1],
                    recv_sem=recv_sems.at[stage, direction, step - 1],
                    device_id=step_to(sign),
                    device_id_type=MESH_IDS,
                )
        for waiting in pending:
            if waiting is not None:
                waiting.wait_recv()

    def inner_place(offset):
        return out_ref.at[here_outer, lax.rem(here_inner + offset + inner, inner)]

    def outer_place(offset):
        return out_ref.at[lax.rem(here_outer + offset + outer, outer)]

    run_ring(0, inner, inner_place, block_ref, lambda sign: device(here_outer, here_inner + sign))
    own.wait()
    run_ring(1, outer, outer_place, out_ref.at[here_outer], lambda sign: device(here_outer + sign, here_inner))
    for copy in sent:
        copy.wait_send()


def ring_gather(block, inner, outer, kernel_id):
    rows, cols = block.shape
    most_steps = max(inner, outer) // 2
    gathered_bytes = outer * inner * rows * cols * block.dtype.itemsize
    return pl.pallas_call(
        functools.partial(ring_gather_kernel, inner, outer),
        out_shape=jax.ShapeDtypeStruct((outer, inner, rows, cols), block.dtype),
        in_specs=[pl.BlockSpec(memory_space=pl.ANY)],
        out_specs=pl.BlockSpec(memory_space=pl.ANY),
        scratch_shapes=[
            pltpu.SemaphoreType.DMA(()),
            pltpu.SemaphoreType.DMA((2, 2, most_steps)),
            pltpu.SemaphoreType.DMA((2, 2, most_steps)),
        ],
        compiler_params=pltpu.CompilerParams(collective_id=kernel_id, has_side_effects=True),
        cost_estimate=pl.CostEstimate(
            flops=0, transcendentals=0, bytes_accessed=RING_COST * gathered_bytes
        ),
    )(block).reshape(outer * inner * rows, cols)


EPSILON = 1e-05


def from_behind(value, axis, steps):
    count = lax.axis_size(axis)
    leading, last = (max(0, -steps), min(count, count - steps))
    return lax.ppermute(value, axis, [(source, source + steps) for source in range(leading, last)])


def norm_rows(widened, gain, offset_bias):
    average = jnp.mean(widened, axis=-1, keepdims=True)
    centred = widened - average
    spread = jnp.mean(centred * centred, axis=-1, keepdims=True)
    return (centred * lax.rsqrt(spread + EPSILON) * gain + offset_bias).astype(jnp.bfloat16)


def label_rows(places, starts, prefix_lengths):
    labels = jnp.arange(starts.shape[0], dtype=jnp.int32)
    passed = (starts[None, :] <= places[:, None]) & (labels[None, :] >= 1)
    counted = jnp.sum(passed.astype(jnp.int32), axis=1)
    segment = jnp.where(places >= starts[0], 0, counted)
    segment = jnp.where(places < 0, -2, segment)
    onehot = segment[:, None] == labels[None, :]
    earliest = jnp.sum(jnp.where(onehot, starts[None, :], 0), axis=1)
    offset = jnp.sum(jnp.where(onehot, prefix_lengths[None, :], 0), axis=1)
    return (segment, offset + places - earliest)


def prefix_rows(block_id, rows_dev, prefix_count, starts, prefix_lengths):
    labels = jnp.arange(starts.shape[0], dtype=jnp.int32)
    located = (starts >= block_id * rows_dev) & (starts < (block_id + 1) * rows_dev) & (labels >= 1)
    owner_label = jnp.sum(jnp.where(located, labels, 0))
    length = jnp.sum(jnp.where(located, prefix_lengths, 0))
    places = jnp.arange(prefix_count, dtype=jnp.int32)
    usable = jnp.any(located) & (places < length)
    return (jnp.where(usable, owner_label, -2), places)


def rotate_heads(values, position):
    half_rot = ROT // 2
    frequency = 10000.0 ** (-2.0 * jnp.arange(half_rot, dtype=jnp.float32) / ROT)
    angles = position.astype(jnp.float32)[:, None] * frequency[None, :]
    cosine = jnp.cos(angles)[:, None, :]
    sine_vals = jnp.sin(angles)[:, None, :]
    lower = values[..., :half_rot]
    upper = values[..., half_rot:ROT]
    return jnp.concatenate(
        [lower * cosine - upper * sine_vals, upper * cosine + lower * sine_vals, values[..., ROT:]],
        axis=-1,
    )


def head_attention(query_rows, key_rows, value_rows, allowed):
    head_count = query_rows.shape[1] // HEAD_DIM
    score_scale = HEAD_DIM ** (-0.5)

    def one_head(head_index):
        query_cols = lax.dynamic_slice_in_dim(query_rows, head_index * HEAD_DIM, HEAD_DIM, 1)
        key_cols = lax.dynamic_slice_in_dim(key_rows, head_index * HEAD_DIM, HEAD_DIM, 1)
        value_cols = lax.dynamic_slice_in_dim(value_rows, head_index * HEAD_DIM, HEAD_DIM, 1)
        scores = (
            lax.dot_general(
                query_cols, key_cols, (((1,), (1,)), ((), ())), preferred_element_type=jnp.float32
            )
            * score_scale
        )
        masked = jnp.where(allowed, scores, -1e30)
        highest = jnp.max(masked, axis=1, keepdims=True)
        expo = jnp.where(allowed, jnp.exp(masked - highest), 0.0)
        denom = jnp.sum(expo, axis=1, keepdims=True)
        mixed = (
            jnp.dot(expo.astype(jnp.bfloat16), value_cols, preferred_element_type=jnp.float32)
            / denom
        )
        return mixed.astype(jnp.bfloat16)

    outcome = lax.map(one_head, jnp.arange(head_count, dtype=jnp.int32))
    return jnp.transpose(outcome, (1, 0, 2)).reshape(query_rows.shape[0], head_count * HEAD_DIM)


def shards(
    tokens,
    segment_ids,
    prefix_lengths,
    page_owner,
    slot_perm,
    ln_gain,
    ln_bias,
    qkv_weight,
    qkv_bias,
    dense_weight,
    dense_bias,
    fc1_weight,
    fc1_bias,
    fc2_weight,
    fc2_bias,
    prefix_cache,
    cache_pool,
):
    req_count = lax.axis_size("req")
    req_index = lax.axis_index("req")
    tok_rows = tokens.shape[0]
    prefix_count = prefix_cache.shape[0]
    head_cols = qkv_weight.shape[2]
    pool_count = slot_perm.shape[1]
    page_cap = pool_count // req_count
    gathered = lax.all_gather(tokens, "tensor", axis=1, tiled=True)
    normed = norm_rows(gathered.astype(jnp.float32), ln_gain, ln_bias)
    row_ids = jnp.arange(tok_rows, dtype=jnp.int32)
    places = req_index * tok_rows + row_ids
    labels = jnp.arange(prefix_lengths.shape[0], dtype=jnp.int32)
    label_count = labels.shape[0]
    beyond = tok_rows * req_count
    earliest_rows = jnp.min(
        jnp.where(segment_ids[:, None] == labels[None, :], places[:, None], beyond), axis=0
    )
    weight_rows = qkv_weight.shape[0]
    digit_cols = 128
    digits = jnp.concatenate([earliest_rows // 128, earliest_rows % 128]).astype(jnp.bfloat16)
    digits = jnp.pad(digits, (0, weight_rows * digit_cols - 2 * label_count)).reshape(
        weight_rows, digit_cols
    )
    qkv_local = qkv_weight.reshape(weight_rows, 3 * head_cols)
    fc1_cols = fc1_weight.shape[1]
    dense_cols = dense_weight.shape[0]
    fc2_cols = fc2_weight.shape[0]
    first_pack = jnp.concatenate([qkv_local, digits], axis=1)
    qkv_full, digits_full = jnp.split(
        ring_gather(first_pack, INNER, req_count // INNER, 0), [3 * head_cols], axis=1
    )
    digit_table = digits_full.reshape(req_count, weight_rows * digit_cols)[:, : 2 * label_count]
    digit_table = digit_table.astype(jnp.int32)
    starts = jnp.min(
        digit_table[:, :label_count] * 128 + digit_table[:, label_count:], axis=0
    )

    def add_rows(portion):
        return jnp.dot(normed, portion, preferred_element_type=jnp.float32)

    projected = add_rows(qkv_full)
    projected = (projected + qkv_bias.reshape(1, 3 * head_cols)).reshape(
        tok_rows, 3, head_cols // HEAD_DIM, HEAD_DIM
    )
    segment, position = label_rows(places, starts, prefix_lengths)
    queries = (
        rotate_heads(projected[:, 0], position).astype(jnp.bfloat16).reshape(tok_rows, head_cols)
    )
    new_keys = (
        rotate_heads(projected[:, 1], position).astype(jnp.bfloat16).reshape(tok_rows, head_cols)
    )
    new_values = projected[:, 2].astype(jnp.bfloat16).reshape(tok_rows, head_cols)
    key_value = jnp.stack([new_keys, new_values], axis=1)
    pages_here = tok_rows // PAGE
    page_width = PAGE * 2 * head_cols
    pages = key_value.reshape(pages_here, page_width)
    owners = page_owner[:, 0]
    onehot = (owners[:, None] == jnp.arange(req_count, dtype=jnp.int32)[None, :]).astype(jnp.int32)
    earlier = jnp.cumsum(onehot, axis=0) - onehot
    earlier_count = jnp.sum(earlier * onehot, axis=1)
    target = owners * page_cap + earlier_count
    selecting = (target[None, :] == jnp.arange(pool_count, dtype=jnp.int32)[:, None]).astype(
        jnp.bfloat16
    )
    outgoing = jnp.dot(selecting, pages, preferred_element_type=jnp.float32).astype(jnp.bfloat16)
    filled = jnp.sum(selecting, axis=1)
    flag_cols = 128
    flagged = jnp.concatenate(
        [outgoing, jnp.broadcast_to(filled[:, None], (pool_count, flag_cols)).astype(jnp.bfloat16)],
        axis=1,
    )
    second_pack = jnp.concatenate([fc1_weight, dense_weight.T, fc2_weight.T], axis=1)
    second_pack, flagged = lax.optimization_barrier((second_pack, flagged))
    fc1_full, dense_full_t, fc2_full_t = jnp.split(
        ring_gather(second_pack, INNER, req_count // INNER, 1),
        [fc1_cols, fc1_cols + dense_cols],
        axis=1,
    )
    arrived = lax.all_to_all(
        flagged.reshape(req_count, page_cap, page_width + flag_cols),
        "req",
        split_axis=0,
        concat_axis=0,
        tiled=True,
    ).reshape(pool_count, page_width + flag_cols)
    fc1_full, arrived = lax.optimization_barrier((fc1_full, arrived))
    lifted = add_rows(fc1_full)
    incoming = arrived[:, :page_width]
    incoming_filled = arrived[:, page_width]
    slot_ids = slot_perm[0]
    placing = (slot_ids[None, :] == jnp.arange(pool_count, dtype=jnp.int32)[:, None]) & (
        incoming_filled[None, :] > 0
    )
    written = jnp.dot(
        placing.astype(jnp.bfloat16),
        incoming,
        preferred_element_type=jnp.float32,
    ).astype(jnp.bfloat16)
    written_mask = jnp.any(placing, axis=1)
    pool_pages = cache_pool.reshape(pool_count, page_width)
    new_pool = jnp.where(written_mask[:, None], written, pool_pages).reshape(cache_pool.shape)
    local_keys = jnp.concatenate([key_value, prefix_cache], axis=0)
    blocks = [local_keys]
    for shift_by in range(1, SPAN + 1):
        blocks.append(from_behind(local_keys, "req", shift_by))
    key_segs = []
    key_poss = []
    for step_back in range(SPAN + 1):
        block_id = req_index - step_back
        seg_new, pos_new = label_rows(block_id * tok_rows + row_ids, starts, prefix_lengths)
        seg_old, pos_old = prefix_rows(block_id, tok_rows, prefix_count, starts, prefix_lengths)
        key_segs.extend([seg_new, seg_old])
        key_poss.extend([pos_new, pos_old])
    key_segment = jnp.concatenate(key_segs)
    key_position = jnp.concatenate(key_poss)
    allowed = (key_segment[None, :] == segment[:, None]) & (
        key_position[None, :] <= position[:, None]
    )
    allowed = allowed & (
        (position[:, None] - key_position[None, :] < WINDOW) | (key_position[None, :] < SINKS)
    )
    all_keys = jnp.concatenate(blocks, axis=0)
    attended = head_attention(queries, all_keys[:, 0, :], all_keys[:, 1, :], allowed)
    hidden = jax.nn.gelu(lifted + fc1_bias, approximate=True).astype(jnp.bfloat16)
    contract_rows = (((1,), (1,)), ((), ()))
    attn_part = lax.dot_general(
        attended, dense_full_t, contract_rows, preferred_element_type=jnp.float32
    )
    mlp_part = lax.dot_general(
        hidden, fc2_full_t, contract_rows, preferred_element_type=jnp.float32
    )
    branches = attn_part + mlp_part
    summed = lax.psum_scatter(branches, "tensor", scatter_dimension=1, tiled=True)
    layer_out = (tokens.astype(jnp.float32) + summed + dense_bias + fc2_bias).astype(jnp.bfloat16)
    return (layer_out, new_pool)


def solution(mesh):
    placed = (
        P("req", "tensor"),
        P("req"),
        P(),
        P("req", None),
        P("req", None),
        P(),
        P(),
        P("req", None, "tensor"),
        P(None, "tensor"),
        P("tensor", "req"),
        P("tensor"),
        P("req", "tensor"),
        P("tensor"),
        P("tensor", "req"),
        P("tensor"),
        P("req", None, "tensor"),
        P("req", None, "tensor"),
    )
    return jax.shard_map(
        shards,
        mesh=mesh,
        in_specs=placed,
        out_specs=(P("req", "tensor"), P("req", None, "tensor")),
        check_vma=False,
    )
```

```python
import functools

import jax
import jax.numpy as jnp
from jax import lax
from jax.experimental import pallas as pl
from jax.experimental.pallas import tpu as pltpu
from jax.sharding import PartitionSpec as P

HEAD_DIM = 64
ROT = 32
SPAN = 2
SINKS = 4
PAGE = 4
WINDOW = 512
INNER = 4


MESH_IDS = pl.DeviceIdType.MESH


def ring_gather_kernel(inner, outer, block_ref, out_ref, own_sem, send_sems, recv_sems):
    req_index = lax.axis_index("req")
    tensor_index = lax.axis_index("tensor")
    here_outer = req_index // inner
    here_inner = req_index % inner

    def device(outer_at, inner_at):
        outer_at = lax.rem(outer_at + outer, outer)
        inner_at = lax.rem(inner_at + inner, inner)
        return (outer_at * inner + inner_at, tensor_index)

    neighbours = (
        device(here_outer, here_inner + 1),
        device(here_outer, here_inner - 1),
        device(here_outer + 1, here_inner),
        device(here_outer - 1, here_inner),
    )
    barrier = pltpu.get_barrier_semaphore()
    for neighbour in neighbours:
        pl.semaphore_signal(barrier, inc=1, device_id=neighbour, device_id_type=MESH_IDS)
    pl.semaphore_wait(barrier, len(neighbours))

    own = pltpu.make_async_copy(block_ref, out_ref.at[here_outer, here_inner], own_sem)
    own.start()
    sent = []

    def run_ring(stage, count, place, first_source, step_to):
        plans = [(0, 1, count // 2), (1, -1, (count - 1) // 2)]
        pending = [None, None]
        for step in range(1, count // 2 + 1):
            for direction, sign, steps in plans:
                if step > steps:
                    continue
                origin = -sign * (step - 1)
                if step > 1:
                    pending[direction].wait_recv()
                source = first_source if step == 1 else place(origin)
                copy = pltpu.make_async_remote_copy(
                    src_ref=source,
                    dst_ref=place(origin),
                    send_sem=send_sems.at[stage, direction, step - 1],
                    recv_sem=recv_sems.at[stage, direction, step - 1],
                    device_id=step_to(sign),
                    device_id_type=MESH_IDS,
                )
                copy.start()
                sent.append(copy)
                pending[direction] = pltpu.make_async_remote_copy(
                    src_ref=source,
                    dst_ref=place(-sign * step),
                    send_sem=send_sems.at[stage, direction, step - 1],
                    recv_sem=recv_sems.at[stage, direction, step - 1],
                    device_id=step_to(sign),
                    device_id_type=MESH_IDS,
                )
        for waiting in pending:
            if waiting is not None:
                waiting.wait_recv()

    def inner_place(offset):
        return out_ref.at[here_outer, lax.rem(here_inner + offset + inner, inner)]

    def outer_place(offset):
        return out_ref.at[lax.rem(here_outer + offset + outer, outer)]

    run_ring(0, inner, inner_place, block_ref, lambda sign: device(here_outer, here_inner + sign))
    own.wait()
    run_ring(1, outer, outer_place, out_ref.at[here_outer], lambda sign: device(here_outer + sign, here_inner))
    for copy in sent:
        copy.wait_send()


def ring_gather(block, inner, outer):
    rows, cols = block.shape
    most_steps = max(inner, outer) // 2
    return pl.pallas_call(
        functools.partial(ring_gather_kernel, inner, outer),
        out_shape=jax.ShapeDtypeStruct((outer, inner, rows, cols), block.dtype),
        in_specs=[pl.BlockSpec(memory_space=pl.ANY)],
        out_specs=pl.BlockSpec(memory_space=pl.ANY),
        scratch_shapes=[
            pltpu.SemaphoreType.DMA(()),
            pltpu.SemaphoreType.DMA((2, 2, most_steps)),
            pltpu.SemaphoreType.DMA((2, 2, most_steps)),
        ],
        compiler_params=pltpu.CompilerParams(collective_id=0, has_side_effects=True),
    )(block).reshape(outer * inner * rows, cols)


EPSILON = 1e-05


def from_behind(value, axis, steps):
    count = lax.axis_size(axis)
    leading, last = (max(0, -steps), min(count, count - steps))
    return lax.ppermute(value, axis, [(source, source + steps) for source in range(leading, last)])


def norm_rows(widened, gain, offset_bias):
    average = jnp.mean(widened, axis=-1, keepdims=True)
    centred = widened - average
    spread = jnp.mean(centred * centred, axis=-1, keepdims=True)
    return (centred * lax.rsqrt(spread + EPSILON) * gain + offset_bias).astype(jnp.bfloat16)


def label_rows(places, starts, prefix_lengths):
    labels = jnp.arange(starts.shape[0], dtype=jnp.int32)
    passed = (starts[None, :] <= places[:, None]) & (labels[None, :] >= 1)
    counted = jnp.sum(passed.astype(jnp.int32), axis=1)
    segment = jnp.where(places >= starts[0], 0, counted)
    segment = jnp.where(places < 0, -2, segment)
    onehot = segment[:, None] == labels[None, :]
    earliest = jnp.sum(jnp.where(onehot, starts[None, :], 0), axis=1)
    offset = jnp.sum(jnp.where(onehot, prefix_lengths[None, :], 0), axis=1)
    return (segment, offset + places - earliest)


def prefix_rows(block_id, rows_dev, prefix_count, starts, prefix_lengths):
    labels = jnp.arange(starts.shape[0], dtype=jnp.int32)
    located = (starts >= block_id * rows_dev) & (starts < (block_id + 1) * rows_dev) & (labels >= 1)
    owner_label = jnp.sum(jnp.where(located, labels, 0))
    length = jnp.sum(jnp.where(located, prefix_lengths, 0))
    places = jnp.arange(prefix_count, dtype=jnp.int32)
    usable = jnp.any(located) & (places < length)
    return (jnp.where(usable, owner_label, -2), places)


def rotate_heads(values, position):
    half_rot = ROT // 2
    frequency = 10000.0 ** (-2.0 * jnp.arange(half_rot, dtype=jnp.float32) / ROT)
    angles = position.astype(jnp.float32)[:, None] * frequency[None, :]
    cosine = jnp.cos(angles)[:, None, :]
    sine_vals = jnp.sin(angles)[:, None, :]
    lower = values[..., :half_rot]
    upper = values[..., half_rot:ROT]
    return jnp.concatenate(
        [lower * cosine - upper * sine_vals, upper * cosine + lower * sine_vals, values[..., ROT:]],
        axis=-1,
    )


def head_attention(query_rows, key_rows, value_rows, allowed):
    head_count = query_rows.shape[1] // HEAD_DIM
    score_scale = HEAD_DIM ** (-0.5)

    def one_head(head_index):
        query_cols = lax.dynamic_slice_in_dim(query_rows, head_index * HEAD_DIM, HEAD_DIM, 1)
        key_cols = lax.dynamic_slice_in_dim(key_rows, head_index * HEAD_DIM, HEAD_DIM, 1)
        value_cols = lax.dynamic_slice_in_dim(value_rows, head_index * HEAD_DIM, HEAD_DIM, 1)
        scores = (
            lax.dot_general(
                query_cols, key_cols, (((1,), (1,)), ((), ())), preferred_element_type=jnp.float32
            )
            * score_scale
        )
        masked = jnp.where(allowed, scores, -1e30)
        highest = jnp.max(masked, axis=1, keepdims=True)
        expo = jnp.where(allowed, jnp.exp(masked - highest), 0.0)
        denom = jnp.sum(expo, axis=1, keepdims=True)
        mixed = (
            jnp.dot(expo.astype(jnp.bfloat16), value_cols, preferred_element_type=jnp.float32)
            / denom
        )
        return mixed.astype(jnp.bfloat16)

    outcome = lax.map(one_head, jnp.arange(head_count, dtype=jnp.int32))
    return jnp.transpose(outcome, (1, 0, 2)).reshape(query_rows.shape[0], head_count * HEAD_DIM)


def shards(
    tokens,
    segment_ids,
    prefix_lengths,
    page_owner,
    slot_perm,
    ln_gain,
    ln_bias,
    qkv_weight,
    qkv_bias,
    dense_weight,
    dense_bias,
    fc1_weight,
    fc1_bias,
    fc2_weight,
    fc2_bias,
    prefix_cache,
    cache_pool,
):
    req_count = lax.axis_size("req")
    req_index = lax.axis_index("req")
    tok_rows = tokens.shape[0]
    prefix_count = prefix_cache.shape[0]
    head_cols = qkv_weight.shape[2]
    pool_count = slot_perm.shape[1]
    page_cap = pool_count // req_count
    gathered = lax.all_gather(tokens, "tensor", axis=1, tiled=True)
    normed = norm_rows(gathered.astype(jnp.float32), ln_gain, ln_bias)
    row_ids = jnp.arange(tok_rows, dtype=jnp.int32)
    places = req_index * tok_rows + row_ids
    labels = jnp.arange(prefix_lengths.shape[0], dtype=jnp.int32)
    label_count = labels.shape[0]
    beyond = tok_rows * req_count
    earliest_rows = jnp.min(
        jnp.where(segment_ids[:, None] == labels[None, :], places[:, None], beyond), axis=0
    )
    weight_rows = qkv_weight.shape[0]
    digit_cols = 128
    digits = jnp.concatenate([earliest_rows // 128, earliest_rows % 128]).astype(jnp.bfloat16)
    digits = jnp.pad(digits, (0, weight_rows * digit_cols - 2 * label_count)).reshape(
        weight_rows, digit_cols
    )
    qkv_local = qkv_weight.reshape(weight_rows, 3 * head_cols)
    fc1_cols = fc1_weight.shape[1]
    dense_cols = dense_weight.shape[0]
    fc2_cols = fc2_weight.shape[0]
    packed = jnp.concatenate(
        [qkv_local, fc1_weight, dense_weight.T, fc2_weight.T, digits], axis=1
    )
    everything = ring_gather(packed, INNER, req_count // INNER)
    edges = [0]
    for width in (3 * head_cols, fc1_cols, dense_cols, fc2_cols, digit_cols):
        edges.append(edges[-1] + width)
    qkv_full, fc1_full, dense_full_t, fc2_full_t, digits_full = [
        everything[:, edges[i] : edges[i + 1]] for i in range(5)
    ]
    digit_table = digits_full.reshape(req_count, weight_rows * digit_cols)[:, : 2 * label_count]
    digit_table = digit_table.astype(jnp.int32)
    starts = jnp.min(
        digit_table[:, :label_count] * 128 + digit_table[:, label_count:], axis=0
    )

    def add_rows(portion):
        return jnp.dot(normed, portion, preferred_element_type=jnp.float32)

    projected = add_rows(qkv_full)
    lifted = add_rows(fc1_full)
    projected = (projected + qkv_bias.reshape(1, 3 * head_cols)).reshape(
        tok_rows, 3, head_cols // HEAD_DIM, HEAD_DIM
    )
    segment, position = label_rows(places, starts, prefix_lengths)
    queries = (
        rotate_heads(projected[:, 0], position).astype(jnp.bfloat16).reshape(tok_rows, head_cols)
    )
    new_keys = (
        rotate_heads(projected[:, 1], position).astype(jnp.bfloat16).reshape(tok_rows, head_cols)
    )
    new_values = projected[:, 2].astype(jnp.bfloat16).reshape(tok_rows, head_cols)
    key_value = jnp.stack([new_keys, new_values], axis=1)
    pages_here = tok_rows // PAGE
    page_width = PAGE * 2 * head_cols
    pages = key_value.reshape(pages_here, page_width)
    owners = page_owner[:, 0]
    onehot = (owners[:, None] == jnp.arange(req_count, dtype=jnp.int32)[None, :]).astype(jnp.int32)
    earlier = jnp.cumsum(onehot, axis=0) - onehot
    earlier_count = jnp.sum(earlier * onehot, axis=1)
    target = owners * page_cap + earlier_count
    selecting = (target[None, :] == jnp.arange(pool_count, dtype=jnp.int32)[:, None]).astype(
        jnp.bfloat16
    )
    outgoing = jnp.dot(selecting, pages, preferred_element_type=jnp.float32).astype(jnp.bfloat16)
    filled = jnp.sum(selecting, axis=1)
    flag_cols = 128
    flagged = jnp.concatenate(
        [outgoing, jnp.broadcast_to(filled[:, None], (pool_count, flag_cols)).astype(jnp.bfloat16)],
        axis=1,
    )
    arrived = lax.all_to_all(
        flagged.reshape(req_count, page_cap, page_width + flag_cols),
        "req",
        split_axis=0,
        concat_axis=0,
        tiled=True,
    ).reshape(pool_count, page_width + flag_cols)
    local_keys = jnp.concatenate([key_value, prefix_cache], axis=0)
    blocks = [local_keys]
    for shift_by in range(1, SPAN + 1):
        blocks.append(from_behind(local_keys, "req", shift_by))
    key_segs = []
    key_poss = []
    for step_back in range(SPAN + 1):
        block_id = req_index - step_back
        seg_new, pos_new = label_rows(block_id * tok_rows + row_ids, starts, prefix_lengths)
        seg_old, pos_old = prefix_rows(block_id, tok_rows, prefix_count, starts, prefix_lengths)
        key_segs.extend([seg_new, seg_old])
        key_poss.extend([pos_new, pos_old])
    key_segment = jnp.concatenate(key_segs)
    key_position = jnp.concatenate(key_poss)
    allowed = (key_segment[None, :] == segment[:, None]) & (
        key_position[None, :] <= position[:, None]
    )
    allowed = allowed & (
        (position[:, None] - key_position[None, :] < WINDOW) | (key_position[None, :] < SINKS)
    )
    all_keys = jnp.concatenate(blocks, axis=0)
    attended = head_attention(queries, all_keys[:, 0, :], all_keys[:, 1, :], allowed)
    attended, arrived = lax.optimization_barrier((attended, arrived))
    incoming = arrived[:, :page_width]
    incoming_filled = arrived[:, page_width]
    slot_ids = slot_perm[0]
    placing = (slot_ids[None, :] == jnp.arange(pool_count, dtype=jnp.int32)[:, None]) & (
        incoming_filled[None, :] > 0
    )
    written = jnp.dot(
        placing.astype(jnp.bfloat16),
        incoming,
        preferred_element_type=jnp.float32,
    ).astype(jnp.bfloat16)
    written_mask = jnp.any(placing, axis=1)
    pool_pages = cache_pool.reshape(pool_count, page_width)
    new_pool = jnp.where(written_mask[:, None], written, pool_pages).reshape(cache_pool.shape)
    hidden = jax.nn.gelu(lifted + fc1_bias, approximate=True).astype(jnp.bfloat16)
    contract_rows = (((1,), (1,)), ((), ()))
    attn_part = lax.dot_general(
        attended, dense_full_t, contract_rows, preferred_element_type=jnp.float32
    )
    mlp_part = lax.dot_general(
        hidden, fc2_full_t, contract_rows, preferred_element_type=jnp.float32
    )
    branches = attn_part + mlp_part
    summed = lax.psum_scatter(branches, "tensor", scatter_dimension=1, tiled=True)
    layer_out = (tokens.astype(jnp.float32) + summed + dense_bias + fc2_bias).astype(jnp.bfloat16)
    return (layer_out, new_pool)


def solution(mesh):
    placed = (
        P("req", "tensor"),
        P("req"),
        P(),
        P("req", None),
        P("req", None),
        P(),
        P(),
        P("req", None, "tensor"),
        P(None, "tensor"),
        P("tensor", "req"),
        P("tensor"),
        P("req", "tensor"),
        P("tensor"),
        P("tensor", "req"),
        P("tensor"),
        P("req", None, "tensor"),
        P("req", None, "tensor"),
    )
    return jax.shard_map(
        shards,
        mesh=mesh,
        in_specs=placed,
        out_specs=(P("req", "tensor"), P("req", None, "tensor")),
        check_vma=False,
    )
```

```python
import functools

import jax
import jax.numpy as jnp
from jax import lax
from jax.experimental import pallas as pl
from jax.experimental.pallas import tpu as pltpu
from jax.sharding import PartitionSpec as P

HEAD_DIM = 64
ROT = 32
SPAN = 2
SINKS = 4
PAGE = 4
WINDOW = 512
INNER = 4


MESH_IDS = pl.DeviceIdType.MESH


def ring_gather_kernel(inner, outer, block_ref, out_ref, own_sem, send_sems, recv_sems):
    req_index = lax.axis_index("req")
    tensor_index = lax.axis_index("tensor")
    here_outer = req_index // inner
    here_inner = req_index % inner

    def device(outer_at, inner_at):
        outer_at = lax.rem(outer_at + outer, outer)
        inner_at = lax.rem(inner_at + inner, inner)
        return (outer_at * inner + inner_at, tensor_index)

    neighbours = (
        device(here_outer, here_inner + 1),
        device(here_outer, here_inner - 1),
        device(here_outer + 1, here_inner),
        device(here_outer - 1, here_inner),
    )
    barrier = pltpu.get_barrier_semaphore()
    for neighbour in neighbours:
        pl.semaphore_signal(barrier, inc=1, device_id=neighbour, device_id_type=MESH_IDS)
    pl.semaphore_wait(barrier, len(neighbours))

    own = pltpu.make_async_copy(block_ref, out_ref.at[here_outer, here_inner], own_sem)
    own.start()
    sent = []

    def run_ring(stage, count, place, first_source, step_to):
        plans = [(0, 1, count // 2), (1, -1, (count - 1) // 2)]
        pending = [None, None]
        for step in range(1, count // 2 + 1):
            for direction, sign, steps in plans:
                if step > steps:
                    continue
                origin = -sign * (step - 1)
                if step > 1:
                    pending[direction].wait_recv()
                source = first_source if step == 1 else place(origin)
                copy = pltpu.make_async_remote_copy(
                    src_ref=source,
                    dst_ref=place(origin),
                    send_sem=send_sems.at[stage, direction, step - 1],
                    recv_sem=recv_sems.at[stage, direction, step - 1],
                    device_id=step_to(sign),
                    device_id_type=MESH_IDS,
                )
                copy.start()
                sent.append(copy)
                pending[direction] = pltpu.make_async_remote_copy(
                    src_ref=source,
                    dst_ref=place(-sign * step),
                    send_sem=send_sems.at[stage, direction, step - 1],
                    recv_sem=recv_sems.at[stage, direction, step - 1],
                    device_id=step_to(sign),
                    device_id_type=MESH_IDS,
                )
        for waiting in pending:
            if waiting is not None:
                waiting.wait_recv()

    def inner_place(offset):
        return out_ref.at[here_outer, lax.rem(here_inner + offset + inner, inner)]

    def outer_place(offset):
        return out_ref.at[lax.rem(here_outer + offset + outer, outer)]

    run_ring(0, inner, inner_place, block_ref, lambda sign: device(here_outer, here_inner + sign))
    own.wait()
    run_ring(1, outer, outer_place, out_ref.at[here_outer], lambda sign: device(here_outer + sign, here_inner))
    for copy in sent:
        copy.wait_send()


def ring_gather(block, inner, outer):
    rows, cols = block.shape
    most_steps = max(inner, outer) // 2
    return pl.pallas_call(
        functools.partial(ring_gather_kernel, inner, outer),
        out_shape=jax.ShapeDtypeStruct((outer, inner, rows, cols), block.dtype),
        in_specs=[pl.BlockSpec(memory_space=pl.ANY)],
        out_specs=pl.BlockSpec(memory_space=pl.ANY),
        scratch_shapes=[
            pltpu.SemaphoreType.DMA(()),
            pltpu.SemaphoreType.DMA((2, 2, most_steps)),
            pltpu.SemaphoreType.DMA((2, 2, most_steps)),
        ],
        compiler_params=pltpu.CompilerParams(collective_id=0, has_side_effects=True),
    )(block).reshape(outer * inner * rows, cols)


EPSILON = 1e-05


def from_behind(value, axis, steps):
    count = lax.axis_size(axis)
    leading, last = (max(0, -steps), min(count, count - steps))
    return lax.ppermute(value, axis, [(source, source + steps) for source in range(leading, last)])


def norm_rows(widened, gain, offset_bias):
    average = jnp.mean(widened, axis=-1, keepdims=True)
    centred = widened - average
    spread = jnp.mean(centred * centred, axis=-1, keepdims=True)
    return (centred * lax.rsqrt(spread + EPSILON) * gain + offset_bias).astype(jnp.bfloat16)


def label_rows(places, starts, prefix_lengths):
    labels = jnp.arange(starts.shape[0], dtype=jnp.int32)
    passed = (starts[None, :] <= places[:, None]) & (labels[None, :] >= 1)
    counted = jnp.sum(passed.astype(jnp.int32), axis=1)
    segment = jnp.where(places >= starts[0], 0, counted)
    segment = jnp.where(places < 0, -2, segment)
    onehot = segment[:, None] == labels[None, :]
    earliest = jnp.sum(jnp.where(onehot, starts[None, :], 0), axis=1)
    offset = jnp.sum(jnp.where(onehot, prefix_lengths[None, :], 0), axis=1)
    return (segment, offset + places - earliest)


def prefix_rows(block_id, rows_dev, prefix_count, starts, prefix_lengths):
    labels = jnp.arange(starts.shape[0], dtype=jnp.int32)
    located = (starts >= block_id * rows_dev) & (starts < (block_id + 1) * rows_dev) & (labels >= 1)
    owner_label = jnp.sum(jnp.where(located, labels, 0))
    length = jnp.sum(jnp.where(located, prefix_lengths, 0))
    places = jnp.arange(prefix_count, dtype=jnp.int32)
    usable = jnp.any(located) & (places < length)
    return (jnp.where(usable, owner_label, -2), places)


def rotate_heads(values, position):
    half_rot = ROT // 2
    frequency = 10000.0 ** (-2.0 * jnp.arange(half_rot, dtype=jnp.float32) / ROT)
    angles = position.astype(jnp.float32)[:, None] * frequency[None, :]
    cosine = jnp.cos(angles)[:, None, :]
    sine_vals = jnp.sin(angles)[:, None, :]
    lower = values[..., :half_rot]
    upper = values[..., half_rot:ROT]
    return jnp.concatenate(
        [lower * cosine - upper * sine_vals, upper * cosine + lower * sine_vals, values[..., ROT:]],
        axis=-1,
    )


def head_attention(query_rows, key_rows, value_rows, allowed):
    head_count = query_rows.shape[1] // HEAD_DIM
    score_scale = HEAD_DIM ** (-0.5)

    def one_head(head_index):
        query_cols = lax.dynamic_slice_in_dim(query_rows, head_index * HEAD_DIM, HEAD_DIM, 1)
        key_cols = lax.dynamic_slice_in_dim(key_rows, head_index * HEAD_DIM, HEAD_DIM, 1)
        value_cols = lax.dynamic_slice_in_dim(value_rows, head_index * HEAD_DIM, HEAD_DIM, 1)
        scores = (
            lax.dot_general(
                query_cols, key_cols, (((1,), (1,)), ((), ())), preferred_element_type=jnp.float32
            )
            * score_scale
        )
        masked = jnp.where(allowed, scores, -1e30)
        highest = jnp.max(masked, axis=1, keepdims=True)
        expo = jnp.where(allowed, jnp.exp(masked - highest), 0.0)
        denom = jnp.sum(expo, axis=1, keepdims=True)
        mixed = (
            jnp.dot(expo.astype(jnp.bfloat16), value_cols, preferred_element_type=jnp.float32)
            / denom
        )
        return mixed.astype(jnp.bfloat16)

    outcome = lax.map(one_head, jnp.arange(head_count, dtype=jnp.int32))
    return jnp.transpose(outcome, (1, 0, 2)).reshape(query_rows.shape[0], head_count * HEAD_DIM)


def shards(
    tokens,
    segment_ids,
    prefix_lengths,
    page_owner,
    slot_perm,
    ln_gain,
    ln_bias,
    qkv_weight,
    qkv_bias,
    dense_weight,
    dense_bias,
    fc1_weight,
    fc1_bias,
    fc2_weight,
    fc2_bias,
    prefix_cache,
    cache_pool,
):
    req_count = lax.axis_size("req")
    req_index = lax.axis_index("req")
    tok_rows = tokens.shape[0]
    prefix_count = prefix_cache.shape[0]
    head_cols = qkv_weight.shape[2]
    pool_count = slot_perm.shape[1]
    page_cap = pool_count // req_count
    gathered = lax.all_gather(tokens, "tensor", axis=1, tiled=True)
    normed = norm_rows(gathered.astype(jnp.float32), ln_gain, ln_bias)
    row_ids = jnp.arange(tok_rows, dtype=jnp.int32)
    places = req_index * tok_rows + row_ids
    labels = jnp.arange(prefix_lengths.shape[0], dtype=jnp.int32)
    label_count = labels.shape[0]
    beyond = tok_rows * req_count
    earliest_rows = jnp.min(
        jnp.where(segment_ids[:, None] == labels[None, :], places[:, None], beyond), axis=0
    )
    weight_rows = qkv_weight.shape[0]
    digit_cols = 128
    digits = jnp.concatenate([earliest_rows // 128, earliest_rows % 128]).astype(jnp.bfloat16)
    digits = jnp.pad(digits, (0, weight_rows * digit_cols - 2 * label_count)).reshape(
        weight_rows, digit_cols
    )
    qkv_local = qkv_weight.reshape(weight_rows, 3 * head_cols)
    fc1_cols = fc1_weight.shape[1]
    dense_cols = dense_weight.shape[0]
    fc2_cols = fc2_weight.shape[0]
    packed = jnp.concatenate(
        [qkv_local, fc1_weight, dense_weight.T, fc2_weight.T, digits], axis=1
    )
    everything = ring_gather(packed, INNER, req_count // INNER)
    edges = [0]
    for width in (3 * head_cols, fc1_cols, dense_cols, fc2_cols, digit_cols):
        edges.append(edges[-1] + width)
    qkv_full, fc1_full, dense_full_t, fc2_full_t, digits_full = [
        everything[:, edges[i] : edges[i + 1]] for i in range(5)
    ]
    digit_table = digits_full.reshape(req_count, weight_rows * digit_cols)[:, : 2 * label_count]
    digit_table = digit_table.astype(jnp.int32)
    starts = jnp.min(
        digit_table[:, :label_count] * 128 + digit_table[:, label_count:], axis=0
    )

    def add_rows(portion):
        return jnp.dot(normed, portion, preferred_element_type=jnp.float32)

    projected = add_rows(qkv_full)
    lifted = add_rows(fc1_full)
    projected = (projected + qkv_bias.reshape(1, 3 * head_cols)).reshape(
        tok_rows, 3, head_cols // HEAD_DIM, HEAD_DIM
    )
    segment, position = label_rows(places, starts, prefix_lengths)
    queries = (
        rotate_heads(projected[:, 0], position).astype(jnp.bfloat16).reshape(tok_rows, head_cols)
    )
    new_keys = (
        rotate_heads(projected[:, 1], position).astype(jnp.bfloat16).reshape(tok_rows, head_cols)
    )
    new_values = projected[:, 2].astype(jnp.bfloat16).reshape(tok_rows, head_cols)
    key_value = jnp.stack([new_keys, new_values], axis=1)
    pages_here = tok_rows // PAGE
    page_width = PAGE * 2 * head_cols
    pages = key_value.reshape(pages_here, page_width)
    owners = page_owner[:, 0]
    onehot = (owners[:, None] == jnp.arange(req_count, dtype=jnp.int32)[None, :]).astype(jnp.int32)
    earlier = jnp.cumsum(onehot, axis=0) - onehot
    earlier_count = jnp.sum(earlier * onehot, axis=1)
    target = owners * page_cap + earlier_count
    selecting = (target[None, :] == jnp.arange(pool_count, dtype=jnp.int32)[:, None]).astype(
        jnp.bfloat16
    )
    outgoing = jnp.dot(selecting, pages, preferred_element_type=jnp.float32).astype(jnp.bfloat16)
    filled = jnp.sum(selecting, axis=1)
    flag_cols = 128
    flagged = jnp.concatenate(
        [outgoing, jnp.broadcast_to(filled[:, None], (pool_count, flag_cols)).astype(jnp.bfloat16)],
        axis=1,
    )
    arrived = lax.all_to_all(
        flagged.reshape(req_count, page_cap, page_width + flag_cols),
        "req",
        split_axis=0,
        concat_axis=0,
        tiled=True,
    ).reshape(pool_count, page_width + flag_cols)
    local_keys = jnp.concatenate([key_value, prefix_cache], axis=0)
    blocks = [local_keys]
    for shift_by in range(1, SPAN + 1):
        blocks.append(from_behind(local_keys, "req", shift_by))
    key_segs = []
    key_poss = []
    for step_back in range(SPAN + 1):
        block_id = req_index - step_back
        seg_new, pos_new = label_rows(block_id * tok_rows + row_ids, starts, prefix_lengths)
        seg_old, pos_old = prefix_rows(block_id, tok_rows, prefix_count, starts, prefix_lengths)
        key_segs.extend([seg_new, seg_old])
        key_poss.extend([pos_new, pos_old])
    key_segment = jnp.concatenate(key_segs)
    key_position = jnp.concatenate(key_poss)
    allowed = (key_segment[None, :] == segment[:, None]) & (
        key_position[None, :] <= position[:, None]
    )
    allowed = allowed & (
        (position[:, None] - key_position[None, :] < WINDOW) | (key_position[None, :] < SINKS)
    )
    all_keys = jnp.concatenate(blocks, axis=0)
    attended = head_attention(queries, all_keys[:, 0, :], all_keys[:, 1, :], allowed)
    attended, arrived = lax.optimization_barrier((attended, arrived))
    incoming = arrived[:, :page_width]
    incoming_filled = arrived[:, page_width]
    slot_ids = slot_perm[0]
    placing = (slot_ids[None, :] == jnp.arange(pool_count, dtype=jnp.int32)[:, None]) & (
        incoming_filled[None, :] > 0
    )
    written = jnp.dot(
        placing.astype(jnp.bfloat16),
        incoming,
        preferred_element_type=jnp.float32,
    ).astype(jnp.bfloat16)
    written_mask = jnp.any(placing, axis=1)
    pool_pages = cache_pool.reshape(pool_count, page_width)
    new_pool = jnp.where(written_mask[:, None], written, pool_pages).reshape(cache_pool.shape)
    hidden = jax.nn.gelu(lifted + fc1_bias, approximate=True).astype(jnp.bfloat16)
    contract_rows = (((1,), (1,)), ((), ()))
    attn_part = lax.dot_general(
        attended, dense_full_t, contract_rows, preferred_element_type=jnp.float32
    )
    mlp_part = lax.dot_general(
        hidden, fc2_full_t, contract_rows, preferred_element_type=jnp.float32
    )
    branches = attn_part + mlp_part
    summed = lax.psum_scatter(
        branches.astype(jnp.bfloat16), "tensor", scatter_dimension=1, tiled=True
    ).astype(jnp.float32)
    layer_out = (tokens.astype(jnp.float32) + summed + dense_bias + fc2_bias).astype(jnp.bfloat16)
    return (layer_out, new_pool)


def solution(mesh):
    placed = (
        P("req", "tensor"),
        P("req"),
        P(),
        P("req", None),
        P("req", None),
        P(),
        P(),
        P("req", None, "tensor"),
        P(None, "tensor"),
        P("tensor", "req"),
        P("tensor"),
        P("req", "tensor"),
        P("tensor"),
        P("tensor", "req"),
        P("tensor"),
        P("req", None, "tensor"),
        P("req", None, "tensor"),
    )
    return jax.shard_map(
        shards,
        mesh=mesh,
        in_specs=placed,
        out_specs=(P("req", "tensor"), P("req", None, "tensor")),
        check_vma=False,
    )
```

```python
import functools

import jax
import jax.numpy as jnp
from jax import lax
from jax.experimental import pallas as pl
from jax.experimental.pallas import tpu as pltpu
from jax.sharding import PartitionSpec as P

HEAD_DIM = 64
ROT = 32
SPAN = 2
SINKS = 4
PAGE = 4
WINDOW = 512
INNER = 4


MESH_IDS = pl.DeviceIdType.MESH


def ring_gather_kernel(inner, outer, block_ref, out_ref, own_sem, inner_send_sems, inner_recv_sems,
                       outer_send_sems, outer_recv_sems):
    req_index = lax.axis_index("req")
    tensor_index = lax.axis_index("tensor")
    here_outer = req_index // inner
    here_inner = req_index % inner

    def device(outer_at, inner_at):
        outer_at = lax.rem(outer_at + outer, outer)
        inner_at = lax.rem(inner_at + inner, inner)
        return (outer_at * inner + inner_at, tensor_index)

    def inner_at(offset):
        return lax.rem(here_inner + offset + inner, inner)

    def outer_at(offset):
        return lax.rem(here_outer + offset + outer, outer)

    neighbours = (
        device(here_outer, here_inner + 1),
        device(here_outer, here_inner - 1),
        device(here_outer + 1, here_inner),
        device(here_outer - 1, here_inner),
    )
    barrier = pltpu.get_barrier_semaphore()
    for neighbour in neighbours:
        pl.semaphore_signal(barrier, inc=1, device_id=neighbour, device_id_type=MESH_IDS)
    pl.semaphore_wait(barrier, len(neighbours))

    own = pltpu.make_async_copy(block_ref, out_ref.at[here_outer, here_inner], own_sem)
    own.start()
    sent = []

    def remote(source, target, send_sem, recv_sem, toward):
        return pltpu.make_async_remote_copy(
            src_ref=source,
            dst_ref=target,
            send_sem=send_sem,
            recv_sem=recv_sem,
            device_id=toward,
            device_id_type=MESH_IDS,
        )

    inner_plans = [(0, 1, inner // 2), (1, -1, (inner - 1) // 2)]
    outer_plans = [(0, 1, outer // 2), (1, -1, (outer - 1) // 2)]

    def inner_copy(direction, sign, step, arriving):
        piece = -sign * step if arriving else -sign * (step - 1)
        source = block_ref if step == 1 else out_ref.at[here_outer, inner_at(piece)]
        return remote(
            source,
            out_ref.at[here_outer, inner_at(piece)],
            inner_send_sems.at[direction, step - 1],
            inner_recv_sems.at[direction, step - 1],
            device(here_outer, here_inner + sign),
        )

    def outer_copy(column, slot, direction, sign, step, arriving):
        piece = -sign * step if arriving else -sign * (step - 1)
        if step == 1 and column == 0:
            source = block_ref
        else:
            source = out_ref.at[outer_at(piece), inner_at(column)]
        return remote(
            source,
            out_ref.at[outer_at(piece), inner_at(column)],
            outer_send_sems.at[slot, direction, step - 1],
            outer_recv_sems.at[slot, direction, step - 1],
            device(here_outer + sign, here_inner),
        )

    def launch(copy):
        copy.start()
        sent.append(copy)

    columns = [0]
    for direction, sign, steps in inner_plans:
        if steps:
            launch(inner_copy(direction, sign, 1, False))
    for direction, sign, steps in outer_plans:
        if steps:
            launch(outer_copy(0, 0, direction, sign, 1, False))
    for step in range(1, inner // 2 + 1):
        for direction, sign, steps in inner_plans:
            if step > steps:
                continue
            inner_copy(direction, sign, step, True).wait_recv()
            if step < steps:
                launch(inner_copy(direction, sign, step + 1, False))
            columns.append(-sign * step)
            for outer_direction, outer_sign, outer_steps in outer_plans:
                if outer_steps:
                    launch(outer_copy(columns[-1], len(columns) - 1, outer_direction, outer_sign, 1, False))
    for step in range(2, outer // 2 + 1):
        for slot, column in enumerate(columns):
            for direction, sign, steps in outer_plans:
                if step > steps:
                    continue
                outer_copy(column, slot, direction, sign, step - 1, True).wait_recv()
                launch(outer_copy(column, slot, direction, sign, step, False))
    for slot, column in enumerate(columns):
        for direction, sign, steps in outer_plans:
            if steps:
                outer_copy(column, slot, direction, sign, steps, True).wait_recv()
    own.wait()
    for copy in sent:
        copy.wait_send()


def ring_gather(block, inner, outer):
    rows, cols = block.shape
    return pl.pallas_call(
        functools.partial(ring_gather_kernel, inner, outer),
        out_shape=jax.ShapeDtypeStruct((outer, inner, rows, cols), block.dtype),
        in_specs=[pl.BlockSpec(memory_space=pl.ANY)],
        out_specs=pl.BlockSpec(memory_space=pl.ANY),
        scratch_shapes=[
            pltpu.SemaphoreType.DMA(()),
            pltpu.SemaphoreType.DMA((2, max(1, inner // 2))),
            pltpu.SemaphoreType.DMA((2, max(1, inner // 2))),
            pltpu.SemaphoreType.DMA((inner, 2, max(1, outer // 2))),
            pltpu.SemaphoreType.DMA((inner, 2, max(1, outer // 2))),
        ],
        compiler_params=pltpu.CompilerParams(collective_id=0, has_side_effects=True),
    )(block).reshape(outer * inner * rows, cols)


EPSILON = 1e-05


def from_behind(value, axis, steps):
    count = lax.axis_size(axis)
    leading, last = (max(0, -steps), min(count, count - steps))
    return lax.ppermute(value, axis, [(source, source + steps) for source in range(leading, last)])


def norm_rows(widened, gain, offset_bias):
    average = jnp.mean(widened, axis=-1, keepdims=True)
    centred = widened - average
    spread = jnp.mean(centred * centred, axis=-1, keepdims=True)
    return (centred * lax.rsqrt(spread + EPSILON) * gain + offset_bias).astype(jnp.bfloat16)


def label_rows(places, starts, prefix_lengths):
    labels = jnp.arange(starts.shape[0], dtype=jnp.int32)
    passed = (starts[None, :] <= places[:, None]) & (labels[None, :] >= 1)
    counted = jnp.sum(passed.astype(jnp.int32), axis=1)
    segment = jnp.where(places >= starts[0], 0, counted)
    segment = jnp.where(places < 0, -2, segment)
    onehot = segment[:, None] == labels[None, :]
    earliest = jnp.sum(jnp.where(onehot, starts[None, :], 0), axis=1)
    offset = jnp.sum(jnp.where(onehot, prefix_lengths[None, :], 0), axis=1)
    return (segment, offset + places - earliest)


def prefix_rows(block_id, rows_dev, prefix_count, starts, prefix_lengths):
    labels = jnp.arange(starts.shape[0], dtype=jnp.int32)
    located = (starts >= block_id * rows_dev) & (starts < (block_id + 1) * rows_dev) & (labels >= 1)
    owner_label = jnp.sum(jnp.where(located, labels, 0))
    length = jnp.sum(jnp.where(located, prefix_lengths, 0))
    places = jnp.arange(prefix_count, dtype=jnp.int32)
    usable = jnp.any(located) & (places < length)
    return (jnp.where(usable, owner_label, -2), places)


def rotate_heads(values, position):
    half_rot = ROT // 2
    frequency = 10000.0 ** (-2.0 * jnp.arange(half_rot, dtype=jnp.float32) / ROT)
    angles = position.astype(jnp.float32)[:, None] * frequency[None, :]
    cosine = jnp.cos(angles)[:, None, :]
    sine_vals = jnp.sin(angles)[:, None, :]
    lower = values[..., :half_rot]
    upper = values[..., half_rot:ROT]
    return jnp.concatenate(
        [lower * cosine - upper * sine_vals, upper * cosine + lower * sine_vals, values[..., ROT:]],
        axis=-1,
    )


def head_attention(query_rows, key_rows, value_rows, allowed):
    head_count = query_rows.shape[1] // HEAD_DIM
    score_scale = HEAD_DIM ** (-0.5)

    def one_head(head_index):
        query_cols = lax.dynamic_slice_in_dim(query_rows, head_index * HEAD_DIM, HEAD_DIM, 1)
        key_cols = lax.dynamic_slice_in_dim(key_rows, head_index * HEAD_DIM, HEAD_DIM, 1)
        value_cols = lax.dynamic_slice_in_dim(value_rows, head_index * HEAD_DIM, HEAD_DIM, 1)
        scores = (
            lax.dot_general(
                query_cols, key_cols, (((1,), (1,)), ((), ())), preferred_element_type=jnp.float32
            )
            * score_scale
        )
        masked = jnp.where(allowed, scores, -1e30)
        highest = jnp.max(masked, axis=1, keepdims=True)
        expo = jnp.where(allowed, jnp.exp(masked - highest), 0.0)
        denom = jnp.sum(expo, axis=1, keepdims=True)
        mixed = (
            jnp.dot(expo.astype(jnp.bfloat16), value_cols, preferred_element_type=jnp.float32)
            / denom
        )
        return mixed.astype(jnp.bfloat16)

    outcome = lax.map(one_head, jnp.arange(head_count, dtype=jnp.int32))
    return jnp.transpose(outcome, (1, 0, 2)).reshape(query_rows.shape[0], head_count * HEAD_DIM)


def shards(
    tokens,
    segment_ids,
    prefix_lengths,
    page_owner,
    slot_perm,
    ln_gain,
    ln_bias,
    qkv_weight,
    qkv_bias,
    dense_weight,
    dense_bias,
    fc1_weight,
    fc1_bias,
    fc2_weight,
    fc2_bias,
    prefix_cache,
    cache_pool,
):
    req_count = lax.axis_size("req")
    req_index = lax.axis_index("req")
    tok_rows = tokens.shape[0]
    prefix_count = prefix_cache.shape[0]
    head_cols = qkv_weight.shape[2]
    pool_count = slot_perm.shape[1]
    page_cap = pool_count // req_count
    gathered = lax.all_gather(tokens, "tensor", axis=1, tiled=True)
    normed = norm_rows(gathered.astype(jnp.float32), ln_gain, ln_bias)
    row_ids = jnp.arange(tok_rows, dtype=jnp.int32)
    places = req_index * tok_rows + row_ids
    labels = jnp.arange(prefix_lengths.shape[0], dtype=jnp.int32)
    label_count = labels.shape[0]
    beyond = tok_rows * req_count
    earliest_rows = jnp.min(
        jnp.where(segment_ids[:, None] == labels[None, :], places[:, None], beyond), axis=0
    )
    weight_rows = qkv_weight.shape[0]
    digit_cols = 128
    digits = jnp.concatenate([earliest_rows // 128, earliest_rows % 128]).astype(jnp.bfloat16)
    digits = jnp.pad(digits, (0, weight_rows * digit_cols - 2 * label_count)).reshape(
        weight_rows, digit_cols
    )
    qkv_local = qkv_weight.reshape(weight_rows, 3 * head_cols)
    fc1_cols = fc1_weight.shape[1]
    dense_cols = dense_weight.shape[0]
    fc2_cols = fc2_weight.shape[0]
    packed = jnp.concatenate(
        [qkv_local, fc1_weight, dense_weight.T, fc2_weight.T, digits], axis=1
    )
    everything = ring_gather(packed, INNER, req_count // INNER)
    edges = [0]
    for width in (3 * head_cols, fc1_cols, dense_cols, fc2_cols, digit_cols):
        edges.append(edges[-1] + width)
    qkv_full, fc1_full, dense_full_t, fc2_full_t, digits_full = [
        everything[:, edges[i] : edges[i + 1]] for i in range(5)
    ]
    digit_table = digits_full.reshape(req_count, weight_rows * digit_cols)[:, : 2 * label_count]
    digit_table = digit_table.astype(jnp.int32)
    starts = jnp.min(
        digit_table[:, :label_count] * 128 + digit_table[:, label_count:], axis=0
    )

    def add_rows(portion):
        return jnp.dot(normed, portion, preferred_element_type=jnp.float32)

    projected = add_rows(qkv_full)
    lifted = add_rows(fc1_full)
    projected = (projected + qkv_bias.reshape(1, 3 * head_cols)).reshape(
        tok_rows, 3, head_cols // HEAD_DIM, HEAD_DIM
    )
    segment, position = label_rows(places, starts, prefix_lengths)
    queries = (
        rotate_heads(projected[:, 0], position).astype(jnp.bfloat16).reshape(tok_rows, head_cols)
    )
    new_keys = (
        rotate_heads(projected[:, 1], position).astype(jnp.bfloat16).reshape(tok_rows, head_cols)
    )
    new_values = projected[:, 2].astype(jnp.bfloat16).reshape(tok_rows, head_cols)
    key_value = jnp.stack([new_keys, new_values], axis=1)
    pages_here = tok_rows // PAGE
    page_width = PAGE * 2 * head_cols
    pages = key_value.reshape(pages_here, page_width)
    owners = page_owner[:, 0]
    onehot = (owners[:, None] == jnp.arange(req_count, dtype=jnp.int32)[None, :]).astype(jnp.int32)
    earlier = jnp.cumsum(onehot, axis=0) - onehot
    earlier_count = jnp.sum(earlier * onehot, axis=1)
    target = owners * page_cap + earlier_count
    selecting = (target[None, :] == jnp.arange(pool_count, dtype=jnp.int32)[:, None]).astype(
        jnp.bfloat16
    )
    outgoing = jnp.dot(selecting, pages, preferred_element_type=jnp.float32).astype(jnp.bfloat16)
    filled = jnp.sum(selecting, axis=1)
    flag_cols = 128
    flagged = jnp.concatenate(
        [outgoing, jnp.broadcast_to(filled[:, None], (pool_count, flag_cols)).astype(jnp.bfloat16)],
        axis=1,
    )
    arrived = lax.all_to_all(
        flagged.reshape(req_count, page_cap, page_width + flag_cols),
        "req",
        split_axis=0,
        concat_axis=0,
        tiled=True,
    ).reshape(pool_count, page_width + flag_cols)
    incoming = arrived[:, :page_width]
    incoming_filled = arrived[:, page_width]
    slot_ids = slot_perm[0]
    placing = (slot_ids[None, :] == jnp.arange(pool_count, dtype=jnp.int32)[:, None]) & (
        incoming_filled[None, :] > 0
    )
    written = jnp.dot(
        placing.astype(jnp.bfloat16),
        incoming,
        preferred_element_type=jnp.float32,
    ).astype(jnp.bfloat16)
    written_mask = jnp.any(placing, axis=1)
    pool_pages = cache_pool.reshape(pool_count, page_width)
    new_pool = jnp.where(written_mask[:, None], written, pool_pages).reshape(cache_pool.shape)
    local_keys = jnp.concatenate([key_value, prefix_cache], axis=0)
    blocks = [local_keys]
    for shift_by in range(1, SPAN + 1):
        blocks.append(from_behind(local_keys, "req", shift_by))
    key_segs = []
    key_poss = []
    for step_back in range(SPAN + 1):
        block_id = req_index - step_back
        seg_new, pos_new = label_rows(block_id * tok_rows + row_ids, starts, prefix_lengths)
        seg_old, pos_old = prefix_rows(block_id, tok_rows, prefix_count, starts, prefix_lengths)
        key_segs.extend([seg_new, seg_old])
        key_poss.extend([pos_new, pos_old])
    key_segment = jnp.concatenate(key_segs)
    key_position = jnp.concatenate(key_poss)
    allowed = (key_segment[None, :] == segment[:, None]) & (
        key_position[None, :] <= position[:, None]
    )
    allowed = allowed & (
        (position[:, None] - key_position[None, :] < WINDOW) | (key_position[None, :] < SINKS)
    )
    all_keys = jnp.concatenate(blocks, axis=0)
    attended = head_attention(queries, all_keys[:, 0, :], all_keys[:, 1, :], allowed)
    hidden = jax.nn.gelu(lifted + fc1_bias, approximate=True).astype(jnp.bfloat16)
    contract_rows = (((1,), (1,)), ((), ()))
    attn_part = lax.dot_general(
        attended, dense_full_t, contract_rows, preferred_element_type=jnp.float32
    )
    mlp_part = lax.dot_general(
        hidden, fc2_full_t, contract_rows, preferred_element_type=jnp.float32
    )
    branches = attn_part + mlp_part
    summed = lax.psum_scatter(branches, "tensor", scatter_dimension=1, tiled=True)
    layer_out = (tokens.astype(jnp.float32) + summed + dense_bias + fc2_bias).astype(jnp.bfloat16)
    return (layer_out, new_pool)


def solution(mesh):
    placed = (
        P("req", "tensor"),
        P("req"),
        P(),
        P("req", None),
        P("req", None),
        P(),
        P(),
        P("req", None, "tensor"),
        P(None, "tensor"),
        P("tensor", "req"),
        P("tensor"),
        P("req", "tensor"),
        P("tensor"),
        P("tensor", "req"),
        P("tensor"),
        P("req", None, "tensor"),
        P("req", None, "tensor"),
    )
    return jax.shard_map(
        shards,
        mesh=mesh,
        in_specs=placed,
        out_specs=(P("req", "tensor"), P("req", None, "tensor")),
        check_vma=False,
    )
```

```python
import functools

import jax
import jax.numpy as jnp
from jax import lax
from jax.experimental import pallas as pl
from jax.experimental.pallas import tpu as pltpu
from jax.sharding import PartitionSpec as P

HEAD_DIM = 64
ROT = 32
SPAN = 2
SINKS = 4
PAGE = 4
WINDOW = 512
INNER = 4
HOP_US = 3.5
LINK_BYTES_PER_US = 45000.0


MESH_IDS = pl.DeviceIdType.MESH


def ring_gather_kernel(inner, outer, first_block, second_block, first_out, second_out, own_sems,
                       *sems):
    req_index = lax.axis_index("req")
    tensor_index = lax.axis_index("tensor")
    here = (req_index // inner, req_index % inner)
    sizes = (outer, inner)

    def device(shifts):
        at = [lax.rem(here[axis] + shifts[axis] + sizes[axis], sizes[axis]) for axis in range(2)]
        return (at[0] * inner + at[1], tensor_index)

    def index(offsets):
        return tuple(lax.rem(here[axis] + offsets[axis] + sizes[axis], sizes[axis]) for axis in range(2))

    neighbours = (device((0, 1)), device((0, -1)), device((1, 0)), device((-1, 0)))
    barrier = pltpu.get_barrier_semaphore()
    for neighbour in neighbours:
        pl.semaphore_signal(barrier, inc=1, device_id=neighbour, device_id_type=MESH_IDS)
    pl.semaphore_wait(barrier, len(neighbours))

    lanes = []
    for lane, (block_ref, out_ref, first_axis) in enumerate(
        ((first_block, first_out, 1), (second_block, second_out, 0))
    ):
        own = pltpu.make_async_copy(block_ref, out_ref.at[here[0], here[1]], own_sems.at[lane])
        own.start()
        lanes.append((block_ref, out_ref, first_axis, own, sems[4 * lane : 4 * lane + 4]))

    def plans(count):
        return [(0, 1, count // 2), (1, -1, (count - 1) // 2)]

    def offsets_of(axis, offset, other_axis, other_offset):
        pair = [0, 0]
        pair[axis] = offset
        pair[other_axis] = other_offset
        return tuple(pair)

    def copy_of(lane, ring, column, slot, direction, sign, step, arriving):
        block_ref, out_ref, first_axis, _, lane_sems = lanes[lane]
        axis = first_axis if ring == 0 else 1 - first_axis
        piece = -sign * step if arriving else -sign * (step - 1)
        place = offsets_of(axis, piece, 1 - axis, column)
        target = out_ref.at[index(place)]
        if step == 1 and (ring == 0 or column == 0):
            source = block_ref
        else:
            source = target
        first_send, first_recv, second_send, second_recv = lane_sems
        if ring == 0:
            send_sem, recv_sem = first_send.at[direction, step - 1], first_recv.at[direction, step - 1]
        else:
            send_sem = second_send.at[slot, direction, step - 1]
            recv_sem = second_recv.at[slot, direction, step - 1]
        return pltpu.make_async_remote_copy(
            src_ref=source,
            dst_ref=target,
            send_sem=send_sem,
            recv_sem=recv_sem,
            device_id=device(offsets_of(axis, sign, 1 - axis, 0)),
            device_id_type=MESH_IDS,
        )

    tasks = []
    for lane, (block_ref, _, first_axis, _, _) in enumerate(lanes):
        block_bytes = block_ref.shape[0] * block_ref.shape[1] * 2
        duration = HOP_US + block_bytes / LINK_BYTES_PER_US
        first_count = sizes[first_axis]
        second_count = sizes[1 - first_axis]
        columns = [(0, 0.0, None)]
        for direction, sign, steps in plans(first_count):
            ready = 0.0
            for step in range(1, steps + 1):
                need = None if step == 1 else (lane, 0, 0, 0, direction, sign, step - 1)
                tasks.append((ready, len(tasks), (lane, 0, 0, 0, direction, sign, step), need))
                ready += duration
                columns.append((-sign * step, ready, (lane, 0, 0, 0, direction, sign, step)))
        columns.sort(key=lambda entry: entry[1])
        for slot, (column, start, need) in enumerate(columns):
            for direction, sign, steps in plans(second_count):
                ready = start
                for step in range(1, steps + 1):
                    if step > 1:
                        need = (lane, 1, column, slot, direction, sign, step - 1)
                    tasks.append((ready, len(tasks), (lane, 1, column, slot, direction, sign, step), need))
                    ready += duration
                final = (lane, 1, column, slot, direction, sign, steps)
                if steps:
                    tasks.append((float("inf"), len(tasks), None, final))
                need = columns[slot][2]
    tasks.sort(key=lambda entry: (entry[0], entry[1]))
    sent = []
    waited = set()
    for _, _, send, need in tasks:
        if need is not None and need not in waited:
            waited.add(need)
            copy_of(*need, True).wait_recv()
        if send is not None:
            copy = copy_of(*send, False)
            copy.start()
            sent.append(copy)
    for _, _, _, own, _ in lanes:
        own.wait()
    for copy in sent:
        copy.wait_send()


def ring_gather(first_block, second_block, inner, outer):
    semaphores = []
    for first_count, second_count in ((inner, outer), (outer, inner)):
        first_shape = (2, max(1, first_count // 2))
        second_shape = (first_count, 2, max(1, second_count // 2))
        semaphores += [pltpu.SemaphoreType.DMA(first_shape)] * 2
        semaphores += [pltpu.SemaphoreType.DMA(second_shape)] * 2
    gathered = pl.pallas_call(
        functools.partial(ring_gather_kernel, inner, outer),
        out_shape=tuple(
            jax.ShapeDtypeStruct((outer, inner) + block.shape, block.dtype)
            for block in (first_block, second_block)
        ),
        in_specs=[pl.BlockSpec(memory_space=pl.ANY)] * 2,
        out_specs=(pl.BlockSpec(memory_space=pl.ANY),) * 2,
        scratch_shapes=[pltpu.SemaphoreType.DMA((2,))] + semaphores,
        compiler_params=pltpu.CompilerParams(collective_id=0, has_side_effects=True),
    )(first_block, second_block)
    return [part.reshape(outer * inner * part.shape[2], part.shape[3]) for part in gathered]


EPSILON = 1e-05


def from_behind(value, axis, steps):
    count = lax.axis_size(axis)
    leading, last = (max(0, -steps), min(count, count - steps))
    return lax.ppermute(value, axis, [(source, source + steps) for source in range(leading, last)])


def norm_rows(widened, gain, offset_bias):
    average = jnp.mean(widened, axis=-1, keepdims=True)
    centred = widened - average
    spread = jnp.mean(centred * centred, axis=-1, keepdims=True)
    return (centred * lax.rsqrt(spread + EPSILON) * gain + offset_bias).astype(jnp.bfloat16)


def label_rows(places, starts, prefix_lengths):
    labels = jnp.arange(starts.shape[0], dtype=jnp.int32)
    passed = (starts[None, :] <= places[:, None]) & (labels[None, :] >= 1)
    counted = jnp.sum(passed.astype(jnp.int32), axis=1)
    segment = jnp.where(places >= starts[0], 0, counted)
    segment = jnp.where(places < 0, -2, segment)
    onehot = segment[:, None] == labels[None, :]
    earliest = jnp.sum(jnp.where(onehot, starts[None, :], 0), axis=1)
    offset = jnp.sum(jnp.where(onehot, prefix_lengths[None, :], 0), axis=1)
    return (segment, offset + places - earliest)


def prefix_rows(block_id, rows_dev, prefix_count, starts, prefix_lengths):
    labels = jnp.arange(starts.shape[0], dtype=jnp.int32)
    located = (starts >= block_id * rows_dev) & (starts < (block_id + 1) * rows_dev) & (labels >= 1)
    owner_label = jnp.sum(jnp.where(located, labels, 0))
    length = jnp.sum(jnp.where(located, prefix_lengths, 0))
    places = jnp.arange(prefix_count, dtype=jnp.int32)
    usable = jnp.any(located) & (places < length)
    return (jnp.where(usable, owner_label, -2), places)


def rotate_heads(values, position):
    half_rot = ROT // 2
    frequency = 10000.0 ** (-2.0 * jnp.arange(half_rot, dtype=jnp.float32) / ROT)
    angles = position.astype(jnp.float32)[:, None] * frequency[None, :]
    cosine = jnp.cos(angles)[:, None, :]
    sine_vals = jnp.sin(angles)[:, None, :]
    lower = values[..., :half_rot]
    upper = values[..., half_rot:ROT]
    return jnp.concatenate(
        [lower * cosine - upper * sine_vals, upper * cosine + lower * sine_vals, values[..., ROT:]],
        axis=-1,
    )


def head_attention(query_rows, key_rows, value_rows, allowed):
    head_count = query_rows.shape[1] // HEAD_DIM
    score_scale = HEAD_DIM ** (-0.5)

    def one_head(head_index):
        query_cols = lax.dynamic_slice_in_dim(query_rows, head_index * HEAD_DIM, HEAD_DIM, 1)
        key_cols = lax.dynamic_slice_in_dim(key_rows, head_index * HEAD_DIM, HEAD_DIM, 1)
        value_cols = lax.dynamic_slice_in_dim(value_rows, head_index * HEAD_DIM, HEAD_DIM, 1)
        scores = (
            lax.dot_general(
                query_cols, key_cols, (((1,), (1,)), ((), ())), preferred_element_type=jnp.float32
            )
            * score_scale
        )
        masked = jnp.where(allowed, scores, -1e30)
        highest = jnp.max(masked, axis=1, keepdims=True)
        expo = jnp.where(allowed, jnp.exp(masked - highest), 0.0)
        denom = jnp.sum(expo, axis=1, keepdims=True)
        mixed = (
            jnp.dot(expo.astype(jnp.bfloat16), value_cols, preferred_element_type=jnp.float32)
            / denom
        )
        return mixed.astype(jnp.bfloat16)

    outcome = lax.map(one_head, jnp.arange(head_count, dtype=jnp.int32))
    return jnp.transpose(outcome, (1, 0, 2)).reshape(query_rows.shape[0], head_count * HEAD_DIM)


def shards(
    tokens,
    segment_ids,
    prefix_lengths,
    page_owner,
    slot_perm,
    ln_gain,
    ln_bias,
    qkv_weight,
    qkv_bias,
    dense_weight,
    dense_bias,
    fc1_weight,
    fc1_bias,
    fc2_weight,
    fc2_bias,
    prefix_cache,
    cache_pool,
):
    req_count = lax.axis_size("req")
    req_index = lax.axis_index("req")
    tok_rows = tokens.shape[0]
    prefix_count = prefix_cache.shape[0]
    head_cols = qkv_weight.shape[2]
    pool_count = slot_perm.shape[1]
    page_cap = pool_count // req_count
    gathered = lax.all_gather(tokens, "tensor", axis=1, tiled=True)
    normed = norm_rows(gathered.astype(jnp.float32), ln_gain, ln_bias)
    row_ids = jnp.arange(tok_rows, dtype=jnp.int32)
    places = req_index * tok_rows + row_ids
    labels = jnp.arange(prefix_lengths.shape[0], dtype=jnp.int32)
    label_count = labels.shape[0]
    beyond = tok_rows * req_count
    earliest_rows = jnp.min(
        jnp.where(segment_ids[:, None] == labels[None, :], places[:, None], beyond), axis=0
    )
    weight_rows = qkv_weight.shape[0]
    digit_cols = 128
    digits = jnp.concatenate([earliest_rows // 128, earliest_rows % 128]).astype(jnp.bfloat16)
    digits = jnp.pad(digits, (0, weight_rows * digit_cols - 2 * label_count)).reshape(
        weight_rows, digit_cols
    )
    qkv_local = qkv_weight.reshape(weight_rows, 3 * head_cols)
    fc1_cols = fc1_weight.shape[1]
    dense_cols = dense_weight.shape[0]
    fc2_cols = fc2_weight.shape[0]
    first_pack = jnp.concatenate([qkv_local, digits], axis=1)
    second_pack = jnp.concatenate([fc1_weight, dense_weight.T, fc2_weight.T], axis=1)
    first_full, second_full = ring_gather(first_pack, second_pack, INNER, req_count // INNER)
    qkv_full, digits_full = jnp.split(first_full, [3 * head_cols], axis=1)
    fc1_full, dense_full_t, fc2_full_t = jnp.split(
        second_full, [fc1_cols, fc1_cols + dense_cols], axis=1
    )
    digit_table = digits_full.reshape(req_count, weight_rows * digit_cols)[:, : 2 * label_count]
    digit_table = digit_table.astype(jnp.int32)
    starts = jnp.min(
        digit_table[:, :label_count] * 128 + digit_table[:, label_count:], axis=0
    )

    def add_rows(portion):
        return jnp.dot(normed, portion, preferred_element_type=jnp.float32)

    projected = add_rows(qkv_full)
    lifted = add_rows(fc1_full)
    projected = (projected + qkv_bias.reshape(1, 3 * head_cols)).reshape(
        tok_rows, 3, head_cols // HEAD_DIM, HEAD_DIM
    )
    segment, position = label_rows(places, starts, prefix_lengths)
    queries = (
        rotate_heads(projected[:, 0], position).astype(jnp.bfloat16).reshape(tok_rows, head_cols)
    )
    new_keys = (
        rotate_heads(projected[:, 1], position).astype(jnp.bfloat16).reshape(tok_rows, head_cols)
    )
    new_values = projected[:, 2].astype(jnp.bfloat16).reshape(tok_rows, head_cols)
    key_value = jnp.stack([new_keys, new_values], axis=1)
    pages_here = tok_rows // PAGE
    page_width = PAGE * 2 * head_cols
    pages = key_value.reshape(pages_here, page_width)
    owners = page_owner[:, 0]
    onehot = (owners[:, None] == jnp.arange(req_count, dtype=jnp.int32)[None, :]).astype(jnp.int32)
    earlier = jnp.cumsum(onehot, axis=0) - onehot
    earlier_count = jnp.sum(earlier * onehot, axis=1)
    target = owners * page_cap + earlier_count
    selecting = (target[None, :] == jnp.arange(pool_count, dtype=jnp.int32)[:, None]).astype(
        jnp.bfloat16
    )
    outgoing = jnp.dot(selecting, pages, preferred_element_type=jnp.float32).astype(jnp.bfloat16)
    filled = jnp.sum(selecting, axis=1)
    flag_cols = 128
    flagged = jnp.concatenate(
        [outgoing, jnp.broadcast_to(filled[:, None], (pool_count, flag_cols)).astype(jnp.bfloat16)],
        axis=1,
    )
    arrived = lax.all_to_all(
        flagged.reshape(req_count, page_cap, page_width + flag_cols),
        "req",
        split_axis=0,
        concat_axis=0,
        tiled=True,
    ).reshape(pool_count, page_width + flag_cols)
    incoming = arrived[:, :page_width]
    incoming_filled = arrived[:, page_width]
    slot_ids = slot_perm[0]
    placing = (slot_ids[None, :] == jnp.arange(pool_count, dtype=jnp.int32)[:, None]) & (
        incoming_filled[None, :] > 0
    )
    written = jnp.dot(
        placing.astype(jnp.bfloat16),
        incoming,
        preferred_element_type=jnp.float32,
    ).astype(jnp.bfloat16)
    written_mask = jnp.any(placing, axis=1)
    pool_pages = cache_pool.reshape(pool_count, page_width)
    new_pool = jnp.where(written_mask[:, None], written, pool_pages).reshape(cache_pool.shape)
    local_keys = jnp.concatenate([key_value, prefix_cache], axis=0)
    blocks = [local_keys]
    for shift_by in range(1, SPAN + 1):
        blocks.append(from_behind(local_keys, "req", shift_by))
    key_segs = []
    key_poss = []
    for step_back in range(SPAN + 1):
        block_id = req_index - step_back
        seg_new, pos_new = label_rows(block_id * tok_rows + row_ids, starts, prefix_lengths)
        seg_old, pos_old = prefix_rows(block_id, tok_rows, prefix_count, starts, prefix_lengths)
        key_segs.extend([seg_new, seg_old])
        key_poss.extend([pos_new, pos_old])
    key_segment = jnp.concatenate(key_segs)
    key_position = jnp.concatenate(key_poss)
    allowed = (key_segment[None, :] == segment[:, None]) & (
        key_position[None, :] <= position[:, None]
    )
    allowed = allowed & (
        (position[:, None] - key_position[None, :] < WINDOW) | (key_position[None, :] < SINKS)
    )
    all_keys = jnp.concatenate(blocks, axis=0)
    attended = head_attention(queries, all_keys[:, 0, :], all_keys[:, 1, :], allowed)
    hidden = jax.nn.gelu(lifted + fc1_bias, approximate=True).astype(jnp.bfloat16)
    contract_rows = (((1,), (1,)), ((), ()))
    attn_part = lax.dot_general(
        attended, dense_full_t, contract_rows, preferred_element_type=jnp.float32
    )
    mlp_part = lax.dot_general(
        hidden, fc2_full_t, contract_rows, preferred_element_type=jnp.float32
    )
    branches = attn_part + mlp_part
    summed = lax.psum_scatter(branches, "tensor", scatter_dimension=1, tiled=True)
    layer_out = (tokens.astype(jnp.float32) + summed + dense_bias + fc2_bias).astype(jnp.bfloat16)
    return (layer_out, new_pool)


def solution(mesh):
    placed = (
        P("req", "tensor"),
        P("req"),
        P(),
        P("req", None),
        P("req", None),
        P(),
        P(),
        P("req", None, "tensor"),
        P(None, "tensor"),
        P("tensor", "req"),
        P("tensor"),
        P("req", "tensor"),
        P("tensor"),
        P("tensor", "req"),
        P("tensor"),
        P("req", None, "tensor"),
        P("req", None, "tensor"),
    )
    return jax.shard_map(
        shards,
        mesh=mesh,
        in_specs=placed,
        out_specs=(P("req", "tensor"), P("req", None, "tensor")),
        check_vma=False,
    )
```

```python
import functools

import jax
import jax.numpy as jnp
from jax import lax
from jax.experimental import pallas as pl
from jax.experimental.pallas import tpu as pltpu
from jax.sharding import PartitionSpec as P

HEAD_DIM = 64
ROT = 32
SPAN = 2
SINKS = 4
PAGE = 4
WINDOW = 512
INNER = 4
HOP_US = 3.5
LINK_BYTES_PER_US = 45000.0


MESH_IDS = pl.DeviceIdType.MESH


def ring_gather_kernel(inner, outer, first_block, second_block, first_out, second_out, own_sems,
                       *sems):
    req_index = lax.axis_index("req")
    tensor_index = lax.axis_index("tensor")
    here = (req_index // inner, req_index % inner)
    sizes = (outer, inner)

    def device(shifts):
        at = [lax.rem(here[axis] + shifts[axis] + sizes[axis], sizes[axis]) for axis in range(2)]
        return (at[0] * inner + at[1], tensor_index)

    def index(offsets):
        return tuple(lax.rem(here[axis] + offsets[axis] + sizes[axis], sizes[axis]) for axis in range(2))

    neighbours = (device((0, 1)), device((0, -1)), device((1, 0)), device((-1, 0)))
    barrier = pltpu.get_barrier_semaphore()
    for neighbour in neighbours:
        pl.semaphore_signal(barrier, inc=1, device_id=neighbour, device_id_type=MESH_IDS)
    pl.semaphore_wait(barrier, len(neighbours))

    lanes = []
    for lane, (block_ref, out_ref, first_axis) in enumerate(
        ((first_block, first_out, 1), (second_block, second_out, 0))
    ):
        own = pltpu.make_async_copy(block_ref, out_ref.at[here[0], here[1]], own_sems.at[lane])
        own.start()
        lanes.append((block_ref, out_ref, first_axis, own, sems[4 * lane : 4 * lane + 4]))

    def plans(count):
        return [(0, 1, count // 2), (1, -1, (count - 1) // 2)]

    def offsets_of(axis, offset, other_axis, other_offset):
        pair = [0, 0]
        pair[axis] = offset
        pair[other_axis] = other_offset
        return tuple(pair)

    def copy_of(lane, ring, column, slot, direction, sign, step, arriving):
        block_ref, out_ref, first_axis, _, lane_sems = lanes[lane]
        axis = first_axis if ring == 0 else 1 - first_axis
        piece = -sign * step if arriving else -sign * (step - 1)
        place = offsets_of(axis, piece, 1 - axis, column)
        target = out_ref.at[index(place)]
        if step == 1 and (ring == 0 or column == 0):
            source = block_ref
        else:
            source = target
        first_send, first_recv, second_send, second_recv = lane_sems
        if ring == 0:
            send_sem, recv_sem = first_send.at[direction, step - 1], first_recv.at[direction, step - 1]
        else:
            send_sem = second_send.at[slot, direction, step - 1]
            recv_sem = second_recv.at[slot, direction, step - 1]
        return pltpu.make_async_remote_copy(
            src_ref=source,
            dst_ref=target,
            send_sem=send_sem,
            recv_sem=recv_sem,
            device_id=device(offsets_of(axis, sign, 1 - axis, 0)),
            device_id_type=MESH_IDS,
        )

    tasks = []
    for lane, (block_ref, _, first_axis, _, _) in enumerate(lanes):
        block_bytes = block_ref.shape[0] * block_ref.shape[1] * 2
        duration = HOP_US + block_bytes / LINK_BYTES_PER_US
        first_count = sizes[first_axis]
        second_count = sizes[1 - first_axis]
        columns = [(0, 0.0, None)]
        for direction, sign, steps in plans(first_count):
            ready = 0.0
            for step in range(1, steps + 1):
                need = None if step == 1 else (lane, 0, 0, 0, direction, sign, step - 1)
                tasks.append((ready, len(tasks), (lane, 0, 0, 0, direction, sign, step), need))
                ready += duration
                columns.append((-sign * step, ready, (lane, 0, 0, 0, direction, sign, step)))
        columns.sort(key=lambda entry: entry[1])
        for slot, (column, start, need) in enumerate(columns):
            for direction, sign, steps in plans(second_count):
                ready = start
                for step in range(1, steps + 1):
                    if step > 1:
                        need = (lane, 1, column, slot, direction, sign, step - 1)
                    tasks.append((ready, len(tasks), (lane, 1, column, slot, direction, sign, step), need))
                    ready += duration
                final = (lane, 1, column, slot, direction, sign, steps)
                if steps:
                    tasks.append((float("inf"), len(tasks), None, final))
                need = columns[slot][2]
    tasks.sort(key=lambda entry: (entry[0], entry[1]))
    sent = []
    waited = set()
    for _, _, send, need in tasks:
        if need is not None and need not in waited:
            waited.add(need)
            copy_of(*need, True).wait_recv()
        if send is not None:
            copy = copy_of(*send, False)
            copy.start()
            sent.append(copy)
    for _, _, _, own, _ in lanes:
        own.wait()
    for copy in sent:
        copy.wait_send()


def ring_gather(first_block, second_block, inner, outer):
    semaphores = []
    for first_count, second_count in ((inner, outer), (outer, inner)):
        first_shape = (2, max(1, first_count // 2))
        second_shape = (first_count, 2, max(1, second_count // 2))
        semaphores += [pltpu.SemaphoreType.DMA(first_shape)] * 2
        semaphores += [pltpu.SemaphoreType.DMA(second_shape)] * 2
    gathered = pl.pallas_call(
        functools.partial(ring_gather_kernel, inner, outer),
        out_shape=tuple(
            jax.ShapeDtypeStruct((outer, inner) + block.shape, block.dtype)
            for block in (first_block, second_block)
        ),
        in_specs=[pl.BlockSpec(memory_space=pl.ANY)] * 2,
        out_specs=(pl.BlockSpec(memory_space=pl.ANY),) * 2,
        scratch_shapes=[pltpu.SemaphoreType.DMA((2,))] + semaphores,
        compiler_params=pltpu.CompilerParams(collective_id=0, has_side_effects=True),
    )(first_block, second_block)
    return [part.reshape(outer * inner * part.shape[2], part.shape[3]) for part in gathered]


EPSILON = 1e-05


def from_behind(value, axis, steps):
    count = lax.axis_size(axis)
    leading, last = (max(0, -steps), min(count, count - steps))
    return lax.ppermute(value, axis, [(source, source + steps) for source in range(leading, last)])


def norm_rows(widened, gain, offset_bias):
    average = jnp.mean(widened, axis=-1, keepdims=True)
    centred = widened - average
    spread = jnp.mean(centred * centred, axis=-1, keepdims=True)
    return (centred * lax.rsqrt(spread + EPSILON) * gain + offset_bias).astype(jnp.bfloat16)


def label_rows(places, starts, prefix_lengths):
    labels = jnp.arange(starts.shape[0], dtype=jnp.int32)
    passed = (starts[None, :] <= places[:, None]) & (labels[None, :] >= 1)
    counted = jnp.sum(passed.astype(jnp.int32), axis=1)
    segment = jnp.where(places >= starts[0], 0, counted)
    segment = jnp.where(places < 0, -2, segment)
    onehot = segment[:, None] == labels[None, :]
    earliest = jnp.sum(jnp.where(onehot, starts[None, :], 0), axis=1)
    offset = jnp.sum(jnp.where(onehot, prefix_lengths[None, :], 0), axis=1)
    return (segment, offset + places - earliest)


def prefix_rows(block_id, rows_dev, prefix_count, starts, prefix_lengths):
    labels = jnp.arange(starts.shape[0], dtype=jnp.int32)
    located = (starts >= block_id * rows_dev) & (starts < (block_id + 1) * rows_dev) & (labels >= 1)
    owner_label = jnp.sum(jnp.where(located, labels, 0))
    length = jnp.sum(jnp.where(located, prefix_lengths, 0))
    places = jnp.arange(prefix_count, dtype=jnp.int32)
    usable = jnp.any(located) & (places < length)
    return (jnp.where(usable, owner_label, -2), places)


def rotate_heads(values, position):
    half_rot = ROT // 2
    frequency = 10000.0 ** (-2.0 * jnp.arange(half_rot, dtype=jnp.float32) / ROT)
    angles = position.astype(jnp.float32)[:, None] * frequency[None, :]
    cosine = jnp.cos(angles)[:, None, :]
    sine_vals = jnp.sin(angles)[:, None, :]
    lower = values[..., :half_rot]
    upper = values[..., half_rot:ROT]
    return jnp.concatenate(
        [lower * cosine - upper * sine_vals, upper * cosine + lower * sine_vals, values[..., ROT:]],
        axis=-1,
    )


def head_attention(query_rows, key_rows, value_rows, allowed):
    head_count = query_rows.shape[1] // HEAD_DIM
    score_scale = HEAD_DIM ** (-0.5)

    def one_head(head_index):
        query_cols = lax.dynamic_slice_in_dim(query_rows, head_index * HEAD_DIM, HEAD_DIM, 1)
        key_cols = lax.dynamic_slice_in_dim(key_rows, head_index * HEAD_DIM, HEAD_DIM, 1)
        value_cols = lax.dynamic_slice_in_dim(value_rows, head_index * HEAD_DIM, HEAD_DIM, 1)
        scores = (
            lax.dot_general(
                query_cols, key_cols, (((1,), (1,)), ((), ())), preferred_element_type=jnp.float32
            )
            * score_scale
        )
        masked = jnp.where(allowed, scores, -1e30)
        highest = jnp.max(masked, axis=1, keepdims=True)
        expo = jnp.where(allowed, jnp.exp(masked - highest), 0.0)
        denom = jnp.sum(expo, axis=1, keepdims=True)
        mixed = (
            jnp.dot(expo.astype(jnp.bfloat16), value_cols, preferred_element_type=jnp.float32)
            / denom
        )
        return mixed.astype(jnp.bfloat16)

    outcome = lax.map(one_head, jnp.arange(head_count, dtype=jnp.int32))
    return jnp.transpose(outcome, (1, 0, 2)).reshape(query_rows.shape[0], head_count * HEAD_DIM)


def shards(
    tokens,
    segment_ids,
    prefix_lengths,
    page_owner,
    slot_perm,
    ln_gain,
    ln_bias,
    qkv_weight,
    qkv_bias,
    dense_weight,
    dense_bias,
    fc1_weight,
    fc1_bias,
    fc2_weight,
    fc2_bias,
    prefix_cache,
    cache_pool,
):
    req_count = lax.axis_size("req")
    req_index = lax.axis_index("req")
    tok_rows = tokens.shape[0]
    prefix_count = prefix_cache.shape[0]
    head_cols = qkv_weight.shape[2]
    pool_count = slot_perm.shape[1]
    page_cap = pool_count // req_count
    gathered = lax.all_gather(tokens, "tensor", axis=1, tiled=True)
    normed = norm_rows(gathered.astype(jnp.float32), ln_gain, ln_bias)
    row_ids = jnp.arange(tok_rows, dtype=jnp.int32)
    places = req_index * tok_rows + row_ids
    labels = jnp.arange(prefix_lengths.shape[0], dtype=jnp.int32)
    label_count = labels.shape[0]
    beyond = tok_rows * req_count
    earliest_rows = jnp.min(
        jnp.where(segment_ids[:, None] == labels[None, :], places[:, None], beyond), axis=0
    )
    weight_rows = qkv_weight.shape[0]
    digit_cols = 128
    owners = page_owner[:, 0]
    owner_count = owners.shape[0]
    digits = jnp.concatenate([earliest_rows // 128, earliest_rows % 128, owners])
    digits = digits.astype(jnp.bfloat16)
    digit_used = 2 * label_count + owner_count
    digits = jnp.pad(digits, (0, weight_rows * digit_cols - digit_used)).reshape(
        weight_rows, digit_cols
    )
    qkv_local = qkv_weight.reshape(weight_rows, 3 * head_cols)
    fc1_cols = fc1_weight.shape[1]
    dense_cols = dense_weight.shape[0]
    fc2_cols = fc2_weight.shape[0]
    first_pack = jnp.concatenate([qkv_local, digits], axis=1)
    second_pack = jnp.concatenate([fc1_weight, dense_weight.T, fc2_weight.T], axis=1)
    first_full, second_full = ring_gather(first_pack, second_pack, INNER, req_count // INNER)
    qkv_full, digits_full = jnp.split(first_full, [3 * head_cols], axis=1)
    fc1_full, dense_full_t, fc2_full_t = jnp.split(
        second_full, [fc1_cols, fc1_cols + dense_cols], axis=1
    )
    digit_table = digits_full.reshape(req_count, weight_rows * digit_cols)[:, :digit_used]
    digit_table = digit_table.astype(jnp.int32)
    owner_table = digit_table[:, 2 * label_count :]
    starts = jnp.min(
        digit_table[:, :label_count] * 128 + digit_table[:, label_count : 2 * label_count], axis=0
    )

    def add_rows(portion):
        return jnp.dot(normed, portion, preferred_element_type=jnp.float32)

    projected = add_rows(qkv_full)
    lifted = add_rows(fc1_full)
    projected = (projected + qkv_bias.reshape(1, 3 * head_cols)).reshape(
        tok_rows, 3, head_cols // HEAD_DIM, HEAD_DIM
    )
    segment, position = label_rows(places, starts, prefix_lengths)
    queries = (
        rotate_heads(projected[:, 0], position).astype(jnp.bfloat16).reshape(tok_rows, head_cols)
    )
    new_keys = (
        rotate_heads(projected[:, 1], position).astype(jnp.bfloat16).reshape(tok_rows, head_cols)
    )
    new_values = projected[:, 2].astype(jnp.bfloat16).reshape(tok_rows, head_cols)
    key_value = jnp.stack([new_keys, new_values], axis=1)
    pages_here = tok_rows // PAGE
    page_width = PAGE * 2 * head_cols
    pages = key_value.reshape(pages_here, page_width)
    onehot = (owners[:, None] == jnp.arange(req_count, dtype=jnp.int32)[None, :]).astype(jnp.int32)
    earlier = jnp.cumsum(onehot, axis=0) - onehot
    earlier_count = jnp.sum(earlier * onehot, axis=1)
    target = owners * page_cap + earlier_count
    selecting = (target[None, :] == jnp.arange(pool_count, dtype=jnp.int32)[:, None]).astype(
        jnp.bfloat16
    )
    outgoing = jnp.dot(selecting, pages, preferred_element_type=jnp.float32).astype(jnp.bfloat16)
    incoming = lax.all_to_all(
        outgoing.reshape(req_count, page_cap, page_width), "req", split_axis=0, concat_axis=0, tiled=True
    ).reshape(pool_count, page_width)
    mine = jnp.sum((owner_table == req_index).astype(jnp.int32), axis=1)
    incoming_filled = (
        mine[:, None] > jnp.arange(page_cap, dtype=jnp.int32)[None, :]
    ).reshape(pool_count)
    slot_ids = slot_perm[0]
    placing = (slot_ids[None, :] == jnp.arange(pool_count, dtype=jnp.int32)[:, None]) & (
        incoming_filled[None, :] > 0
    )
    written = jnp.dot(
        placing.astype(jnp.bfloat16),
        incoming,
        preferred_element_type=jnp.float32,
    ).astype(jnp.bfloat16)
    written_mask = jnp.any(placing, axis=1)
    pool_pages = cache_pool.reshape(pool_count, page_width)
    new_pool = jnp.where(written_mask[:, None], written, pool_pages).reshape(cache_pool.shape)
    local_keys = jnp.concatenate([key_value, prefix_cache], axis=0)
    blocks = [local_keys]
    for shift_by in range(1, SPAN + 1):
        blocks.append(from_behind(local_keys, "req", shift_by))
    key_segs = []
    key_poss = []
    for step_back in range(SPAN + 1):
        block_id = req_index - step_back
        seg_new, pos_new = label_rows(block_id * tok_rows + row_ids, starts, prefix_lengths)
        seg_old, pos_old = prefix_rows(block_id, tok_rows, prefix_count, starts, prefix_lengths)
        key_segs.extend([seg_new, seg_old])
        key_poss.extend([pos_new, pos_old])
    key_segment = jnp.concatenate(key_segs)
    key_position = jnp.concatenate(key_poss)
    allowed = (key_segment[None, :] == segment[:, None]) & (
        key_position[None, :] <= position[:, None]
    )
    allowed = allowed & (
        (position[:, None] - key_position[None, :] < WINDOW) | (key_position[None, :] < SINKS)
    )
    all_keys = jnp.concatenate(blocks, axis=0)
    hidden = jax.nn.gelu(lifted + fc1_bias, approximate=True).astype(jnp.bfloat16)
    mlp_part = lax.dot_general(
        hidden, fc2_full_t, (((1,), (1,)), ((), ())), preferred_element_type=jnp.float32
    )
    queries, mlp_part = lax.optimization_barrier((queries, mlp_part))
    attended = head_attention(queries, all_keys[:, 0, :], all_keys[:, 1, :], allowed)
    contract_rows = (((1,), (1,)), ((), ()))
    attn_part = lax.dot_general(
        attended, dense_full_t, contract_rows, preferred_element_type=jnp.float32
    )
    branches = attn_part + mlp_part
    summed = lax.psum_scatter(branches, "tensor", scatter_dimension=1, tiled=True)
    layer_out = (tokens.astype(jnp.float32) + summed + dense_bias + fc2_bias).astype(jnp.bfloat16)
    return (layer_out, new_pool)


def solution(mesh):
    placed = (
        P("req", "tensor"),
        P("req"),
        P(),
        P("req", None),
        P("req", None),
        P(),
        P(),
        P("req", None, "tensor"),
        P(None, "tensor"),
        P("tensor", "req"),
        P("tensor"),
        P("req", "tensor"),
        P("tensor"),
        P("tensor", "req"),
        P("tensor"),
        P("req", None, "tensor"),
        P("req", None, "tensor"),
    )
    return jax.shard_map(
        shards,
        mesh=mesh,
        in_specs=placed,
        out_specs=(P("req", "tensor"), P("req", None, "tensor")),
        check_vma=False,
    )
```

```python
import functools

import jax
import jax.numpy as jnp
from jax import lax
from jax.experimental import pallas as pl
from jax.experimental.pallas import tpu as pltpu
from jax.sharding import PartitionSpec as P

HEAD_DIM = 64
ROT = 32
SPAN = 2
SINKS = 4
PAGE = 4
WINDOW = 512
INNER = 4
HOP_US = 3.5
LINK_BYTES_PER_US = 45000.0


MESH_IDS = pl.DeviceIdType.MESH


def ring_gather_kernel(inner, outer, first_block, second_block, first_out, second_out, own_sems,
                       *sems):
    req_index = lax.axis_index("req")
    tensor_index = lax.axis_index("tensor")
    here = (req_index // inner, req_index % inner)
    sizes = (outer, inner)

    def device(shifts):
        at = [lax.rem(here[axis] + shifts[axis] + sizes[axis], sizes[axis]) for axis in range(2)]
        return (at[0] * inner + at[1], tensor_index)

    def index(offsets):
        return tuple(lax.rem(here[axis] + offsets[axis] + sizes[axis], sizes[axis]) for axis in range(2))

    neighbours = (device((0, 1)), device((0, -1)), device((1, 0)), device((-1, 0)))
    barrier = pltpu.get_barrier_semaphore()
    for neighbour in neighbours:
        pl.semaphore_signal(barrier, inc=1, device_id=neighbour, device_id_type=MESH_IDS)
    pl.semaphore_wait(barrier, len(neighbours))

    lanes = []
    for lane, (block_ref, out_ref, first_axis) in enumerate(
        ((first_block, first_out, 1), (second_block, second_out, 0))
    ):
        own = pltpu.make_async_copy(block_ref, out_ref.at[here[0], here[1]], own_sems.at[lane])
        own.start()
        lanes.append((block_ref, out_ref, first_axis, own, sems[4 * lane : 4 * lane + 4]))

    def plans(count):
        return [(0, 1, count // 2), (1, -1, (count - 1) // 2)]

    def offsets_of(axis, offset, other_axis, other_offset):
        pair = [0, 0]
        pair[axis] = offset
        pair[other_axis] = other_offset
        return tuple(pair)

    def copy_of(lane, ring, column, slot, direction, sign, step, arriving):
        block_ref, out_ref, first_axis, _, lane_sems = lanes[lane]
        axis = first_axis if ring == 0 else 1 - first_axis
        piece = -sign * step if arriving else -sign * (step - 1)
        place = offsets_of(axis, piece, 1 - axis, column)
        target = out_ref.at[index(place)]
        if step == 1 and (ring == 0 or column == 0):
            source = block_ref
        else:
            source = target
        first_send, first_recv, second_send, second_recv = lane_sems
        if ring == 0:
            send_sem, recv_sem = first_send.at[direction, step - 1], first_recv.at[direction, step - 1]
        else:
            send_sem = second_send.at[slot, direction, step - 1]
            recv_sem = second_recv.at[slot, direction, step - 1]
        return pltpu.make_async_remote_copy(
            src_ref=source,
            dst_ref=target,
            send_sem=send_sem,
            recv_sem=recv_sem,
            device_id=device(offsets_of(axis, sign, 1 - axis, 0)),
            device_id_type=MESH_IDS,
        )

    tasks = []
    for lane, (block_ref, _, first_axis, _, _) in enumerate(lanes):
        block_bytes = block_ref.shape[0] * block_ref.shape[1] * 2
        duration = HOP_US + block_bytes / LINK_BYTES_PER_US
        first_count = sizes[first_axis]
        second_count = sizes[1 - first_axis]
        columns = [(0, 0.0, None)]
        for direction, sign, steps in plans(first_count):
            ready = 0.0
            for step in range(1, steps + 1):
                need = None if step == 1 else (lane, 0, 0, 0, direction, sign, step - 1)
                tasks.append((ready, len(tasks), (lane, 0, 0, 0, direction, sign, step), need))
                ready += duration
                columns.append((-sign * step, ready, (lane, 0, 0, 0, direction, sign, step)))
        columns.sort(key=lambda entry: entry[1])
        for slot, (column, start, need) in enumerate(columns):
            for direction, sign, steps in plans(second_count):
                ready = start
                for step in range(1, steps + 1):
                    if step > 1:
                        need = (lane, 1, column, slot, direction, sign, step - 1)
                    tasks.append((ready, len(tasks), (lane, 1, column, slot, direction, sign, step), need))
                    ready += duration
                final = (lane, 1, column, slot, direction, sign, steps)
                if steps:
                    tasks.append((float("inf"), len(tasks), None, final))
                need = columns[slot][2]
    tasks.sort(key=lambda entry: (entry[0], entry[1]))
    sent = []
    waited = set()
    for _, _, send, need in tasks:
        if need is not None and need not in waited:
            waited.add(need)
            copy_of(*need, True).wait_recv()
        if send is not None:
            copy = copy_of(*send, False)
            copy.start()
            sent.append(copy)
    for _, _, _, own, _ in lanes:
        own.wait()
    for copy in sent:
        copy.wait_send()


def ring_gather(first_block, second_block, inner, outer):
    semaphores = []
    for first_count, second_count in ((inner, outer), (outer, inner)):
        first_shape = (2, max(1, first_count // 2))
        second_shape = (first_count, 2, max(1, second_count // 2))
        semaphores += [pltpu.SemaphoreType.DMA(first_shape)] * 2
        semaphores += [pltpu.SemaphoreType.DMA(second_shape)] * 2
    gathered = pl.pallas_call(
        functools.partial(ring_gather_kernel, inner, outer),
        out_shape=tuple(
            jax.ShapeDtypeStruct((outer, inner) + block.shape, block.dtype)
            for block in (first_block, second_block)
        ),
        in_specs=[pl.BlockSpec(memory_space=pl.ANY)] * 2,
        out_specs=(pl.BlockSpec(memory_space=pl.ANY),) * 2,
        scratch_shapes=[pltpu.SemaphoreType.DMA((2,))] + semaphores,
        compiler_params=pltpu.CompilerParams(collective_id=0, has_side_effects=True),
    )(first_block, second_block)
    return [part.reshape(outer * inner * part.shape[2], part.shape[3]) for part in gathered]


EPSILON = 1e-05


def from_behind(value, axis, steps):
    count = lax.axis_size(axis)
    leading, last = (max(0, -steps), min(count, count - steps))
    return lax.ppermute(value, axis, [(source, source + steps) for source in range(leading, last)])


def norm_rows(widened, gain, offset_bias):
    average = jnp.mean(widened, axis=-1, keepdims=True)
    centred = widened - average
    spread = jnp.mean(centred * centred, axis=-1, keepdims=True)
    return (centred * lax.rsqrt(spread + EPSILON) * gain + offset_bias).astype(jnp.bfloat16)


def label_rows(places, starts, prefix_lengths):
    labels = jnp.arange(starts.shape[0], dtype=jnp.int32)
    passed = (starts[None, :] <= places[:, None]) & (labels[None, :] >= 1)
    counted = jnp.sum(passed.astype(jnp.int32), axis=1)
    segment = jnp.where(places >= starts[0], 0, counted)
    segment = jnp.where(places < 0, -2, segment)
    onehot = segment[:, None] == labels[None, :]
    earliest = jnp.sum(jnp.where(onehot, starts[None, :], 0), axis=1)
    offset = jnp.sum(jnp.where(onehot, prefix_lengths[None, :], 0), axis=1)
    return (segment, offset + places - earliest)


def prefix_rows(block_id, rows_dev, prefix_count, starts, prefix_lengths):
    labels = jnp.arange(starts.shape[0], dtype=jnp.int32)
    located = (starts >= block_id * rows_dev) & (starts < (block_id + 1) * rows_dev) & (labels >= 1)
    owner_label = jnp.sum(jnp.where(located, labels, 0))
    length = jnp.sum(jnp.where(located, prefix_lengths, 0))
    places = jnp.arange(prefix_count, dtype=jnp.int32)
    usable = jnp.any(located) & (places < length)
    return (jnp.where(usable, owner_label, -2), places)


def rotate_heads(values, position):
    half_rot = ROT // 2
    frequency = 10000.0 ** (-2.0 * jnp.arange(half_rot, dtype=jnp.float32) / ROT)
    angles = position.astype(jnp.float32)[:, None] * frequency[None, :]
    cosine = jnp.cos(angles)[:, None, :]
    sine_vals = jnp.sin(angles)[:, None, :]
    lower = values[..., :half_rot]
    upper = values[..., half_rot:ROT]
    return jnp.concatenate(
        [lower * cosine - upper * sine_vals, upper * cosine + lower * sine_vals, values[..., ROT:]],
        axis=-1,
    )


def head_attention(query_rows, key_rows, value_rows, allowed):
    head_count = query_rows.shape[1] // HEAD_DIM
    score_scale = HEAD_DIM ** (-0.5)

    def one_head(head_index):
        query_cols = lax.dynamic_slice_in_dim(query_rows, head_index * HEAD_DIM, HEAD_DIM, 1)
        key_cols = lax.dynamic_slice_in_dim(key_rows, head_index * HEAD_DIM, HEAD_DIM, 1)
        value_cols = lax.dynamic_slice_in_dim(value_rows, head_index * HEAD_DIM, HEAD_DIM, 1)
        scores = (
            lax.dot_general(
                query_cols, key_cols, (((1,), (1,)), ((), ())), preferred_element_type=jnp.float32
            )
            * score_scale
        )
        masked = jnp.where(allowed, scores, -1e30)
        highest = jnp.max(masked, axis=1, keepdims=True)
        expo = jnp.where(allowed, jnp.exp(masked - highest), 0.0)
        denom = jnp.sum(expo, axis=1, keepdims=True)
        mixed = (
            jnp.dot(expo.astype(jnp.bfloat16), value_cols, preferred_element_type=jnp.float32)
            / denom
        )
        return mixed.astype(jnp.bfloat16)

    outcome = lax.map(one_head, jnp.arange(head_count, dtype=jnp.int32))
    return jnp.transpose(outcome, (1, 0, 2)).reshape(query_rows.shape[0], head_count * HEAD_DIM)


def shards(
    tokens,
    segment_ids,
    prefix_lengths,
    page_owner,
    slot_perm,
    ln_gain,
    ln_bias,
    qkv_weight,
    qkv_bias,
    dense_weight,
    dense_bias,
    fc1_weight,
    fc1_bias,
    fc2_weight,
    fc2_bias,
    prefix_cache,
    cache_pool,
):
    req_count = lax.axis_size("req")
    req_index = lax.axis_index("req")
    tok_rows = tokens.shape[0]
    prefix_count = prefix_cache.shape[0]
    head_cols = qkv_weight.shape[2]
    pool_count = slot_perm.shape[1]
    page_cap = pool_count // req_count
    gathered = lax.all_gather(tokens, "tensor", axis=1, tiled=True)
    normed = norm_rows(gathered.astype(jnp.float32), ln_gain, ln_bias)
    row_ids = jnp.arange(tok_rows, dtype=jnp.int32)
    places = req_index * tok_rows + row_ids
    labels = jnp.arange(prefix_lengths.shape[0], dtype=jnp.int32)
    label_count = labels.shape[0]
    beyond = tok_rows * req_count
    earliest_rows = jnp.min(
        jnp.where(segment_ids[:, None] == labels[None, :], places[:, None], beyond), axis=0
    )
    weight_rows = qkv_weight.shape[0]
    digit_cols = 128
    digits = jnp.concatenate([earliest_rows // 128, earliest_rows % 128]).astype(jnp.bfloat16)
    digits = jnp.pad(digits, (0, weight_rows * digit_cols - 2 * label_count)).reshape(
        weight_rows, digit_cols
    )
    qkv_local = qkv_weight.reshape(weight_rows, 3 * head_cols)
    fc1_cols = fc1_weight.shape[1]
    dense_cols = dense_weight.shape[0]
    fc2_cols = fc2_weight.shape[0]
    second_pack = jnp.concatenate([fc1_weight, dense_weight.T, fc2_weight.T, digits], axis=1)
    qkv_full, second_full = ring_gather(qkv_local, second_pack, INNER, req_count // INNER)
    fc1_full, dense_full_t, fc2_full_t, digits_full = jnp.split(
        second_full, [fc1_cols, fc1_cols + dense_cols, fc1_cols + dense_cols + fc2_cols], axis=1
    )
    digit_table = digits_full.reshape(req_count, weight_rows * digit_cols)[:, : 2 * label_count]
    digit_table = digit_table.astype(jnp.int32)
    starts = jnp.min(
        digit_table[:, :label_count] * 128 + digit_table[:, label_count:], axis=0
    )

    def add_rows(portion):
        return jnp.dot(normed, portion, preferred_element_type=jnp.float32)

    projected = add_rows(qkv_full)
    lifted = add_rows(fc1_full)
    projected = (projected + qkv_bias.reshape(1, 3 * head_cols)).reshape(
        tok_rows, 3, head_cols // HEAD_DIM, HEAD_DIM
    )
    segment, position = label_rows(places, starts, prefix_lengths)
    queries = (
        rotate_heads(projected[:, 0], position).astype(jnp.bfloat16).reshape(tok_rows, head_cols)
    )
    new_keys = (
        rotate_heads(projected[:, 1], position).astype(jnp.bfloat16).reshape(tok_rows, head_cols)
    )
    new_values = projected[:, 2].astype(jnp.bfloat16).reshape(tok_rows, head_cols)
    key_value = jnp.stack([new_keys, new_values], axis=1)
    pages_here = tok_rows // PAGE
    page_width = PAGE * 2 * head_cols
    pages = key_value.reshape(pages_here, page_width)
    owners = page_owner[:, 0]
    onehot = (owners[:, None] == jnp.arange(req_count, dtype=jnp.int32)[None, :]).astype(jnp.int32)
    earlier = jnp.cumsum(onehot, axis=0) - onehot
    earlier_count = jnp.sum(earlier * onehot, axis=1)
    target = owners * page_cap + earlier_count
    selecting = (target[None, :] == jnp.arange(pool_count, dtype=jnp.int32)[:, None]).astype(
        jnp.bfloat16
    )
    outgoing = jnp.dot(selecting, pages, preferred_element_type=jnp.float32).astype(jnp.bfloat16)
    filled = jnp.sum(selecting, axis=1)
    flag_cols = 128
    flagged = jnp.concatenate(
        [outgoing, jnp.broadcast_to(filled[:, None], (pool_count, flag_cols)).astype(jnp.bfloat16)],
        axis=1,
    )
    arrived = lax.all_to_all(
        flagged.reshape(req_count, page_cap, page_width + flag_cols),
        "req",
        split_axis=0,
        concat_axis=0,
        tiled=True,
    ).reshape(pool_count, page_width + flag_cols)
    incoming = arrived[:, :page_width]
    incoming_filled = arrived[:, page_width]
    slot_ids = slot_perm[0]
    placing = (slot_ids[None, :] == jnp.arange(pool_count, dtype=jnp.int32)[:, None]) & (
        incoming_filled[None, :] > 0
    )
    written = jnp.dot(
        placing.astype(jnp.bfloat16),
        incoming,
        preferred_element_type=jnp.float32,
    ).astype(jnp.bfloat16)
    written_mask = jnp.any(placing, axis=1)
    pool_pages = cache_pool.reshape(pool_count, page_width)
    new_pool = jnp.where(written_mask[:, None], written, pool_pages).reshape(cache_pool.shape)
    local_keys = jnp.concatenate([key_value, prefix_cache], axis=0)
    blocks = [local_keys]
    for shift_by in range(1, SPAN + 1):
        blocks.append(from_behind(local_keys, "req", shift_by))
    key_segs = []
    key_poss = []
    for step_back in range(SPAN + 1):
        block_id = req_index - step_back
        seg_new, pos_new = label_rows(block_id * tok_rows + row_ids, starts, prefix_lengths)
        seg_old, pos_old = prefix_rows(block_id, tok_rows, prefix_count, starts, prefix_lengths)
        key_segs.extend([seg_new, seg_old])
        key_poss.extend([pos_new, pos_old])
    key_segment = jnp.concatenate(key_segs)
    key_position = jnp.concatenate(key_poss)
    allowed = (key_segment[None, :] == segment[:, None]) & (
        key_position[None, :] <= position[:, None]
    )
    allowed = allowed & (
        (position[:, None] - key_position[None, :] < WINDOW) | (key_position[None, :] < SINKS)
    )
    all_keys = jnp.concatenate(blocks, axis=0)
    attended = head_attention(queries, all_keys[:, 0, :], all_keys[:, 1, :], allowed)
    hidden = jax.nn.gelu(lifted + fc1_bias, approximate=True).astype(jnp.bfloat16)
    contract_rows = (((1,), (1,)), ((), ()))
    attn_part = lax.dot_general(
        attended, dense_full_t, contract_rows, preferred_element_type=jnp.float32
    )
    mlp_part = lax.dot_general(
        hidden, fc2_full_t, contract_rows, preferred_element_type=jnp.float32
    )
    branches = attn_part + mlp_part
    summed = lax.psum_scatter(branches, "tensor", scatter_dimension=1, tiled=True)
    layer_out = (tokens.astype(jnp.float32) + summed + dense_bias + fc2_bias).astype(jnp.bfloat16)
    return (layer_out, new_pool)


def solution(mesh):
    placed = (
        P("req", "tensor"),
        P("req"),
        P(),
        P("req", None),
        P("req", None),
        P(),
        P(),
        P("req", None, "tensor"),
        P(None, "tensor"),
        P("tensor", "req"),
        P("tensor"),
        P("req", "tensor"),
        P("tensor"),
        P("tensor", "req"),
        P("tensor"),
        P("req", None, "tensor"),
        P("req", None, "tensor"),
    )
    return jax.shard_map(
        shards,
        mesh=mesh,
        in_specs=placed,
        out_specs=(P("req", "tensor"), P("req", None, "tensor")),
        check_vma=False,
    )
```

```python
import functools

import jax
import jax.numpy as jnp
from jax import lax
from jax.experimental import pallas as pl
from jax.experimental.pallas import tpu as pltpu
from jax.sharding import PartitionSpec as P

HEAD_DIM = 64
ROT = 32
SPAN = 2
SINKS = 4
PAGE = 4
WINDOW = 512
INNER = 4
HOP_US = 3.5
LINK_BYTES_PER_US = 45000.0


MESH_IDS = pl.DeviceIdType.MESH


def ring_gather_kernel(inner, outer, first_block, second_block, first_out, second_out, own_sems,
                       *sems):
    req_index = lax.axis_index("req")
    tensor_index = lax.axis_index("tensor")
    here = (req_index // inner, req_index % inner)
    sizes = (outer, inner)

    def device(shifts):
        at = [lax.rem(here[axis] + shifts[axis] + sizes[axis], sizes[axis]) for axis in range(2)]
        return (at[0] * inner + at[1], tensor_index)

    def index(offsets):
        return tuple(lax.rem(here[axis] + offsets[axis] + sizes[axis], sizes[axis]) for axis in range(2))

    neighbours = (device((0, 1)), device((0, -1)), device((1, 0)), device((-1, 0)))
    barrier = pltpu.get_barrier_semaphore()
    for neighbour in neighbours:
        pl.semaphore_signal(barrier, inc=1, device_id=neighbour, device_id_type=MESH_IDS)
    pl.semaphore_wait(barrier, len(neighbours))

    lanes = []
    for lane, (block_ref, out_ref, first_axis) in enumerate(
        ((first_block, first_out, 1), (second_block, second_out, 0))
    ):
        own = pltpu.make_async_copy(block_ref, out_ref.at[here[0], here[1]], own_sems.at[lane])
        own.start()
        lanes.append((block_ref, out_ref, first_axis, own, sems[4 * lane : 4 * lane + 4]))

    def plans(count):
        return [(0, 1, count // 2), (1, -1, (count - 1) // 2)]

    def offsets_of(axis, offset, other_axis, other_offset):
        pair = [0, 0]
        pair[axis] = offset
        pair[other_axis] = other_offset
        return tuple(pair)

    def copy_of(lane, ring, column, slot, direction, sign, step, arriving):
        block_ref, out_ref, first_axis, _, lane_sems = lanes[lane]
        axis = first_axis if ring == 0 else 1 - first_axis
        piece = -sign * step if arriving else -sign * (step - 1)
        place = offsets_of(axis, piece, 1 - axis, column)
        target = out_ref.at[index(place)]
        if step == 1 and (ring == 0 or column == 0):
            source = block_ref
        else:
            source = target
        first_send, first_recv, second_send, second_recv = lane_sems
        if ring == 0:
            send_sem, recv_sem = first_send.at[direction, step - 1], first_recv.at[direction, step - 1]
        else:
            send_sem = second_send.at[slot, direction, step - 1]
            recv_sem = second_recv.at[slot, direction, step - 1]
        return pltpu.make_async_remote_copy(
            src_ref=source,
            dst_ref=target,
            send_sem=send_sem,
            recv_sem=recv_sem,
            device_id=device(offsets_of(axis, sign, 1 - axis, 0)),
            device_id_type=MESH_IDS,
        )

    tasks = []
    for lane, (block_ref, _, first_axis, _, _) in enumerate(lanes):
        block_bytes = block_ref.shape[0] * block_ref.shape[1] * 2
        duration = HOP_US + block_bytes / LINK_BYTES_PER_US
        first_count = sizes[first_axis]
        second_count = sizes[1 - first_axis]
        columns = [(0, 0.0, None)]
        for direction, sign, steps in plans(first_count):
            ready = 0.0
            for step in range(1, steps + 1):
                need = None if step == 1 else (lane, 0, 0, 0, direction, sign, step - 1)
                tasks.append((ready, len(tasks), (lane, 0, 0, 0, direction, sign, step), need))
                ready += duration
                columns.append((-sign * step, ready, (lane, 0, 0, 0, direction, sign, step)))
        columns.sort(key=lambda entry: entry[1])
        for slot, (column, start, need) in enumerate(columns):
            for direction, sign, steps in plans(second_count):
                ready = start
                for step in range(1, steps + 1):
                    if step > 1:
                        need = (lane, 1, column, slot, direction, sign, step - 1)
                    tasks.append((ready, len(tasks), (lane, 1, column, slot, direction, sign, step), need))
                    ready += duration
                final = (lane, 1, column, slot, direction, sign, steps)
                if steps:
                    tasks.append((float("inf"), len(tasks), None, final))
                need = columns[slot][2]
    tasks.sort(key=lambda entry: (entry[0], entry[1]))
    sent = []
    waited = set()
    for _, _, send, need in tasks:
        if need is not None and need not in waited:
            waited.add(need)
            copy_of(*need, True).wait_recv()
        if send is not None:
            copy = copy_of(*send, False)
            copy.start()
            sent.append(copy)
    for _, _, _, own, _ in lanes:
        own.wait()
    for copy in sent:
        copy.wait_send()


def ring_gather(first_block, second_block, inner, outer):
    semaphores = []
    for first_count, second_count in ((inner, outer), (outer, inner)):
        first_shape = (2, max(1, first_count // 2))
        second_shape = (first_count, 2, max(1, second_count // 2))
        semaphores += [pltpu.SemaphoreType.DMA(first_shape)] * 2
        semaphores += [pltpu.SemaphoreType.DMA(second_shape)] * 2
    gathered = pl.pallas_call(
        functools.partial(ring_gather_kernel, inner, outer),
        out_shape=tuple(
            jax.ShapeDtypeStruct((outer, inner) + block.shape, block.dtype)
            for block in (first_block, second_block)
        ),
        in_specs=[pl.BlockSpec(memory_space=pl.ANY)] * 2,
        out_specs=(pl.BlockSpec(memory_space=pl.ANY),) * 2,
        scratch_shapes=[pltpu.SemaphoreType.DMA((2,))] + semaphores,
        compiler_params=pltpu.CompilerParams(collective_id=0, has_side_effects=True),
    )(first_block, second_block)
    return [part.reshape(outer * inner * part.shape[2], part.shape[3]) for part in gathered]


EPSILON = 1e-05


def from_behind(value, axis, steps):
    count = lax.axis_size(axis)
    leading, last = (max(0, -steps), min(count, count - steps))
    return lax.ppermute(value, axis, [(source, source + steps) for source in range(leading, last)])


def norm_rows(widened, gain, offset_bias):
    average = jnp.mean(widened, axis=-1, keepdims=True)
    centred = widened - average
    spread = jnp.mean(centred * centred, axis=-1, keepdims=True)
    return (centred * lax.rsqrt(spread + EPSILON) * gain + offset_bias).astype(jnp.bfloat16)


def label_rows(places, starts, prefix_lengths):
    labels = jnp.arange(starts.shape[0], dtype=jnp.int32)
    passed = (starts[None, :] <= places[:, None]) & (labels[None, :] >= 1)
    counted = jnp.sum(passed.astype(jnp.int32), axis=1)
    segment = jnp.where(places >= starts[0], 0, counted)
    segment = jnp.where(places < 0, -2, segment)
    onehot = segment[:, None] == labels[None, :]
    earliest = jnp.sum(jnp.where(onehot, starts[None, :], 0), axis=1)
    offset = jnp.sum(jnp.where(onehot, prefix_lengths[None, :], 0), axis=1)
    return (segment, offset + places - earliest)


def prefix_rows(block_id, rows_dev, prefix_count, starts, prefix_lengths):
    labels = jnp.arange(starts.shape[0], dtype=jnp.int32)
    located = (starts >= block_id * rows_dev) & (starts < (block_id + 1) * rows_dev) & (labels >= 1)
    owner_label = jnp.sum(jnp.where(located, labels, 0))
    length = jnp.sum(jnp.where(located, prefix_lengths, 0))
    places = jnp.arange(prefix_count, dtype=jnp.int32)
    usable = jnp.any(located) & (places < length)
    return (jnp.where(usable, owner_label, -2), places)


def rotate_heads(values, position):
    half_rot = ROT // 2
    frequency = 10000.0 ** (-2.0 * jnp.arange(half_rot, dtype=jnp.float32) / ROT)
    angles = position.astype(jnp.float32)[:, None] * frequency[None, :]
    cosine = jnp.cos(angles)[:, None, :]
    sine_vals = jnp.sin(angles)[:, None, :]
    lower = values[..., :half_rot]
    upper = values[..., half_rot:ROT]
    return jnp.concatenate(
        [lower * cosine - upper * sine_vals, upper * cosine + lower * sine_vals, values[..., ROT:]],
        axis=-1,
    )


def head_attention(query_rows, key_rows, value_rows, allowed):
    head_count = query_rows.shape[1] // HEAD_DIM
    score_scale = HEAD_DIM ** (-0.5)

    def one_head(head_index):
        query_cols = lax.dynamic_slice_in_dim(query_rows, head_index * HEAD_DIM, HEAD_DIM, 1)
        key_cols = lax.dynamic_slice_in_dim(key_rows, head_index * HEAD_DIM, HEAD_DIM, 1)
        value_cols = lax.dynamic_slice_in_dim(value_rows, head_index * HEAD_DIM, HEAD_DIM, 1)
        scores = (
            lax.dot_general(
                query_cols, key_cols, (((1,), (1,)), ((), ())), preferred_element_type=jnp.float32
            )
            * score_scale
        )
        masked = jnp.where(allowed, scores, -1e30)
        highest = jnp.max(masked, axis=1, keepdims=True)
        expo = jnp.where(allowed, jnp.exp(masked - highest), 0.0)
        denom = jnp.sum(expo, axis=1, keepdims=True)
        mixed = (
            jnp.dot(expo.astype(jnp.bfloat16), value_cols, preferred_element_type=jnp.float32)
            / denom
        )
        return mixed.astype(jnp.bfloat16)

    outcome = lax.map(one_head, jnp.arange(head_count, dtype=jnp.int32))
    return jnp.transpose(outcome, (1, 0, 2)).reshape(query_rows.shape[0], head_count * HEAD_DIM)


def shards(
    tokens,
    segment_ids,
    prefix_lengths,
    page_owner,
    slot_perm,
    ln_gain,
    ln_bias,
    qkv_weight,
    qkv_bias,
    dense_weight,
    dense_bias,
    fc1_weight,
    fc1_bias,
    fc2_weight,
    fc2_bias,
    prefix_cache,
    cache_pool,
):
    req_count = lax.axis_size("req")
    req_index = lax.axis_index("req")
    tok_rows = tokens.shape[0]
    prefix_count = prefix_cache.shape[0]
    head_cols = qkv_weight.shape[2]
    pool_count = slot_perm.shape[1]
    page_cap = pool_count // req_count
    gathered = lax.all_gather(tokens, "tensor", axis=1, tiled=True)
    normed = norm_rows(gathered.astype(jnp.float32), ln_gain, ln_bias)
    row_ids = jnp.arange(tok_rows, dtype=jnp.int32)
    places = req_index * tok_rows + row_ids
    labels = jnp.arange(prefix_lengths.shape[0], dtype=jnp.int32)
    label_count = labels.shape[0]
    beyond = tok_rows * req_count
    earliest_rows = jnp.min(
        jnp.where(segment_ids[:, None] == labels[None, :], places[:, None], beyond), axis=0
    )
    weight_rows = qkv_weight.shape[0]
    digit_cols = 128
    digits = jnp.concatenate([earliest_rows // 128, earliest_rows % 128]).astype(jnp.bfloat16)
    digits = jnp.pad(digits, (0, weight_rows * digit_cols - 2 * label_count)).reshape(
        weight_rows, digit_cols
    )
    qkv_local = qkv_weight.reshape(weight_rows, 3 * head_cols)
    fc1_cols = fc1_weight.shape[1]
    dense_cols = dense_weight.shape[0]
    fc2_cols = fc2_weight.shape[0]
    first_pack = jnp.concatenate([qkv_local, digits, dense_weight.T], axis=1)
    second_pack = jnp.concatenate([fc1_weight, fc2_weight.T], axis=1)
    first_full, second_full = ring_gather(first_pack, second_pack, INNER, req_count // INNER)
    qkv_full, digits_full, dense_full_t = jnp.split(
        first_full, [3 * head_cols, 3 * head_cols + digit_cols], axis=1
    )
    fc1_full, fc2_full_t = jnp.split(second_full, [fc1_cols], axis=1)
    digit_table = digits_full.reshape(req_count, weight_rows * digit_cols)[:, : 2 * label_count]
    digit_table = digit_table.astype(jnp.int32)
    starts = jnp.min(
        digit_table[:, :label_count] * 128 + digit_table[:, label_count:], axis=0
    )

    def add_rows(portion):
        return jnp.dot(normed, portion, preferred_element_type=jnp.float32)

    projected = add_rows(qkv_full)
    lifted = add_rows(fc1_full)
    projected = (projected + qkv_bias.reshape(1, 3 * head_cols)).reshape(
        tok_rows, 3, head_cols // HEAD_DIM, HEAD_DIM
    )
    segment, position = label_rows(places, starts, prefix_lengths)
    queries = (
        rotate_heads(projected[:, 0], position).astype(jnp.bfloat16).reshape(tok_rows, head_cols)
    )
    new_keys = (
        rotate_heads(projected[:, 1], position).astype(jnp.bfloat16).reshape(tok_rows, head_cols)
    )
    new_values = projected[:, 2].astype(jnp.bfloat16).reshape(tok_rows, head_cols)
    key_value = jnp.stack([new_keys, new_values], axis=1)
    pages_here = tok_rows // PAGE
    page_width = PAGE * 2 * head_cols
    pages = key_value.reshape(pages_here, page_width)
    owners = page_owner[:, 0]
    onehot = (owners[:, None] == jnp.arange(req_count, dtype=jnp.int32)[None, :]).astype(jnp.int32)
    earlier = jnp.cumsum(onehot, axis=0) - onehot
    earlier_count = jnp.sum(earlier * onehot, axis=1)
    target = owners * page_cap + earlier_count
    selecting = (target[None, :] == jnp.arange(pool_count, dtype=jnp.int32)[:, None]).astype(
        jnp.bfloat16
    )
    outgoing = jnp.dot(selecting, pages, preferred_element_type=jnp.float32).astype(jnp.bfloat16)
    filled = jnp.sum(selecting, axis=1)
    flag_cols = 128
    flagged = jnp.concatenate(
        [outgoing, jnp.broadcast_to(filled[:, None], (pool_count, flag_cols)).astype(jnp.bfloat16)],
        axis=1,
    )
    arrived = lax.all_to_all(
        flagged.reshape(req_count, page_cap, page_width + flag_cols),
        "req",
        split_axis=0,
        concat_axis=0,
        tiled=True,
    ).reshape(pool_count, page_width + flag_cols)
    incoming = arrived[:, :page_width]
    incoming_filled = arrived[:, page_width]
    slot_ids = slot_perm[0]
    placing = (slot_ids[None, :] == jnp.arange(pool_count, dtype=jnp.int32)[:, None]) & (
        incoming_filled[None, :] > 0
    )
    written = jnp.dot(
        placing.astype(jnp.bfloat16),
        incoming,
        preferred_element_type=jnp.float32,
    ).astype(jnp.bfloat16)
    written_mask = jnp.any(placing, axis=1)
    pool_pages = cache_pool.reshape(pool_count, page_width)
    new_pool = jnp.where(written_mask[:, None], written, pool_pages).reshape(cache_pool.shape)
    local_keys = jnp.concatenate([key_value, prefix_cache], axis=0)
    blocks = [local_keys]
    for shift_by in range(1, SPAN + 1):
        blocks.append(from_behind(local_keys, "req", shift_by))
    key_segs = []
    key_poss = []
    for step_back in range(SPAN + 1):
        block_id = req_index - step_back
        seg_new, pos_new = label_rows(block_id * tok_rows + row_ids, starts, prefix_lengths)
        seg_old, pos_old = prefix_rows(block_id, tok_rows, prefix_count, starts, prefix_lengths)
        key_segs.extend([seg_new, seg_old])
        key_poss.extend([pos_new, pos_old])
    key_segment = jnp.concatenate(key_segs)
    key_position = jnp.concatenate(key_poss)
    allowed = (key_segment[None, :] == segment[:, None]) & (
        key_position[None, :] <= position[:, None]
    )
    allowed = allowed & (
        (position[:, None] - key_position[None, :] < WINDOW) | (key_position[None, :] < SINKS)
    )
    all_keys = jnp.concatenate(blocks, axis=0)
    attended = head_attention(queries, all_keys[:, 0, :], all_keys[:, 1, :], allowed)
    hidden = jax.nn.gelu(lifted + fc1_bias, approximate=True).astype(jnp.bfloat16)
    contract_rows = (((1,), (1,)), ((), ()))
    attn_part = lax.dot_general(
        attended, dense_full_t, contract_rows, preferred_element_type=jnp.float32
    )
    mlp_part = lax.dot_general(
        hidden, fc2_full_t, contract_rows, preferred_element_type=jnp.float32
    )
    branches = attn_part + mlp_part
    summed = lax.psum_scatter(branches, "tensor", scatter_dimension=1, tiled=True)
    layer_out = (tokens.astype(jnp.float32) + summed + dense_bias + fc2_bias).astype(jnp.bfloat16)
    return (layer_out, new_pool)


def solution(mesh):
    placed = (
        P("req", "tensor"),
        P("req"),
        P(),
        P("req", None),
        P("req", None),
        P(),
        P(),
        P("req", None, "tensor"),
        P(None, "tensor"),
        P("tensor", "req"),
        P("tensor"),
        P("req", "tensor"),
        P("tensor"),
        P("tensor", "req"),
        P("tensor"),
        P("req", None, "tensor"),
        P("req", None, "tensor"),
    )
    return jax.shard_map(
        shards,
        mesh=mesh,
        in_specs=placed,
        out_specs=(P("req", "tensor"), P("req", None, "tensor")),
        check_vma=False,
    )
```

```python
import functools

import jax
import jax.numpy as jnp
from jax import lax
from jax.experimental import pallas as pl
from jax.experimental.pallas import tpu as pltpu
from jax.sharding import PartitionSpec as P

HEAD_DIM = 64
ROT = 32
SPAN = 2
SINKS = 4
PAGE = 4
WINDOW = 512
INNER = 4
HOP_US = 3.5
LINK_BYTES_PER_US = 45000.0


MESH_IDS = pl.DeviceIdType.MESH


def ring_gather_kernel(inner, outer, first_block, second_block, first_out, second_out, own_sems,
                       *sems):
    req_index = lax.axis_index("req")
    tensor_index = lax.axis_index("tensor")
    here = (req_index // inner, req_index % inner)
    sizes = (outer, inner)

    def device(shifts):
        at = [lax.rem(here[axis] + shifts[axis] + sizes[axis], sizes[axis]) for axis in range(2)]
        return (at[0] * inner + at[1], tensor_index)

    def index(offsets):
        return tuple(lax.rem(here[axis] + offsets[axis] + sizes[axis], sizes[axis]) for axis in range(2))

    neighbours = (device((0, 1)), device((0, -1)), device((1, 0)), device((-1, 0)))
    barrier = pltpu.get_barrier_semaphore()
    for neighbour in neighbours:
        pl.semaphore_signal(barrier, inc=1, device_id=neighbour, device_id_type=MESH_IDS)
    pl.semaphore_wait(barrier, len(neighbours))

    lanes = []
    for lane, (block_ref, out_ref, first_axis) in enumerate(
        ((first_block, first_out, 1), (second_block, second_out, 0))
    ):
        own = pltpu.make_async_copy(block_ref, out_ref.at[here[0], here[1]], own_sems.at[lane])
        own.start()
        lanes.append((block_ref, out_ref, first_axis, own, sems[4 * lane : 4 * lane + 4]))

    def plans(count):
        return [(0, 1, count // 2), (1, -1, (count - 1) // 2)]

    def offsets_of(axis, offset, other_axis, other_offset):
        pair = [0, 0]
        pair[axis] = offset
        pair[other_axis] = other_offset
        return tuple(pair)

    def copy_of(lane, ring, column, slot, direction, sign, step, arriving):
        block_ref, out_ref, first_axis, _, lane_sems = lanes[lane]
        axis = first_axis if ring == 0 else 1 - first_axis
        piece = -sign * step if arriving else -sign * (step - 1)
        place = offsets_of(axis, piece, 1 - axis, column)
        target = out_ref.at[index(place)]
        if step == 1 and (ring == 0 or column == 0):
            source = block_ref
        else:
            source = target
        first_send, first_recv, second_send, second_recv = lane_sems
        if ring == 0:
            send_sem, recv_sem = first_send.at[direction, step - 1], first_recv.at[direction, step - 1]
        else:
            send_sem = second_send.at[slot, direction, step - 1]
            recv_sem = second_recv.at[slot, direction, step - 1]
        return pltpu.make_async_remote_copy(
            src_ref=source,
            dst_ref=target,
            send_sem=send_sem,
            recv_sem=recv_sem,
            device_id=device(offsets_of(axis, sign, 1 - axis, 0)),
            device_id_type=MESH_IDS,
        )

    tasks = []
    for lane, (block_ref, _, first_axis, _, _) in enumerate(lanes):
        block_bytes = block_ref.shape[0] * block_ref.shape[1] * 2
        duration = HOP_US + block_bytes / LINK_BYTES_PER_US
        first_count = sizes[first_axis]
        second_count = sizes[1 - first_axis]
        columns = [(0, 0.0, None)]
        for direction, sign, steps in plans(first_count):
            ready = 0.0
            for step in range(1, steps + 1):
                need = None if step == 1 else (lane, 0, 0, 0, direction, sign, step - 1)
                tasks.append((ready, len(tasks), (lane, 0, 0, 0, direction, sign, step), need))
                ready += duration
                columns.append((-sign * step, ready, (lane, 0, 0, 0, direction, sign, step)))
        columns.sort(key=lambda entry: entry[1])
        for slot, (column, start, need) in enumerate(columns):
            for direction, sign, steps in plans(second_count):
                ready = start
                for step in range(1, steps + 1):
                    if step > 1:
                        need = (lane, 1, column, slot, direction, sign, step - 1)
                    tasks.append((ready, len(tasks), (lane, 1, column, slot, direction, sign, step), need))
                    ready += duration
                final = (lane, 1, column, slot, direction, sign, steps)
                if steps:
                    tasks.append((float("inf"), len(tasks), None, final))
                need = columns[slot][2]
    tasks.sort(key=lambda entry: (entry[0], entry[1]))
    sent = []
    waited = set()
    for _, _, send, need in tasks:
        if need is not None and need not in waited:
            waited.add(need)
            copy_of(*need, True).wait_recv()
        if send is not None:
            copy = copy_of(*send, False)
            copy.start()
            sent.append(copy)
    for _, _, _, own, _ in lanes:
        own.wait()
    for copy in sent:
        copy.wait_send()


def ring_gather(first_block, second_block, inner, outer):
    semaphores = []
    for first_count, second_count in ((inner, outer), (outer, inner)):
        first_shape = (2, max(1, first_count // 2))
        second_shape = (first_count, 2, max(1, second_count // 2))
        semaphores += [pltpu.SemaphoreType.DMA(first_shape)] * 2
        semaphores += [pltpu.SemaphoreType.DMA(second_shape)] * 2
    gathered = pl.pallas_call(
        functools.partial(ring_gather_kernel, inner, outer),
        out_shape=tuple(
            jax.ShapeDtypeStruct((outer, inner) + block.shape, block.dtype)
            for block in (first_block, second_block)
        ),
        in_specs=[pl.BlockSpec(memory_space=pl.ANY)] * 2,
        out_specs=(pl.BlockSpec(memory_space=pl.ANY),) * 2,
        scratch_shapes=[pltpu.SemaphoreType.DMA((2,))] + semaphores,
        compiler_params=pltpu.CompilerParams(collective_id=0, has_side_effects=True),
    )(first_block, second_block)
    return [part.reshape(outer * inner * part.shape[2], part.shape[3]) for part in gathered]


EPSILON = 1e-05


def from_behind(value, axis, steps):
    count = lax.axis_size(axis)
    leading, last = (max(0, -steps), min(count, count - steps))
    return lax.ppermute(value, axis, [(source, source + steps) for source in range(leading, last)])


def norm_rows(widened, gain, offset_bias):
    average = jnp.mean(widened, axis=-1, keepdims=True)
    centred = widened - average
    spread = jnp.mean(centred * centred, axis=-1, keepdims=True)
    return (centred * lax.rsqrt(spread + EPSILON) * gain + offset_bias).astype(jnp.bfloat16)


def label_rows(places, starts, prefix_lengths):
    labels = jnp.arange(starts.shape[0], dtype=jnp.int32)
    passed = (starts[None, :] <= places[:, None]) & (labels[None, :] >= 1)
    counted = jnp.sum(passed.astype(jnp.int32), axis=1)
    segment = jnp.where(places >= starts[0], 0, counted)
    segment = jnp.where(places < 0, -2, segment)
    onehot = segment[:, None] == labels[None, :]
    earliest = jnp.sum(jnp.where(onehot, starts[None, :], 0), axis=1)
    offset = jnp.sum(jnp.where(onehot, prefix_lengths[None, :], 0), axis=1)
    return (segment, offset + places - earliest)


def prefix_rows(block_id, rows_dev, prefix_count, starts, prefix_lengths):
    labels = jnp.arange(starts.shape[0], dtype=jnp.int32)
    located = (starts >= block_id * rows_dev) & (starts < (block_id + 1) * rows_dev) & (labels >= 1)
    owner_label = jnp.sum(jnp.where(located, labels, 0))
    length = jnp.sum(jnp.where(located, prefix_lengths, 0))
    places = jnp.arange(prefix_count, dtype=jnp.int32)
    usable = jnp.any(located) & (places < length)
    return (jnp.where(usable, owner_label, -2), places)


def rotate_heads(values, position):
    half_rot = ROT // 2
    frequency = 10000.0 ** (-2.0 * jnp.arange(half_rot, dtype=jnp.float32) / ROT)
    angles = position.astype(jnp.float32)[:, None] * frequency[None, :]
    cosine = jnp.cos(angles)[:, None, :]
    sine_vals = jnp.sin(angles)[:, None, :]
    lower = values[..., :half_rot]
    upper = values[..., half_rot:ROT]
    return jnp.concatenate(
        [lower * cosine - upper * sine_vals, upper * cosine + lower * sine_vals, values[..., ROT:]],
        axis=-1,
    )


def head_attention(query_rows, key_rows, value_rows, allowed):
    head_count = query_rows.shape[1] // HEAD_DIM
    score_scale = HEAD_DIM ** (-0.5)

    def one_head(head_index):
        query_cols = lax.dynamic_slice_in_dim(query_rows, head_index * HEAD_DIM, HEAD_DIM, 1)
        key_cols = lax.dynamic_slice_in_dim(key_rows, head_index * HEAD_DIM, HEAD_DIM, 1)
        value_cols = lax.dynamic_slice_in_dim(value_rows, head_index * HEAD_DIM, HEAD_DIM, 1)
        scores = (
            lax.dot_general(
                query_cols, key_cols, (((1,), (1,)), ((), ())), preferred_element_type=jnp.float32
            )
            * score_scale
        )
        masked = jnp.where(allowed, scores, -1e30)
        highest = jnp.max(masked, axis=1, keepdims=True)
        expo = jnp.where(allowed, jnp.exp(masked - highest), 0.0)
        denom = jnp.sum(expo, axis=1, keepdims=True)
        mixed = (
            jnp.dot(expo.astype(jnp.bfloat16), value_cols, preferred_element_type=jnp.float32)
            / denom
        )
        return mixed.astype(jnp.bfloat16)

    outcome = lax.map(one_head, jnp.arange(head_count, dtype=jnp.int32))
    return jnp.transpose(outcome, (1, 0, 2)).reshape(query_rows.shape[0], head_count * HEAD_DIM)


def shards(
    tokens,
    segment_ids,
    prefix_lengths,
    page_owner,
    slot_perm,
    ln_gain,
    ln_bias,
    qkv_weight,
    qkv_bias,
    dense_weight,
    dense_bias,
    fc1_weight,
    fc1_bias,
    fc2_weight,
    fc2_bias,
    prefix_cache,
    cache_pool,
):
    req_count = lax.axis_size("req")
    req_index = lax.axis_index("req")
    tok_rows = tokens.shape[0]
    prefix_count = prefix_cache.shape[0]
    head_cols = qkv_weight.shape[2]
    pool_count = slot_perm.shape[1]
    page_cap = pool_count // req_count
    gathered = lax.all_gather(tokens, "tensor", axis=1, tiled=True)
    normed = norm_rows(gathered.astype(jnp.float32), ln_gain, ln_bias)
    row_ids = jnp.arange(tok_rows, dtype=jnp.int32)
    places = req_index * tok_rows + row_ids
    labels = jnp.arange(prefix_lengths.shape[0], dtype=jnp.int32)
    label_count = labels.shape[0]
    beyond = tok_rows * req_count
    earliest_rows = jnp.min(
        jnp.where(segment_ids[:, None] == labels[None, :], places[:, None], beyond), axis=0
    )
    weight_rows = qkv_weight.shape[0]
    digit_cols = 128
    owners = page_owner[:, 0]
    owner_count = owners.shape[0]
    digits = jnp.concatenate([earliest_rows // 128, earliest_rows % 128, owners])
    digits = digits.astype(jnp.bfloat16)
    digit_used = 2 * label_count + owner_count
    digits = jnp.pad(digits, (0, weight_rows * digit_cols - digit_used)).reshape(
        weight_rows, digit_cols
    )
    qkv_local = qkv_weight.reshape(weight_rows, 3 * head_cols)
    fc1_cols = fc1_weight.shape[1]
    dense_cols = dense_weight.shape[0]
    fc2_cols = fc2_weight.shape[0]
    first_pack = jnp.concatenate([qkv_local, digits], axis=1)
    second_pack = jnp.concatenate([fc1_weight, dense_weight.T, fc2_weight.T], axis=1)
    first_full, second_full = ring_gather(first_pack, second_pack, INNER, req_count // INNER)
    qkv_full, digits_full = jnp.split(first_full, [3 * head_cols], axis=1)
    fc1_full, dense_full_t, fc2_full_t = jnp.split(
        second_full, [fc1_cols, fc1_cols + dense_cols], axis=1
    )
    digit_table = digits_full.reshape(req_count, weight_rows * digit_cols)[:, :digit_used]
    digit_table = digit_table.astype(jnp.int32)
    owner_table = digit_table[:, 2 * label_count :]
    starts = jnp.min(
        digit_table[:, :label_count] * 128 + digit_table[:, label_count : 2 * label_count], axis=0
    )

    def add_rows(portion):
        return jnp.dot(normed, portion, preferred_element_type=jnp.float32)

    projected = add_rows(qkv_full)
    lifted = add_rows(fc1_full)
    projected = (projected + qkv_bias.reshape(1, 3 * head_cols)).reshape(
        tok_rows, 3, head_cols // HEAD_DIM, HEAD_DIM
    )
    segment, position = label_rows(places, starts, prefix_lengths)
    queries = (
        rotate_heads(projected[:, 0], position).astype(jnp.bfloat16).reshape(tok_rows, head_cols)
    )
    new_keys = (
        rotate_heads(projected[:, 1], position).astype(jnp.bfloat16).reshape(tok_rows, head_cols)
    )
    new_values = projected[:, 2].astype(jnp.bfloat16).reshape(tok_rows, head_cols)
    key_value = jnp.stack([new_keys, new_values], axis=1)
    pages_here = tok_rows // PAGE
    page_width = PAGE * 2 * head_cols
    pages = key_value.reshape(pages_here, page_width)
    onehot = (owners[:, None] == jnp.arange(req_count, dtype=jnp.int32)[None, :]).astype(jnp.int32)
    earlier = jnp.cumsum(onehot, axis=0) - onehot
    earlier_count = jnp.sum(earlier * onehot, axis=1)
    target = owners * page_cap + earlier_count
    selecting = (target[None, :] == jnp.arange(pool_count, dtype=jnp.int32)[:, None]).astype(
        jnp.bfloat16
    )
    outgoing = jnp.dot(selecting, pages, preferred_element_type=jnp.float32).astype(jnp.bfloat16)
    incoming = lax.all_to_all(
        outgoing.reshape(req_count, page_cap, page_width), "req", split_axis=0, concat_axis=0, tiled=True
    ).reshape(pool_count, page_width)
    mine = jnp.sum((owner_table == req_index).astype(jnp.int32), axis=1)
    incoming_filled = (
        mine[:, None] > jnp.arange(page_cap, dtype=jnp.int32)[None, :]
    ).reshape(pool_count)
    slot_ids = slot_perm[0]
    placing = (slot_ids[None, :] == jnp.arange(pool_count, dtype=jnp.int32)[:, None]) & (
        incoming_filled[None, :] > 0
    )
    written = jnp.dot(
        placing.astype(jnp.bfloat16),
        incoming,
        preferred_element_type=jnp.float32,
    ).astype(jnp.bfloat16)
    written_mask = jnp.any(placing, axis=1)
    pool_pages = cache_pool.reshape(pool_count, page_width)
    new_pool = jnp.where(written_mask[:, None], written, pool_pages).reshape(cache_pool.shape)
    local_keys = jnp.concatenate([key_value, prefix_cache], axis=0)
    blocks = [local_keys]
    for shift_by in range(1, SPAN + 1):
        blocks.append(from_behind(local_keys, "req", shift_by))
    key_segs = []
    key_poss = []
    for step_back in range(SPAN + 1):
        block_id = req_index - step_back
        seg_new, pos_new = label_rows(block_id * tok_rows + row_ids, starts, prefix_lengths)
        seg_old, pos_old = prefix_rows(block_id, tok_rows, prefix_count, starts, prefix_lengths)
        key_segs.extend([seg_new, seg_old])
        key_poss.extend([pos_new, pos_old])
    key_segment = jnp.concatenate(key_segs)
    key_position = jnp.concatenate(key_poss)
    allowed = (key_segment[None, :] == segment[:, None]) & (
        key_position[None, :] <= position[:, None]
    )
    allowed = allowed & (
        (position[:, None] - key_position[None, :] < WINDOW) | (key_position[None, :] < SINKS)
    )
    all_keys = jnp.concatenate(blocks, axis=0)
    attended = head_attention(queries, all_keys[:, 0, :], all_keys[:, 1, :], allowed)
    hidden = jax.nn.gelu(lifted + fc1_bias, approximate=True).astype(jnp.bfloat16)
    contract_rows = (((1,), (1,)), ((), ()))
    attn_part = lax.dot_general(
        attended, dense_full_t, contract_rows, preferred_element_type=jnp.float32
    )
    mlp_part = lax.dot_general(
        hidden, fc2_full_t, contract_rows, preferred_element_type=jnp.float32
    )
    branches = attn_part + mlp_part
    summed = lax.psum_scatter(branches, "tensor", scatter_dimension=1, tiled=True)
    layer_out = (tokens.astype(jnp.float32) + summed + dense_bias + fc2_bias).astype(jnp.bfloat16)
    return (layer_out, new_pool)


def solution(mesh):
    placed = (
        P("req", "tensor"),
        P("req"),
        P(),
        P("req", None),
        P("req", None),
        P(),
        P(),
        P("req", None, "tensor"),
        P(None, "tensor"),
        P("tensor", "req"),
        P("tensor"),
        P("req", "tensor"),
        P("tensor"),
        P("tensor", "req"),
        P("tensor"),
        P("req", None, "tensor"),
        P("req", None, "tensor"),
    )
    return jax.shard_map(
        shards,
        mesh=mesh,
        in_specs=placed,
        out_specs=(P("req", "tensor"), P("req", None, "tensor")),
        check_vma=False,
    )
```

```python
import functools

import jax
import jax.numpy as jnp
from jax import lax
from jax.experimental import pallas as pl
from jax.experimental.pallas import tpu as pltpu
from jax.sharding import PartitionSpec as P

HEAD_DIM = 64
ROT = 32
SPAN = 2
SINKS = 4
PAGE = 4
WINDOW = 512
INNER = 4
HOP_US = 3.5
LINK_BYTES_PER_US = 45000.0


MESH_IDS = pl.DeviceIdType.MESH


def ring_gather_kernel(inner, outer, first_block, second_block, first_out, second_out, own_sems,
                       *sems):
    req_index = lax.axis_index("req")
    tensor_index = lax.axis_index("tensor")
    here = (req_index // inner, req_index % inner)
    sizes = (outer, inner)

    def device(shifts):
        at = [lax.rem(here[axis] + shifts[axis] + sizes[axis], sizes[axis]) for axis in range(2)]
        return (at[0] * inner + at[1], tensor_index)

    def index(offsets):
        return tuple(lax.rem(here[axis] + offsets[axis] + sizes[axis], sizes[axis]) for axis in range(2))

    neighbours = (device((0, 1)), device((0, -1)), device((1, 0)), device((-1, 0)))
    barrier = pltpu.get_barrier_semaphore()
    for neighbour in neighbours:
        pl.semaphore_signal(barrier, inc=1, device_id=neighbour, device_id_type=MESH_IDS)
    pl.semaphore_wait(barrier, len(neighbours))

    lanes = []
    for lane, (block_ref, out_ref, first_axis) in enumerate(
        ((first_block, first_out, 1), (second_block, second_out, 0))
    ):
        own = pltpu.make_async_copy(block_ref, out_ref.at[here[0], here[1]], own_sems.at[lane])
        own.start()
        lanes.append((block_ref, out_ref, first_axis, own, sems[4 * lane : 4 * lane + 4]))

    def plans(count):
        return [(0, 1, count // 2), (1, -1, (count - 1) // 2)]

    def offsets_of(axis, offset, other_axis, other_offset):
        pair = [0, 0]
        pair[axis] = offset
        pair[other_axis] = other_offset
        return tuple(pair)

    def copy_of(lane, ring, column, slot, direction, sign, step, arriving):
        block_ref, out_ref, first_axis, _, lane_sems = lanes[lane]
        axis = first_axis if ring == 0 else 1 - first_axis
        piece = -sign * step if arriving else -sign * (step - 1)
        place = offsets_of(axis, piece, 1 - axis, column)
        target = out_ref.at[index(place)]
        if step == 1 and (ring == 0 or column == 0):
            source = block_ref
        else:
            source = target
        first_send, first_recv, second_send, second_recv = lane_sems
        if ring == 0:
            send_sem, recv_sem = first_send.at[direction, step - 1], first_recv.at[direction, step - 1]
        else:
            send_sem = second_send.at[slot, direction, step - 1]
            recv_sem = second_recv.at[slot, direction, step - 1]
        return pltpu.make_async_remote_copy(
            src_ref=source,
            dst_ref=target,
            send_sem=send_sem,
            recv_sem=recv_sem,
            device_id=device(offsets_of(axis, sign, 1 - axis, 0)),
            device_id_type=MESH_IDS,
        )

    tasks = []
    for lane, (block_ref, _, first_axis, _, _) in enumerate(lanes):
        block_bytes = block_ref.shape[0] * block_ref.shape[1] * 2
        duration = HOP_US + block_bytes / LINK_BYTES_PER_US
        first_count = sizes[first_axis]
        second_count = sizes[1 - first_axis]
        columns = [(0, 0.0, None)]
        for direction, sign, steps in plans(first_count):
            ready = 0.0
            for step in range(1, steps + 1):
                need = None if step == 1 else (lane, 0, 0, 0, direction, sign, step - 1)
                tasks.append((ready, len(tasks), (lane, 0, 0, 0, direction, sign, step), need))
                ready += duration
                columns.append((-sign * step, ready, (lane, 0, 0, 0, direction, sign, step)))
        columns.sort(key=lambda entry: entry[1])
        for slot, (column, start, need) in enumerate(columns):
            for direction, sign, steps in plans(second_count):
                ready = start
                for step in range(1, steps + 1):
                    if step > 1:
                        need = (lane, 1, column, slot, direction, sign, step - 1)
                    tasks.append((ready, len(tasks), (lane, 1, column, slot, direction, sign, step), need))
                    ready += duration
                final = (lane, 1, column, slot, direction, sign, steps)
                if steps:
                    tasks.append((float("inf"), len(tasks), None, final))
                need = columns[slot][2]
    tasks.sort(key=lambda entry: (entry[0], entry[1]))
    sent = []
    waited = set()
    for _, _, send, need in tasks:
        if need is not None and need not in waited:
            waited.add(need)
            copy_of(*need, True).wait_recv()
        if send is not None:
            copy = copy_of(*send, False)
            copy.start()
            sent.append(copy)
    for _, _, _, own, _ in lanes:
        own.wait()
    for copy in sent:
        copy.wait_send()


def ring_gather(first_block, second_block, inner, outer):
    semaphores = []
    for first_count, second_count in ((inner, outer), (outer, inner)):
        first_shape = (2, max(1, first_count // 2))
        second_shape = (first_count, 2, max(1, second_count // 2))
        semaphores += [pltpu.SemaphoreType.DMA(first_shape)] * 2
        semaphores += [pltpu.SemaphoreType.DMA(second_shape)] * 2
    gathered = pl.pallas_call(
        functools.partial(ring_gather_kernel, inner, outer),
        out_shape=tuple(
            jax.ShapeDtypeStruct((outer, inner) + block.shape, block.dtype)
            for block in (first_block, second_block)
        ),
        in_specs=[pl.BlockSpec(memory_space=pl.ANY)] * 2,
        out_specs=(pl.BlockSpec(memory_space=pl.ANY),) * 2,
        scratch_shapes=[pltpu.SemaphoreType.DMA((2,))] + semaphores,
        compiler_params=pltpu.CompilerParams(collective_id=0, has_side_effects=True),
    )(first_block, second_block)
    return [part.reshape(outer * inner * part.shape[2], part.shape[3]) for part in gathered]


EPSILON = 1e-05


def from_behind(value, axis, steps):
    count = lax.axis_size(axis)
    leading, last = (max(0, -steps), min(count, count - steps))
    return lax.ppermute(value, axis, [(source, source + steps) for source in range(leading, last)])


def norm_rows(widened, gain, offset_bias):
    average = jnp.mean(widened, axis=-1, keepdims=True)
    centred = widened - average
    spread = jnp.mean(centred * centred, axis=-1, keepdims=True)
    return (centred * lax.rsqrt(spread + EPSILON) * gain + offset_bias).astype(jnp.bfloat16)


def label_rows(places, starts, prefix_lengths):
    labels = jnp.arange(starts.shape[0], dtype=jnp.int32)
    passed = (starts[None, :] <= places[:, None]) & (labels[None, :] >= 1)
    counted = jnp.sum(passed.astype(jnp.int32), axis=1)
    segment = jnp.where(places >= starts[0], 0, counted)
    segment = jnp.where(places < 0, -2, segment)
    onehot = segment[:, None] == labels[None, :]
    earliest = jnp.sum(jnp.where(onehot, starts[None, :], 0), axis=1)
    offset = jnp.sum(jnp.where(onehot, prefix_lengths[None, :], 0), axis=1)
    return (segment, offset + places - earliest)


def prefix_rows(block_id, rows_dev, prefix_count, starts, prefix_lengths):
    labels = jnp.arange(starts.shape[0], dtype=jnp.int32)
    located = (starts >= block_id * rows_dev) & (starts < (block_id + 1) * rows_dev) & (labels >= 1)
    owner_label = jnp.sum(jnp.where(located, labels, 0))
    length = jnp.sum(jnp.where(located, prefix_lengths, 0))
    places = jnp.arange(prefix_count, dtype=jnp.int32)
    usable = jnp.any(located) & (places < length)
    return (jnp.where(usable, owner_label, -2), places)


def rotate_heads(values, position):
    half_rot = ROT // 2
    frequency = 10000.0 ** (-2.0 * jnp.arange(half_rot, dtype=jnp.float32) / ROT)
    angles = position.astype(jnp.float32)[:, None] * frequency[None, :]
    cosine = jnp.cos(angles)[:, None, :]
    sine_vals = jnp.sin(angles)[:, None, :]
    lower = values[..., :half_rot]
    upper = values[..., half_rot:ROT]
    return jnp.concatenate(
        [lower * cosine - upper * sine_vals, upper * cosine + lower * sine_vals, values[..., ROT:]],
        axis=-1,
    )


def head_attention(query_rows, key_rows, value_rows, allowed):
    head_count = query_rows.shape[1] // HEAD_DIM
    score_scale = HEAD_DIM ** (-0.5)

    def one_head(head_index):
        query_cols = lax.dynamic_slice_in_dim(query_rows, head_index * HEAD_DIM, HEAD_DIM, 1)
        key_cols = lax.dynamic_slice_in_dim(key_rows, head_index * HEAD_DIM, HEAD_DIM, 1)
        value_cols = lax.dynamic_slice_in_dim(value_rows, head_index * HEAD_DIM, HEAD_DIM, 1)
        scores = (
            lax.dot_general(
                query_cols, key_cols, (((1,), (1,)), ((), ())), preferred_element_type=jnp.float32
            )
            * score_scale
        )
        masked = jnp.where(allowed, scores, -1e30)
        highest = jnp.max(masked, axis=1, keepdims=True)
        expo = jnp.where(allowed, jnp.exp(masked - highest), 0.0)
        denom = jnp.sum(expo, axis=1, keepdims=True)
        mixed = (
            jnp.dot(expo.astype(jnp.bfloat16), value_cols, preferred_element_type=jnp.float32)
            / denom
        )
        return mixed.astype(jnp.bfloat16)

    outcome = lax.map(one_head, jnp.arange(head_count, dtype=jnp.int32))
    return jnp.transpose(outcome, (1, 0, 2)).reshape(query_rows.shape[0], head_count * HEAD_DIM)


def shards(
    tokens,
    segment_ids,
    prefix_lengths,
    page_owner,
    slot_perm,
    ln_gain,
    ln_bias,
    qkv_weight,
    qkv_bias,
    dense_weight,
    dense_bias,
    fc1_weight,
    fc1_bias,
    fc2_weight,
    fc2_bias,
    prefix_cache,
    cache_pool,
):
    req_count = lax.axis_size("req")
    req_index = lax.axis_index("req")
    tok_rows = tokens.shape[0]
    prefix_count = prefix_cache.shape[0]
    head_cols = qkv_weight.shape[2]
    pool_count = slot_perm.shape[1]
    page_cap = pool_count // req_count
    gathered = lax.all_gather(tokens, "tensor", axis=1, tiled=True)
    normed = norm_rows(gathered.astype(jnp.float32), ln_gain, ln_bias)
    row_ids = jnp.arange(tok_rows, dtype=jnp.int32)
    places = req_index * tok_rows + row_ids
    labels = jnp.arange(prefix_lengths.shape[0], dtype=jnp.int32)
    label_count = labels.shape[0]
    beyond = tok_rows * req_count
    earliest_rows = jnp.min(
        jnp.where(segment_ids[:, None] == labels[None, :], places[:, None], beyond), axis=0
    )
    weight_rows = qkv_weight.shape[0]
    digit_cols = 128
    owners = page_owner[:, 0]
    owner_count = owners.shape[0]
    digits = jnp.concatenate([earliest_rows // 128, earliest_rows % 128, owners])
    digits = digits.astype(jnp.bfloat16)
    digit_used = 2 * label_count + owner_count
    digits = jnp.pad(digits, (0, weight_rows * digit_cols - digit_used)).reshape(
        weight_rows, digit_cols
    )
    qkv_local = qkv_weight.reshape(weight_rows, 3 * head_cols)
    fc1_cols = fc1_weight.shape[1]
    dense_cols = dense_weight.shape[0]
    fc2_cols = fc2_weight.shape[0]
    first_pack = jnp.concatenate([qkv_local, digits], axis=1)
    second_pack = jnp.concatenate([fc1_weight, dense_weight.T, fc2_weight.T], axis=1)
    first_full, second_full = ring_gather(first_pack, second_pack, INNER, req_count // INNER)
    qkv_full, digits_full = jnp.split(first_full, [3 * head_cols], axis=1)
    fc1_full, dense_full_t, fc2_full_t = jnp.split(
        second_full, [fc1_cols, fc1_cols + dense_cols], axis=1
    )
    digit_table = digits_full.reshape(req_count, weight_rows * digit_cols)[:, :digit_used]
    digit_table = digit_table.astype(jnp.int32)
    owner_table = digit_table[:, 2 * label_count :]
    starts = jnp.min(
        digit_table[:, :label_count] * 128 + digit_table[:, label_count : 2 * label_count], axis=0
    )

    def add_rows(portion):
        return jnp.dot(normed, portion, preferred_element_type=jnp.float32)

    projected = add_rows(qkv_full)
    lifted = add_rows(fc1_full)
    projected = (projected + qkv_bias.reshape(1, 3 * head_cols)).reshape(
        tok_rows, 3, head_cols // HEAD_DIM, HEAD_DIM
    )
    segment, position = label_rows(places, starts, prefix_lengths)
    queries = (
        rotate_heads(projected[:, 0], position).astype(jnp.bfloat16).reshape(tok_rows, head_cols)
    )
    new_keys = (
        rotate_heads(projected[:, 1], position).astype(jnp.bfloat16).reshape(tok_rows, head_cols)
    )
    new_values = projected[:, 2].astype(jnp.bfloat16).reshape(tok_rows, head_cols)
    key_value = jnp.stack([new_keys, new_values], axis=1)
    pages_here = tok_rows // PAGE
    page_width = PAGE * 2 * head_cols
    pages = key_value.reshape(pages_here, page_width)
    onehot = (owners[:, None] == jnp.arange(req_count, dtype=jnp.int32)[None, :]).astype(jnp.int32)
    earlier = jnp.cumsum(onehot, axis=0) - onehot
    earlier_count = jnp.sum(earlier * onehot, axis=1)
    target = owners * page_cap + earlier_count
    selecting = (target[None, :] == jnp.arange(pool_count, dtype=jnp.int32)[:, None]).astype(
        jnp.bfloat16
    )
    outgoing = jnp.dot(selecting, pages, preferred_element_type=jnp.float32).astype(jnp.bfloat16)
    incoming = lax.all_to_all(
        outgoing.reshape(req_count, page_cap, page_width), "req", split_axis=0, concat_axis=0, tiled=True
    ).reshape(pool_count, page_width)
    mine = jnp.sum((owner_table == req_index).astype(jnp.int32), axis=1)
    incoming_filled = (
        mine[:, None] > jnp.arange(page_cap, dtype=jnp.int32)[None, :]
    ).reshape(pool_count)
    slot_ids = slot_perm[0]
    placing = (slot_ids[None, :] == jnp.arange(pool_count, dtype=jnp.int32)[:, None]) & (
        incoming_filled[None, :] > 0
    )
    written = jnp.dot(
        placing.astype(jnp.bfloat16),
        incoming,
        preferred_element_type=jnp.float32,
    ).astype(jnp.bfloat16)
    written_mask = jnp.any(placing, axis=1)
    pool_pages = cache_pool.reshape(pool_count, page_width)
    new_pool = jnp.where(written_mask[:, None], written, pool_pages).reshape(cache_pool.shape)
    local_keys = jnp.concatenate([key_value, prefix_cache], axis=0)
    blocks = [local_keys]
    for shift_by in range(1, SPAN + 1):
        blocks.append(
            jnp.concatenate(
                [
                    from_behind(key_value, "req", shift_by),
                    from_behind(prefix_cache, "req", shift_by),
                ],
                axis=0,
            )
        )
    key_segs = []
    key_poss = []
    for step_back in range(SPAN + 1):
        block_id = req_index - step_back
        seg_new, pos_new = label_rows(block_id * tok_rows + row_ids, starts, prefix_lengths)
        seg_old, pos_old = prefix_rows(block_id, tok_rows, prefix_count, starts, prefix_lengths)
        key_segs.extend([seg_new, seg_old])
        key_poss.extend([pos_new, pos_old])
    key_segment = jnp.concatenate(key_segs)
    key_position = jnp.concatenate(key_poss)
    allowed = (key_segment[None, :] == segment[:, None]) & (
        key_position[None, :] <= position[:, None]
    )
    allowed = allowed & (
        (position[:, None] - key_position[None, :] < WINDOW) | (key_position[None, :] < SINKS)
    )
    all_keys = jnp.concatenate(blocks, axis=0)
    attended = head_attention(queries, all_keys[:, 0, :], all_keys[:, 1, :], allowed)
    hidden = jax.nn.gelu(lifted + fc1_bias, approximate=True).astype(jnp.bfloat16)
    contract_rows = (((1,), (1,)), ((), ()))
    attn_part = lax.dot_general(
        attended, dense_full_t, contract_rows, preferred_element_type=jnp.float32
    )
    mlp_part = lax.dot_general(
        hidden, fc2_full_t, contract_rows, preferred_element_type=jnp.float32
    )
    branches = attn_part + mlp_part
    summed = lax.psum_scatter(branches, "tensor", scatter_dimension=1, tiled=True)
    layer_out = (tokens.astype(jnp.float32) + summed + dense_bias + fc2_bias).astype(jnp.bfloat16)
    return (layer_out, new_pool)


def solution(mesh):
    placed = (
        P("req", "tensor"),
        P("req"),
        P(),
        P("req", None),
        P("req", None),
        P(),
        P(),
        P("req", None, "tensor"),
        P(None, "tensor"),
        P("tensor", "req"),
        P("tensor"),
        P("req", "tensor"),
        P("tensor"),
        P("tensor", "req"),
        P("tensor"),
        P("req", None, "tensor"),
        P("req", None, "tensor"),
    )
    return jax.shard_map(
        shards,
        mesh=mesh,
        in_specs=placed,
        out_specs=(P("req", "tensor"), P("req", None, "tensor")),
        check_vma=False,
    )
```

```python
import functools

import jax
import jax.numpy as jnp
from jax import lax
from jax.experimental import pallas as pl
from jax.experimental.pallas import tpu as pltpu
from jax.sharding import PartitionSpec as P

HEAD_DIM = 64
ROT = 32
SPAN = 2
SINKS = 4
PAGE = 4
WINDOW = 512
INNER = 4
HOP_US = 1.5
LINK_BYTES_PER_US = 45000.0


MESH_IDS = pl.DeviceIdType.MESH


def ring_gather_kernel(inner, outer, first_block, second_block, first_out, second_out, own_sems,
                       *sems):
    req_index = lax.axis_index("req")
    tensor_index = lax.axis_index("tensor")
    here = (req_index // inner, req_index % inner)
    sizes = (outer, inner)

    def device(shifts):
        at = [lax.rem(here[axis] + shifts[axis] + sizes[axis], sizes[axis]) for axis in range(2)]
        return (at[0] * inner + at[1], tensor_index)

    def index(offsets):
        return tuple(lax.rem(here[axis] + offsets[axis] + sizes[axis], sizes[axis]) for axis in range(2))

    neighbours = (device((0, 1)), device((0, -1)), device((1, 0)), device((-1, 0)))
    barrier = pltpu.get_barrier_semaphore()
    for neighbour in neighbours:
        pl.semaphore_signal(barrier, inc=1, device_id=neighbour, device_id_type=MESH_IDS)
    pl.semaphore_wait(barrier, len(neighbours))

    lanes = []
    for lane, (block_ref, out_ref, first_axis) in enumerate(
        ((first_block, first_out, 1), (second_block, second_out, 0))
    ):
        own = pltpu.make_async_copy(block_ref, out_ref.at[here[0], here[1]], own_sems.at[lane])
        own.start()
        lanes.append((block_ref, out_ref, first_axis, own, sems[4 * lane : 4 * lane + 4]))

    def plans(count):
        return [(0, 1, count // 2), (1, -1, (count - 1) // 2)]

    def offsets_of(axis, offset, other_axis, other_offset):
        pair = [0, 0]
        pair[axis] = offset
        pair[other_axis] = other_offset
        return tuple(pair)

    def copy_of(lane, ring, column, slot, direction, sign, step, arriving):
        block_ref, out_ref, first_axis, _, lane_sems = lanes[lane]
        axis = first_axis if ring == 0 else 1 - first_axis
        piece = -sign * step if arriving else -sign * (step - 1)
        place = offsets_of(axis, piece, 1 - axis, column)
        target = out_ref.at[index(place)]
        if step == 1 and (ring == 0 or column == 0):
            source = block_ref
        else:
            source = target
        first_send, first_recv, second_send, second_recv = lane_sems
        if ring == 0:
            send_sem, recv_sem = first_send.at[direction, step - 1], first_recv.at[direction, step - 1]
        else:
            send_sem = second_send.at[slot, direction, step - 1]
            recv_sem = second_recv.at[slot, direction, step - 1]
        return pltpu.make_async_remote_copy(
            src_ref=source,
            dst_ref=target,
            send_sem=send_sem,
            recv_sem=recv_sem,
            device_id=device(offsets_of(axis, sign, 1 - axis, 0)),
            device_id_type=MESH_IDS,
        )

    tasks = []
    for lane, (block_ref, _, first_axis, _, _) in enumerate(lanes):
        block_bytes = block_ref.shape[0] * block_ref.shape[1] * 2
        duration = HOP_US + block_bytes / LINK_BYTES_PER_US
        first_count = sizes[first_axis]
        second_count = sizes[1 - first_axis]
        columns = [(0, 0.0, None)]
        for direction, sign, steps in plans(first_count):
            ready = 0.0
            for step in range(1, steps + 1):
                need = None if step == 1 else (lane, 0, 0, 0, direction, sign, step - 1)
                tasks.append((ready, len(tasks), (lane, 0, 0, 0, direction, sign, step), need))
                ready += duration
                columns.append((-sign * step, ready, (lane, 0, 0, 0, direction, sign, step)))
        columns.sort(key=lambda entry: entry[1])
        for slot, (column, start, need) in enumerate(columns):
            for direction, sign, steps in plans(second_count):
                ready = start
                for step in range(1, steps + 1):
                    if step > 1:
                        need = (lane, 1, column, slot, direction, sign, step - 1)
                    tasks.append((ready, len(tasks), (lane, 1, column, slot, direction, sign, step), need))
                    ready += duration
                final = (lane, 1, column, slot, direction, sign, steps)
                if steps:
                    tasks.append((float("inf"), len(tasks), None, final))
                need = columns[slot][2]
    tasks.sort(key=lambda entry: (entry[0], entry[1]))
    sent = []
    waited = set()
    for _, _, send, need in tasks:
        if need is not None and need not in waited:
            waited.add(need)
            copy_of(*need, True).wait_recv()
        if send is not None:
            copy = copy_of(*send, False)
            copy.start()
            sent.append(copy)
    for _, _, _, own, _ in lanes:
        own.wait()
    for copy in sent:
        copy.wait_send()


def ring_gather(first_block, second_block, inner, outer):
    semaphores = []
    for first_count, second_count in ((inner, outer), (outer, inner)):
        first_shape = (2, max(1, first_count // 2))
        second_shape = (first_count, 2, max(1, second_count // 2))
        semaphores += [pltpu.SemaphoreType.DMA(first_shape)] * 2
        semaphores += [pltpu.SemaphoreType.DMA(second_shape)] * 2
    gathered = pl.pallas_call(
        functools.partial(ring_gather_kernel, inner, outer),
        out_shape=tuple(
            jax.ShapeDtypeStruct((outer, inner) + block.shape, block.dtype)
            for block in (first_block, second_block)
        ),
        in_specs=[pl.BlockSpec(memory_space=pl.ANY)] * 2,
        out_specs=(pl.BlockSpec(memory_space=pl.ANY),) * 2,
        scratch_shapes=[pltpu.SemaphoreType.DMA((2,))] + semaphores,
        compiler_params=pltpu.CompilerParams(collective_id=0, has_side_effects=True),
    )(first_block, second_block)
    return [part.reshape(outer * inner * part.shape[2], part.shape[3]) for part in gathered]


EPSILON = 1e-05


def from_behind(value, axis, steps):
    count = lax.axis_size(axis)
    leading, last = (max(0, -steps), min(count, count - steps))
    return lax.ppermute(value, axis, [(source, source + steps) for source in range(leading, last)])


def norm_rows(widened, gain, offset_bias):
    average = jnp.mean(widened, axis=-1, keepdims=True)
    centred = widened - average
    spread = jnp.mean(centred * centred, axis=-1, keepdims=True)
    return (centred * lax.rsqrt(spread + EPSILON) * gain + offset_bias).astype(jnp.bfloat16)


def label_rows(places, starts, prefix_lengths):
    labels = jnp.arange(starts.shape[0], dtype=jnp.int32)
    passed = (starts[None, :] <= places[:, None]) & (labels[None, :] >= 1)
    counted = jnp.sum(passed.astype(jnp.int32), axis=1)
    segment = jnp.where(places >= starts[0], 0, counted)
    segment = jnp.where(places < 0, -2, segment)
    onehot = segment[:, None] == labels[None, :]
    earliest = jnp.sum(jnp.where(onehot, starts[None, :], 0), axis=1)
    offset = jnp.sum(jnp.where(onehot, prefix_lengths[None, :], 0), axis=1)
    return (segment, offset + places - earliest)


def prefix_rows(block_id, rows_dev, prefix_count, starts, prefix_lengths):
    labels = jnp.arange(starts.shape[0], dtype=jnp.int32)
    located = (starts >= block_id * rows_dev) & (starts < (block_id + 1) * rows_dev) & (labels >= 1)
    owner_label = jnp.sum(jnp.where(located, labels, 0))
    length = jnp.sum(jnp.where(located, prefix_lengths, 0))
    places = jnp.arange(prefix_count, dtype=jnp.int32)
    usable = jnp.any(located) & (places < length)
    return (jnp.where(usable, owner_label, -2), places)


def rotate_heads(values, position):
    half_rot = ROT // 2
    frequency = 10000.0 ** (-2.0 * jnp.arange(half_rot, dtype=jnp.float32) / ROT)
    angles = position.astype(jnp.float32)[:, None] * frequency[None, :]
    cosine = jnp.cos(angles)[:, None, :]
    sine_vals = jnp.sin(angles)[:, None, :]
    lower = values[..., :half_rot]
    upper = values[..., half_rot:ROT]
    return jnp.concatenate(
        [lower * cosine - upper * sine_vals, upper * cosine + lower * sine_vals, values[..., ROT:]],
        axis=-1,
    )


def head_attention(query_rows, key_rows, value_rows, allowed):
    head_count = query_rows.shape[1] // HEAD_DIM
    score_scale = HEAD_DIM ** (-0.5)

    def one_head(head_index):
        query_cols = lax.dynamic_slice_in_dim(query_rows, head_index * HEAD_DIM, HEAD_DIM, 1)
        key_cols = lax.dynamic_slice_in_dim(key_rows, head_index * HEAD_DIM, HEAD_DIM, 1)
        value_cols = lax.dynamic_slice_in_dim(value_rows, head_index * HEAD_DIM, HEAD_DIM, 1)
        scores = (
            lax.dot_general(
                query_cols, key_cols, (((1,), (1,)), ((), ())), preferred_element_type=jnp.float32
            )
            * score_scale
        )
        masked = jnp.where(allowed, scores, -1e30)
        highest = jnp.max(masked, axis=1, keepdims=True)
        expo = jnp.where(allowed, jnp.exp(masked - highest), 0.0)
        denom = jnp.sum(expo, axis=1, keepdims=True)
        mixed = (
            jnp.dot(expo.astype(jnp.bfloat16), value_cols, preferred_element_type=jnp.float32)
            / denom
        )
        return mixed.astype(jnp.bfloat16)

    outcome = lax.map(one_head, jnp.arange(head_count, dtype=jnp.int32))
    return jnp.transpose(outcome, (1, 0, 2)).reshape(query_rows.shape[0], head_count * HEAD_DIM)


def shards(
    tokens,
    segment_ids,
    prefix_lengths,
    page_owner,
    slot_perm,
    ln_gain,
    ln_bias,
    qkv_weight,
    qkv_bias,
    dense_weight,
    dense_bias,
    fc1_weight,
    fc1_bias,
    fc2_weight,
    fc2_bias,
    prefix_cache,
    cache_pool,
):
    req_count = lax.axis_size("req")
    req_index = lax.axis_index("req")
    tok_rows = tokens.shape[0]
    prefix_count = prefix_cache.shape[0]
    head_cols = qkv_weight.shape[2]
    pool_count = slot_perm.shape[1]
    page_cap = pool_count // req_count
    gathered = lax.all_gather(tokens, "tensor", axis=1, tiled=True)
    normed = norm_rows(gathered.astype(jnp.float32), ln_gain, ln_bias)
    row_ids = jnp.arange(tok_rows, dtype=jnp.int32)
    places = req_index * tok_rows + row_ids
    labels = jnp.arange(prefix_lengths.shape[0], dtype=jnp.int32)
    label_count = labels.shape[0]
    beyond = tok_rows * req_count
    earliest_rows = jnp.min(
        jnp.where(segment_ids[:, None] == labels[None, :], places[:, None], beyond), axis=0
    )
    weight_rows = qkv_weight.shape[0]
    digit_cols = 128
    owners = page_owner[:, 0]
    owner_count = owners.shape[0]
    digits = jnp.concatenate([earliest_rows // 128, earliest_rows % 128, owners])
    digits = digits.astype(jnp.bfloat16)
    digit_used = 2 * label_count + owner_count
    digits = jnp.pad(digits, (0, weight_rows * digit_cols - digit_used)).reshape(
        weight_rows, digit_cols
    )
    qkv_local = qkv_weight.reshape(weight_rows, 3 * head_cols)
    fc1_cols = fc1_weight.shape[1]
    dense_cols = dense_weight.shape[0]
    fc2_cols = fc2_weight.shape[0]
    first_pack = jnp.concatenate([qkv_local, digits], axis=1)
    second_pack = jnp.concatenate([fc1_weight, dense_weight.T, fc2_weight.T], axis=1)
    first_full, second_full = ring_gather(first_pack, second_pack, INNER, req_count // INNER)
    qkv_full, digits_full = jnp.split(first_full, [3 * head_cols], axis=1)
    fc1_full, dense_full_t, fc2_full_t = jnp.split(
        second_full, [fc1_cols, fc1_cols + dense_cols], axis=1
    )
    digit_table = digits_full.reshape(req_count, weight_rows * digit_cols)[:, :digit_used]
    digit_table = digit_table.astype(jnp.int32)
    owner_table = digit_table[:, 2 * label_count :]
    starts = jnp.min(
        digit_table[:, :label_count] * 128 + digit_table[:, label_count : 2 * label_count], axis=0
    )

    def add_rows(portion):
        return jnp.dot(normed, portion, preferred_element_type=jnp.float32)

    projected = add_rows(qkv_full)
    lifted = add_rows(fc1_full)
    projected = (projected + qkv_bias.reshape(1, 3 * head_cols)).reshape(
        tok_rows, 3, head_cols // HEAD_DIM, HEAD_DIM
    )
    segment, position = label_rows(places, starts, prefix_lengths)
    queries = (
        rotate_heads(projected[:, 0], position).astype(jnp.bfloat16).reshape(tok_rows, head_cols)
    )
    new_keys = (
        rotate_heads(projected[:, 1], position).astype(jnp.bfloat16).reshape(tok_rows, head_cols)
    )
    new_values = projected[:, 2].astype(jnp.bfloat16).reshape(tok_rows, head_cols)
    key_value = jnp.stack([new_keys, new_values], axis=1)
    pages_here = tok_rows // PAGE
    page_width = PAGE * 2 * head_cols
    pages = key_value.reshape(pages_here, page_width)
    onehot = (owners[:, None] == jnp.arange(req_count, dtype=jnp.int32)[None, :]).astype(jnp.int32)
    earlier = jnp.cumsum(onehot, axis=0) - onehot
    earlier_count = jnp.sum(earlier * onehot, axis=1)
    target = owners * page_cap + earlier_count
    selecting = (target[None, :] == jnp.arange(pool_count, dtype=jnp.int32)[:, None]).astype(
        jnp.bfloat16
    )
    outgoing = jnp.dot(selecting, pages, preferred_element_type=jnp.float32).astype(jnp.bfloat16)
    incoming = lax.all_to_all(
        outgoing.reshape(req_count, page_cap, page_width), "req", split_axis=0, concat_axis=0, tiled=True
    ).reshape(pool_count, page_width)
    mine = jnp.sum((owner_table == req_index).astype(jnp.int32), axis=1)
    incoming_filled = (
        mine[:, None] > jnp.arange(page_cap, dtype=jnp.int32)[None, :]
    ).reshape(pool_count)
    slot_ids = slot_perm[0]
    placing = (slot_ids[None, :] == jnp.arange(pool_count, dtype=jnp.int32)[:, None]) & (
        incoming_filled[None, :] > 0
    )
    written = jnp.dot(
        placing.astype(jnp.bfloat16),
        incoming,
        preferred_element_type=jnp.float32,
    ).astype(jnp.bfloat16)
    written_mask = jnp.any(placing, axis=1)
    pool_pages = cache_pool.reshape(pool_count, page_width)
    new_pool = jnp.where(written_mask[:, None], written, pool_pages).reshape(cache_pool.shape)
    local_keys = jnp.concatenate([key_value, prefix_cache], axis=0)
    blocks = [local_keys]
    for shift_by in range(1, SPAN + 1):
        blocks.append(from_behind(local_keys, "req", shift_by))
    key_segs = []
    key_poss = []
    for step_back in range(SPAN + 1):
        block_id = req_index - step_back
        seg_new, pos_new = label_rows(block_id * tok_rows + row_ids, starts, prefix_lengths)
        seg_old, pos_old = prefix_rows(block_id, tok_rows, prefix_count, starts, prefix_lengths)
        key_segs.extend([seg_new, seg_old])
        key_poss.extend([pos_new, pos_old])
    key_segment = jnp.concatenate(key_segs)
    key_position = jnp.concatenate(key_poss)
    allowed = (key_segment[None, :] == segment[:, None]) & (
        key_position[None, :] <= position[:, None]
    )
    allowed = allowed & (
        (position[:, None] - key_position[None, :] < WINDOW) | (key_position[None, :] < SINKS)
    )
    all_keys = jnp.concatenate(blocks, axis=0)
    attended = head_attention(queries, all_keys[:, 0, :], all_keys[:, 1, :], allowed)
    hidden = jax.nn.gelu(lifted + fc1_bias, approximate=True).astype(jnp.bfloat16)
    contract_rows = (((1,), (1,)), ((), ()))
    attn_part = lax.dot_general(
        attended, dense_full_t, contract_rows, preferred_element_type=jnp.float32
    )
    mlp_part = lax.dot_general(
        hidden, fc2_full_t, contract_rows, preferred_element_type=jnp.float32
    )
    branches = attn_part + mlp_part
    summed = lax.psum_scatter(branches, "tensor", scatter_dimension=1, tiled=True)
    layer_out = (tokens.astype(jnp.float32) + summed + dense_bias + fc2_bias).astype(jnp.bfloat16)
    return (layer_out, new_pool)


def solution(mesh):
    placed = (
        P("req", "tensor"),
        P("req"),
        P(),
        P("req", None),
        P("req", None),
        P(),
        P(),
        P("req", None, "tensor"),
        P(None, "tensor"),
        P("tensor", "req"),
        P("tensor"),
        P("req", "tensor"),
        P("tensor"),
        P("tensor", "req"),
        P("tensor"),
        P("req", None, "tensor"),
        P("req", None, "tensor"),
    )
    return jax.shard_map(
        shards,
        mesh=mesh,
        in_specs=placed,
        out_specs=(P("req", "tensor"), P("req", None, "tensor")),
        check_vma=False,
    )
```
